32 devices in a mesh: gz: 4 (over y, x), ba: 8 (over z, core).
Axes of the slice: x: 2, y: 2, z: 4, core: 2. Of those that a mesh axis runs over, the one named last changes fastest.
Arguments:
- material_fraction: float32 [128, 32, 1024], P(('gz', 'ba')), may hold values from 0.05 to 1
- primal_heat_solution: float32 [128, 32, 1024], P(('gz', 'ba')), may hold values from -6 to 6
- dual_load: float32 [128, 32, 1024], P(('gz', 'ba')), may hold values from -6 to 6
- dual_prior_design: float32 [128, 32, 1024], P(('gz', 'ba')), may hold values from -3 to 3
- holder_cube_location: int32 [128], P(('gz', 'ba')), may hold values from -1 to 31, as said below
Outputs:
- dual_solution: float32 [128, 32, 1024], P(('gz', 'ba'))
- filtered: float32 [256, 64, 256], P(('gz', 'ba'))
The draws below stay inside these ranges and needn't reach their ends.
Inputs may be any that keep to these rules, and one draw needn't show every extreme that they name: `holder_cube_location`: each device's 4 entries list distinct brick positions of 0 to 31 in increasing order, followed by -1 for empty slots; every device's list holds positions 0 and (3) * 4 * 2, every device fills at least a third of its slots and at least two, and some device fills all of them.
All inputs are finite; a program needn't handle non-finite values.
Results may differ from the reference program's by a relative error of at most 0.0003.
Values sent between devices are 32-bit elements; how exact they have to be, the bound alone decides.
No kernel may reach another device: no remote copies, remote signals or barrier semaphores. Data moves between devices by JAX's collectives and lax.ppermute only.
A program may use at most 64 MiB of HBM per device.

```python
import jax
import jax.numpy as jnp
from jax import lax

CUBE_CELL_COUNT = 32
TBX = 2
BY = 4
BZ = 4
BPD = 4
SWEEPS = 2
FILTER_SWEEPS = 2
HOLDER_COUNT = 128
N_GZ = 4
N_BA = 8


def draw_holder_cube_location(key, part):
    devices = HOLDER_COUNT // BPD
    spot_count = TBX * BY * BZ
    top_spot = (BZ - 1) * BY * TBX
    least = max(2, (BPD + 2) // 3)
    key_counts, key_full, key_order = jax.random.split(jax.random.fold_in(key, 11), 3)
    counts = jax.random.randint(key_counts, (devices,), least, BPD + 1)
    full_device = jax.random.randint(key_full, (), 0, devices)
    is_full = jnp.arange(devices) == full_device
    counts = jnp.where(is_full, BPD, counts)
    device_keys = jax.random.split(key_order, devices)
    spots = jnp.arange(spot_count, dtype=jnp.int32)

    def one_device(device_key, filled, full_flag):
        priority = jax.random.permutation(device_key, spot_count).astype(jnp.int32)
        priority = jnp.where(full_flag & (spots == spot_count - 1), -3, priority)
        priority = jnp.where(spots == top_spot, -4, priority)
        priority = jnp.where(spots == 0, -5, priority)
        order = jnp.argsort(priority, stable=True).astype(jnp.int32)[:BPD]
        chosen = jnp.where(jnp.arange(BPD) < filled, order, spot_count)
        chosen = jnp.sort(chosen)
        return jnp.where(chosen < spot_count, chosen, -1).astype(jnp.int32)
    return jax.vmap(one_device)(device_keys, counts, is_full).reshape(-1)


def level_of(key, extent, shards, smallest, high):
    def one(dim, blocks):
        heights = jax.random.uniform(jax.random.fold_in(jax.random.fold_in(key, 6), dim), (blocks,), jnp.float32, smallest / len(shards), high / len(shards))
        return jnp.repeat(jnp.exp(heights), extent[dim] // blocks).reshape((-1,) + (1,) * (len(extent) - dim - 1))

    gain = one(*shards[0])
    for cut in shards[1:]:
        gain = gain * one(*cut)
    return gain


def normal_values(key, shape, width, limit, pieces=(), held_as=jnp.bfloat16):
    level = level_of(key, shape, pieces, -0.22, 0.18) if pieces else 1.0
    entries = jax.random.normal(key, shape, jnp.float32) * width * level
    return jnp.minimum(jnp.maximum(entries, -limit), limit).astype(held_as)


def setup_inputs(seed: int = 0) -> dict:
    streams_of = jax.random.split(jax.random.key(seed), 6)
    return {
        "material_fraction": jnp.clip(0.05 + 0.95 * jax.random.uniform(streams_of[0], (HOLDER_COUNT, CUBE_CELL_COUNT, CUBE_CELL_COUNT * CUBE_CELL_COUNT), jnp.float32) ** level_of(streams_of[0], (HOLDER_COUNT, CUBE_CELL_COUNT, CUBE_CELL_COUNT * CUBE_CELL_COUNT), ((0, 32),), -0.2, 0.2), 0.05, 1.0),
        "primal_heat_solution": normal_values(streams_of[1], (HOLDER_COUNT, CUBE_CELL_COUNT, CUBE_CELL_COUNT * CUBE_CELL_COUNT), 1.0, 6.0, ((0, 32),), jnp.float32),
        "dual_load": normal_values(streams_of[2], (HOLDER_COUNT, CUBE_CELL_COUNT, CUBE_CELL_COUNT * CUBE_CELL_COUNT), 1.0, 6.0, ((0, 32),), jnp.float32),
        "dual_prior_design": normal_values(streams_of[3], (HOLDER_COUNT, CUBE_CELL_COUNT, CUBE_CELL_COUNT * CUBE_CELL_COUNT), 0.5, 3.0, ((0, 32),), jnp.float32),
        "holder_cube_location": draw_holder_cube_location(jax.random.fold_in(streams_of[5], 71), 0),
    }


KMIN = 0.01
HEAT = 0.05
RADIUS2 = 2.0


def coupling_coefficients(values, far_faces):
    east = jnp.concatenate([values[..., 1:], far_faces[0][..., None]], axis=3)
    west = jnp.concatenate([far_faces[1][..., None], values[..., :-1]], axis=3)
    north = jnp.concatenate([values[:, :, 1:, :], far_faces[2][:, :, None, :]], axis=2)
    south = jnp.concatenate([far_faces[3][:, :, None, :], values[:, :, :-1, :]], axis=2)
    upper = jnp.concatenate([values[:, 1:], far_faces[4][:, None]], axis=1)
    lower = jnp.concatenate([far_faces[5][:, None], values[:, :-1]], axis=1)
    return (east, west, north, south, upper, lower)


def collect_boundaries(values, lookup_matrix):
    own_faces = (values[:, :, :, 0], values[:, :, :, -1], values[:, :, 0, :], values[:, :, -1, :], values[:, 0], values[:, -1])
    result = []
    for direction in range(6):
        rows = lookup_matrix[:, direction]
        picked = own_faces[direction][jnp.clip(rows, 0)]
        result.append(jnp.where((rows >= 0)[:, None, None], picked, 0.0))
    return tuple(result)


def conduct(thermal_kappa_cells, kappa_adjacent_cell):
    return 2.0 * thermal_kappa_cells * kappa_adjacent_cell / jnp.maximum(thermal_kappa_cells + kappa_adjacent_cell, KMIN)


def sweep_block(thermal_kappa_cells, dual_solution, rhs, *boundary_layers):
    adjacent_kappa_value = coupling_coefficients(thermal_kappa_cells, boundary_layers[:6])
    adjacent_dual_value = coupling_coefficients(dual_solution, boundary_layers[6:])
    total = HEAT
    flux = rhs
    for kappa_adjacent_cell, value_near in zip(adjacent_kappa_value, adjacent_dual_value):
        weight = conduct(thermal_kappa_cells, kappa_adjacent_cell)
        total = total + weight
        flux = flux + weight * value_near
    return flux / total


def gradient_cube(fraction_volume, thermal_kappa_cells, primal_heat_solution, dual_solution, *boundary_layers):
    adjacent_kappa_value = coupling_coefficients(thermal_kappa_cells, boundary_layers[:6])
    adjacent_heat_value = coupling_coefficients(primal_heat_solution, boundary_layers[6:12])
    adjacent_dual_value = coupling_coefficients(dual_solution, boundary_layers[12:])
    cumulative_sum = jnp.zeros_like(fraction_volume)
    for kappa_adjacent_cell, heat_adjacent_cell, dual_adjacent_cell in zip(adjacent_kappa_value, adjacent_heat_value, adjacent_dual_value):
        cumulative_sum = cumulative_sum + jnp.where(kappa_adjacent_cell > 0, (heat_adjacent_cell - primal_heat_solution) * (dual_adjacent_cell - dual_solution), 0.0)
    sens = jnp.where(thermal_kappa_cells > 0, -1.5 * (1.0 - KMIN) * fraction_volume * fraction_volume * cumulative_sum, 0.0)
    blocks = sens.shape[0]
    half_edge = sens.shape[1] // 2
    return sens.reshape(blocks, half_edge, 2, half_edge, 2, half_edge, 2).mean(axis=(2, 4, 6))


def per_cube_apply(function, arrays):
    shaped = tuple(item.reshape((HOLDER_COUNT // BPD, BPD) + item.shape[1:]) for item in arrays)
    result = lax.map(lambda bundle: function(*bundle), shaped)
    return result.reshape((HOLDER_COUNT,) + result.shape[2:])


def filter_sweep(field_data, rhs_grid):
    padded = jnp.pad(field_data, 1)
    near = padded[2:, 1:-1, 1:-1] + padded[:-2, 1:-1, 1:-1]
    near = near + padded[1:-1, 2:, 1:-1] + padded[1:-1, :-2, 1:-1]
    near = near + padded[1:-1, 1:-1, 2:] + padded[1:-1, 1:-1, :-2]
    return (rhs_grid + RADIUS2 * near) / (1.0 + 6.0 * RADIUS2)


def reference(material_fraction, primal_heat_solution, dual_load, dual_prior_design, holder_cube_location):
    edge_cells = CUBE_CELL_COUNT
    half_edge = CUBE_CELL_COUNT // 2
    rank_quartet_layout = (HOLDER_COUNT, edge_cells, edge_cells, edge_cells)
    fraction_volume = material_fraction.reshape(rank_quartet_layout)
    heat_volume = primal_heat_solution.reshape(rank_quartet_layout)
    load = dual_load.reshape(rank_quartet_layout)
    dual_solution = dual_prior_design.reshape(rank_quartet_layout)
    active = holder_cube_location >= 0
    device = jnp.arange(HOLDER_COUNT, dtype=jnp.int32) // BPD
    group = device // N_BA
    member = device % N_BA
    position = jnp.maximum(holder_cube_location, 0)
    brick_x = member * TBX + position % TBX
    brick_y = (position // TBX) % BY
    brick_z = group * BZ + position // (TBX * BY)
    bricks_x = N_BA * TBX
    bricks_z = N_GZ * BZ
    brick_total = bricks_x * BY * bricks_z
    brick_id = jnp.where(active, (brick_z * BY + brick_y) * bricks_x + brick_x, brick_total)
    slot_map = jnp.full((brick_total,), -1, jnp.int32).at[brick_id].set(jnp.arange(HOLDER_COUNT, dtype=jnp.int32), mode="drop")

    def lookup(step_x, step_y, step_z):
        near_x = brick_x + step_x
        near_y = brick_y + step_y
        near_z = brick_z + step_z
        inside = active & (near_x >= 0) & (near_x < bricks_x) & (near_y >= 0) & (near_y < BY) & (near_z >= 0) & (near_z < bricks_z)
        index = (jnp.clip(near_z, 0, bricks_z - 1) * BY + jnp.clip(near_y, 0, BY - 1)) * bricks_x + jnp.clip(near_x, 0, bricks_x - 1)
        return jnp.where(inside, slot_map[index], -1).astype(jnp.int32)

    lookup_matrix = jnp.stack([lookup(1, 0, 0), lookup(-1, 0, 0), lookup(0, 1, 0), lookup(0, -1, 0), lookup(0, 0, 1), lookup(0, 0, -1)], axis=1)
    active_four = active[:, None, None, None]
    thermal_kappa_cells = jnp.where(active_four, KMIN + (1.0 - KMIN) * fraction_volume * fraction_volume * fraction_volume, 0.0)
    rhs = jnp.where(active_four, load, 0.0)
    foreign_kappa_layers = collect_boundaries(thermal_kappa_cells, lookup_matrix)
    foreign_heat_layers = collect_boundaries(heat_volume, lookup_matrix)
    for sweep_index in range(SWEEPS):
        foreign_dual_layers = collect_boundaries(dual_solution, lookup_matrix)
        dual_solution = per_cube_apply(sweep_block, (thermal_kappa_cells, dual_solution, rhs) + foreign_kappa_layers + foreign_dual_layers)
    foreign_dual_layers = collect_boundaries(dual_solution, lookup_matrix)
    restricted_grid = per_cube_apply(gradient_cube, (fraction_volume, thermal_kappa_cells, heat_volume, dual_solution) + foreign_kappa_layers + foreign_heat_layers + foreign_dual_layers)
    z_index = jnp.where(active, brick_z, bricks_z)
    grid = jnp.zeros((bricks_z, BY, bricks_x, half_edge, half_edge, half_edge), restricted_grid.dtype)
    grid = grid.at[z_index, brick_y, brick_x].set(restricted_grid, mode="drop")
    grid = grid.transpose(0, 3, 1, 4, 2, 5).reshape(bricks_z * half_edge, BY * half_edge, bricks_x * half_edge)
    smoothed = grid
    for filter_index in range(FILTER_SWEEPS):
        smoothed = filter_sweep(smoothed, grid)
    return dual_solution.reshape(HOLDER_COUNT, edge_cells, edge_cells * edge_cells), smoothed
```

```python
import functools

import jax
import jax.numpy as jnp
from jax import lax
from jax.experimental import pallas as pl
from jax.experimental.pallas import tpu as pltpu
from jax.sharding import PartitionSpec as P

SLOTS = 4
KMIN = 0.01
HEAT = 0.05
F32 = jnp.float32
I32 = jnp.int32

Z_UP = 128
Z_DOWN = 152
SLAB = 176
SLAB_SIZE = 22
ZERO = 220
TILES = 252
X_TILES = 49
Z_SLABS = 96
Z_TILES = 115
DUMMY = 29


def lanes():
    return lax.broadcasted_iota(I32, (8, 128), 1)


def rows():
    return lax.broadcasted_iota(I32, (8, 128), 0)


def take(tile, index):
    return jnp.take_along_axis(tile, index, axis=1)


def row_of(values):
    lane = lanes()
    result = jnp.zeros((8, 128), F32)
    for index, value in enumerate(values):
        result = jnp.where(lane == index, (value + 1).astype(F32), result)
    return result


def position_at(meta, index):
    return meta[0, 0, index].astype(I32) - 1


def as_int(flag):
    return jnp.where(flag, 1, 0).astype(I32)


def pack_kernel(place, parity_ref, mat, heat, load, prior, near, far, up, down):
    parity = parity_ref[0]
    lane = lanes()
    depth = lane // 32
    inside = 32 * (lane % 4)
    pick = (lane % 32) // 4
    first = place[0] >= 0
    start = as_int(place[SLOTS - 1] >= 0)
    low = inside + depth
    high = inside + 31 - depth
    near_side = jnp.where(parity == 0, high, low)
    far_side = jnp.where(parity == 0, low, high)
    last_low = inside + jnp.where(depth == 3, 0, depth)
    last_high = inside + 31 - jnp.where(depth == 3, 0, depth)
    near_last = jnp.where(parity == 0, last_high, last_low)
    far_last = jnp.where(parity == 0, last_low, last_high)

    def slab(unit, carry):
        row = pl.multiple_of(unit * 8, 8)
        for field, ref in enumerate((mat, prior)):
            for out, side in ((near, near_side), (far, far_side)):
                tile = jnp.zeros((8, 128), F32)
                for j in range(8):
                    got = take(ref[pl.ds(row, 8), 128 * j : 128 * j + 128], side)
                    tile = jnp.where(pick == j, got, tile)
                out[field * 16 + unit] = tile
        for out, side in ((near, near_last), (far, far_last)):
            tile = jnp.zeros((8, 128), F32)
            for j in range(8):
                got = jnp.where(
                    depth == 3,
                    take(heat[pl.ds(row, 8), 128 * j : 128 * j + 128], side),
                    take(load[pl.ds(row, 8), 128 * j : 128 * j + 128], side),
                )
                tile = jnp.where(pick == j, got, tile)
            out[32 + unit] = tile
        return carry

    lax.fori_loop(0, 16, slab, 0)
    meta = row_of([place[s] for s in range(SLOTS)])
    near[48] = meta
    far[48] = meta
    for field, ref in enumerate((mat, prior, load, heat)):
        for i in range(3):
            top = pl.multiple_of((start + i) * 32 + 24, 8)
            for j in range(8):
                up[(field * 3 + i) * 8 + j] = ref[pl.ds(top, 8), 128 * j : 128 * j + 128]
                down[(field * 3 + i) * 8 + j] = ref[32 * i : 32 * i + 8, 128 * j : 128 * j + 128]


def corner_kernel(
    place, near_meta, far_meta, near, far, up_in, down_in, up, down, meta_tile, sems
):
    del up_in, down_in
    values = [place[s] for s in range(SLOTS)]
    copies = []
    for b, (meta, source) in enumerate(((near_meta, near), (far_meta, far))):
        listed = [position_at(meta, s) for s in range(SLOTS)]
        values = values + listed
        start = as_int(listed[SLOTS - 1] >= 0)
        for field in range(3):
            for i in range(3):
                to = Z_SLABS + b * 9 + field * 3 + i
                copies.append((source.at[field * 16 + (start + i) * 4 + 3], up.at[to]))
                copies.append((source.at[field * 16 + i * 4], down.at[to]))
    meta_tile[...] = row_of(values)
    copies.append((meta_tile, up.at[Z_TILES - 1]))
    copies.append((meta_tile, down.at[Z_TILES - 1]))
    started = [
        pltpu.make_async_copy(source, target, sems.at[index])
        for index, (source, target) in enumerate(copies)
    ]
    for copy in started:
        copy.start()
    for copy in started:
        copy.wait()


def conduct(own, beside):
    return (2.0 * own) * beside / jnp.maximum(own + beside, KMIN)


def main_kernel(
    parts,
    place,
    parity_ref,
    near_meta,
    far_meta,
    up_meta,
    down_meta,
    mat,
    heat,
    load,
    prior,
    near,
    far,
    z_up,
    z_down,
    dual_out,
    chunks,
    cells,
    brick_table,
    slab_table,
    kappa,
    temperature,
    source,
    dual0,
    dual1,
    dual2,
    weights,
    inverse,
    sens,
    summed,
    turned,
):
    parity = parity_ref[0]
    lane = lanes()
    row = rows()

    def clear(index, carry):
        cells[index] = ZERO
        return carry

    lax.fori_loop(0, 144, clear, 0, unroll=8)

    def cell_of(x, y, z):
        return ((z + 1) * 6 + y + 1) * 4 + x + 1

    def enter(position, wanted, x, z, tile):
        here = jnp.where(wanted, cell_of(x, position // 2 % 4, z), 144)
        cells[here] = tile
        return jnp.where(wanted, here, DUMMY)

    own = [place[s] for s in range(SLOTS)]
    own_cell = [
        enter(q, q >= 0, q % 2, q // 8, 32 * s) for s, q in enumerate(own)
    ]
    lists_up = [[position_at(up_meta, 4 * k + s) for s in range(SLOTS)] for k in range(3)]
    lists_down = [[position_at(down_meta, 4 * k + s) for s in range(SLOTS)] for k in range(3)]

    def shifted(listed):
        full = listed[SLOTS - 1] >= 0
        return [jnp.where(full, listed[i + 1], listed[i]) for i in range(3)]

    ups = [listed[:3] for listed in lists_up]
    downs = [shifted(listed) for listed in lists_down]
    up_cell = [
        enter(q, (q >= 0) & (q < 8), q % 2, 4, Z_UP + 8 * i) for i, q in enumerate(ups[0])
    ]
    down_cell = [
        enter(q, q >= 24, q % 2, -1, Z_DOWN + 8 * i) for i, q in enumerate(downs[0])
    ]
    slab_cell = []
    for b, meta in enumerate((near_meta, far_meta)):
        east = parity == b
        column = jnp.where(east, 0, 1)
        x = jnp.where(east, 2, -1)
        base = SLAB + SLAB_SIZE * b
        mine = [position_at(meta, s) for s in range(SLOTS)]
        slab_cell.append(
            [
                enter(q, (q >= 0) & (q % 2 == column), x, q // 8, base + 4 * s)
                for s, q in enumerate(mine)
            ]
            + [
                enter(q, (q >= 0) & (q < 8) & (q % 2 == column), x, 4, base + 16 + i)
                for i, q in enumerate(ups[1 + b])
            ]
            + [
                enter(q, (q >= 24) & (q % 2 == column), x, -1, base + 19 + i)
                for i, q in enumerate(downs[1 + b])
            ]
        )

    def set_brick(unit, up, down, north, south, east, west, px):
        for k, value in enumerate((up, down, north, south, east, west, px)):
            brick_table[unit * 8 + k] = value

    for s in range(SLOTS):
        here = own_cell[s]
        px = jnp.where(own[s] >= 0, own[s] % 2, 0)
        lift = jnp.where(own[s] >= 8, 24, 0)
        north, south = (cells[here + 4], cells[here - 4])
        east, west = (cells[here + 1], cells[here - 1])
        above, below = (cells[here + 24], cells[here - 24] + lift)
        for c in range(4):
            base = s * 32 + c * 8
            set_brick(
                s * 4 + c,
                base + 8 if c < 3 else above,
                base - 8 if c > 0 else below,
                north + 8 * c,
                south + 8 * c,
                east + jnp.where(px == 1, c, 8 * c),
                west + jnp.where(px == 0, c, 8 * c),
                px,
            )
    for k, (listed, cell_list) in enumerate(((ups[0], up_cell), (downs[0], down_cell))):
        for i in range(3):
            here = cell_list[i]
            px = jnp.where(listed[i] >= 0, listed[i] % 2, 0)
            set_brick(
                16 + 3 * k + i,
                ZERO if k == 0 else cells[here + 24],
                cells[here - 24] + 24 if k == 0 else ZERO,
                cells[here + 4],
                cells[here - 4],
                cells[here + 1],
                cells[here - 1],
                px,
            )

    def set_slab(unit, up, down, north, south, face):
        for k, value in enumerate((up, down, north, south, face)):
            slab_table[unit * 8 + k] = value

    for b, meta in enumerate((near_meta, far_meta)):
        inward = jnp.where(parity == b, -1, 1)
        for s in range(SLOTS):
            here = slab_cell[b][s]
            lift = jnp.where(position_at(meta, s) >= 8, 3, 0)
            north, south = (cells[here + 4], cells[here - 4])
            above, below = (cells[here + 24], cells[here - 24] + lift)
            face = cells[here + inward]
            for c in range(4):
                unit = SLAB_SIZE * b + 4 * s + c
                set_slab(
                    unit,
                    SLAB + unit + 1 if c < 3 else above,
                    SLAB + unit - 1 if c > 0 else below,
                    north + c,
                    south + c,
                    face + 8 * c,
                )
        for i in range(6):
            here = slab_cell[b][4 + i]
            set_slab(
                SLAB_SIZE * b + 16 + i,
                ZERO if i < 3 else cells[here + 24],
                cells[here - 24] + 3 if i < 3 else ZERO,
                cells[here + 4],
                cells[here - 4],
                cells[here + inward],
            )

    zeros = jnp.zeros((8, 128), F32)
    for ref in (kappa, temperature, dual0, dual1, dual2):
        for t in range(32):
            ref[ZERO + t] = zeros

    def conductivity(fraction):
        return KMIN + (1.0 - KMIN) * fraction * fraction * fraction

    def own_unit(unit, carry):
        at = pl.multiple_of(unit * 8, 8)
        active = place[unit // 4] >= 0
        for j in range(8):
            span = slice(128 * j, 128 * j + 128)
            t = unit * 8 + j
            kappa[t] = jnp.where(active, conductivity(mat[pl.ds(at, 8), span]), 0.0)
            source[t] = jnp.where(active, load[pl.ds(at, 8), span], 0.0)
            dual0[t] = prior[pl.ds(at, 8), span]
            temperature[t] = heat[pl.ds(at, 8), span]
        return carry

    lax.fori_loop(0, 16, own_unit, 0)

    def halo_tile(t, carry):
        for to, message in ((Z_UP, z_up), (Z_DOWN, z_down)):
            kappa[to + t] = conductivity(message[t])
            dual0[to + t] = message[24 + t]
            source[to + t] = message[48 + t]
            temperature[to + t] = message[72 + t]
        return carry

    lax.fori_loop(0, 24, halo_tile, 0, unroll=4)

    def slab_tile(to, message, at, step):
        third = message[at + 2 * step]
        kappa[to] = conductivity(message[at])
        dual0[to] = message[at + step]
        source[to] = third
        temperature[to] = pltpu.roll(third, 32, 1)

    for b, message in enumerate((near, far)):
        base = SLAB + SLAB_SIZE * b

        def side_tile(t, carry):
            slab_tile(base + t, message, t, 16)
            return carry

        lax.fori_loop(0, 16, side_tile, 0, unroll=4)
        for i in range(3):
            slab_tile(base + 16 + i, z_up, Z_SLABS + 9 * b + i, 3)
            slab_tile(base + 19 + i, z_down, Z_SLABS + 9 * b + i, 3)

    top_row = row == 0
    last_row = row == 7
    x_cell = lane % 32
    y_block = lane // 32

    def above_of(tile, other):
        return pltpu.roll(jnp.where(top_row, other, tile), 7, 0)

    def below_of(tile, other):
        return pltpu.roll(jnp.where(last_row, other, tile), 1, 0)

    def brick_unit(unit):
        up, down, north, south, east, west, px = (brick_table[unit * 8 + k] for k in range(7))
        inner = 1 - px
        east_index = jnp.where(px == 1, y_block, jnp.maximum(lane - 31, 0))
        west_index = jnp.where(px == 0, y_block, jnp.minimum(lane + 31, 127))

        def around(ref, j):
            base = unit * 8
            tile = ref[base + j]
            after = ref[base + j + 1] if j < 7 else ref[north]
            before = ref[base + j - 1] if j > 0 else ref[south + 7]
            over = take(ref[east + inner * j], east_index + 4 * j * px)
            under = take(ref[west + px * j], west_index + 4 * j * inner)
            return tile, (
                jnp.where(x_cell == 31, over, pltpu.roll(tile, 127, 1)),
                jnp.where(x_cell == 0, under, pltpu.roll(tile, 1, 1)),
                pltpu.roll(jnp.where(lane < 32, after, tile), 96, 1),
                pltpu.roll(jnp.where(lane >= 96, before, tile), 32, 1),
                above_of(tile, ref[up + j]),
                below_of(tile, ref[down + j]),
            )

        return around

    def slab_unit(unit, column):
        up, down, north, south, face = (slab_table[unit * 8 + k] for k in range(5))
        index = 32 * (lane % 4) + column
        block = lane // 4

        def around(ref):
            tile = ref[SLAB + unit]
            edge = take(ref[face], index)
            for j in range(1, 8):
                edge = jnp.where(block == j, take(ref[face + j], index), edge)
            return tile, (
                pltpu.roll(tile, 96, 1),
                jnp.where(lane < 32, edge, pltpu.roll(tile, 32, 1)),
                jnp.where(x_cell == 31, pltpu.roll(ref[north], 31, 1), pltpu.roll(tile, 127, 1)),
                jnp.where(x_cell == 0, pltpu.roll(ref[south], 97, 1), pltpu.roll(tile, 1, 1)),
                above_of(tile, ref[up]),
                below_of(tile, ref[down]),
            )

        return around

    def first_sweep(t, own_kappa, beside_kappa, beside):
        total = jnp.full((8, 128), HEAT, F32)
        flux = source[t]
        for k in range(6):
            weight = conduct(own_kappa, beside_kappa[k])
            weights[k * TILES + t] = weight
            total = total + weight
            flux = flux + weight * beside[k]
        scale = 1.0 / total
        inverse[t] = scale
        dual1[t] = flux * scale

    def later_sweep(t, beside):
        flux = source[t]
        for k in range(6):
            flux = flux + weights[k * TILES + t] * beside[k]
        return flux * inverse[t]

    def slabs(body):
        for b in range(2):
            column = jnp.where(parity == b, 31, 0)

            def two(step, carry):
                for k in range(2):
                    unit = SLAB_SIZE * b + 2 * step + k
                    body(SLAB + unit, slab_unit(unit, column))
                return carry

            lax.fori_loop(0, SLAB_SIZE // 2, two, 0)

    def brick_first(unit, carry):
        around = brick_unit(unit)
        for j in range(8):
            own_kappa, beside_kappa = around(kappa, j)
            first_sweep(unit * 8 + j, own_kappa, beside_kappa, around(dual0, j)[1])
        return carry

    lax.fori_loop(0, 22, brick_first, 0)

    def slab_first(t, around):
        own_kappa, beside_kappa = around(kappa)
        first_sweep(t, own_kappa, beside_kappa, around(dual0)[1])

    slabs(slab_first)

    def brick_second(unit, carry):
        around = brick_unit(unit)
        for j in range(8):
            dual2[unit * 8 + j] = later_sweep(unit * 8 + j, around(dual1, j)[1])
        return carry

    lax.fori_loop(0, 22, brick_second, 0)

    def slab_second(t, around):
        dual2[t] = later_sweep(t, around(dual1)[1])

    slabs(slab_second)

    def sensitivity(unit, carry):
        around = brick_unit(unit)
        at = pl.multiple_of(unit * 8, 8)
        for j in range(8):
            t = unit * 8 + j
            dual, duals = around(dual2, j)
            warm, warms = around(temperature, j)
            total = jnp.zeros((8, 128), F32)
            for k in range(6):
                total = total + jnp.where(
                    weights[k * TILES + t] > 0, (warms[k] - warm) * (duals[k] - dual), 0.0
                )
            fraction = sens[pl.ds(at, 8), 128 * j : 128 * j + 128]
            sens[pl.ds(at, 8), 128 * j : 128 * j + 128] = (
                -1.5 * (1.0 - KMIN) * fraction * fraction * total
            )
        return carry

    def stage_own(unit, carry):
        at = pl.multiple_of(unit * 8, 8)
        sens[pl.ds(at, 8), :] = mat[pl.ds(at, 8), :]
        for j in range(8):
            dual_out[pl.ds(at, 8), 128 * j : 128 * j + 128] = dual2[unit * 8 + j]
        return carry

    lax.fori_loop(0, 16, stage_own, 0)
    for k, message in enumerate((z_up, z_down)):
        for i in range(3):
            for j in range(8):
                at = 128 + 24 * k + 8 * i
                sens[at : at + 8, 128 * j : 128 * j + 128] = message[8 * i + j]
    lax.fori_loop(0, 22, sensitivity, 0)

    cell = lax.broadcasted_iota(I32, (512, 128), 0)
    coarse = lax.broadcasted_iota(I32, (512, 128), 1)
    matches = (cell // 64 == coarse // 16) & (cell % 32 // 2 == coarse % 16)
    shrink = jnp.where(matches, 0.125, 0.0).astype(F32)
    for half in range(2):
        summed[...] = jnp.dot(
            sens[:, 512 * half : 512 * half + 512],
            shrink,
            precision=lax.Precision.HIGHEST,
            preferred_element_type=F32,
        )
        for r in range(11):
            tile = summed[pl.ds(16 * r, 8, stride=2), :] + summed[pl.ds(16 * r + 1, 8, stride=2), :]
            for bit in (1, 2, 4):
                low_row = (row & bit) == 0
                low_lane = (lane & (16 * bit)) == 0
                swap_a = pltpu.roll(pltpu.roll(tile, 8 - bit, 0), 16 * bit, 1)
                swap_b = pltpu.roll(pltpu.roll(tile, bit, 0), 128 - 16 * bit, 1)
                tile = jnp.where(low_row == low_lane, tile, jnp.where(low_row, swap_a, swap_b))
            turned[2 * r + half] = tile

    planes = 64 // parts
    level = [jnp.where(q >= 0, q // 8, 9) for q in own]

    def count(test):
        return functools.reduce(lambda a, b: a + b, [as_int(test(v)) for v in level])

    before = [count(lambda v, z=z: v < z) for z in range(5)]

    def nth(z, e):
        index = before[z] + e
        valid = index < before[z + 1]
        slot = jnp.minimum(index, SLOTS - 1)
        code = jnp.where(valid, place[slot] - 8 * z, -1)
        return slot, code

    for d in range(parts):
        z = d * planes // 16
        half = d * planes % 16 // 8
        codes = []
        for e in range(3):
            slot, code = nth(z, e)
            codes.append(code)
            for k in range(2):
                chunks[d * 8 + 2 * e + k] = turned[(slot * 2 + half) * 2 + k]
        start = d * planes % 8 == 0
        end = (d + 1) * planes % 8 == 0
        if planes >= 8:
            outside = -1 if half == 0 else 1
        else:
            outside = -1 if start else 1 if end else 0
        beyond = half + outside
        beside = [zeros, zeros]
        for e in range(3):
            if outside == 0:
                tile_at, lane_at, code = (0, 0, jnp.int32(-1))
            elif beyond in (0, 1):
                slot, code = nth(z, e)
                tile_at, lane_at = (slot * 2 + beyond, 96 if outside < 0 else 0)
            elif 0 <= z + outside <= 3:
                slot, code = nth(z + outside, e)
                tile_at, lane_at = (slot * 2 + (1 if outside < 0 else 0), 96 if outside < 0 else 0)
            elif outside < 0:
                q = downs[0][e]
                code = jnp.where(q >= 24, q - 24, -1)
                tile_at, lane_at = (8 + (3 + e) // 2, 64 * ((3 + e) % 2) + 32)
            else:
                q = ups[0][e]
                code = jnp.where((q >= 0) & (q < 8), q, -1)
                tile_at, lane_at = (8 + e // 2, 64 * (e % 2))
            codes.append(code)
            for k in range(2):
                tile = turned[tile_at * 2 + k]
                shift = (32 * e - lane_at) % 128
                if shift:
                    tile = pltpu.roll(tile, shift, 1)
                beside[k] = jnp.where(y_block == e, tile, beside[k])
        for e, code in enumerate(codes):
            beside[0] = jnp.where(lane == 96 + e, (code + 1).astype(F32), beside[0])
        for k in range(2):
            chunks[d * 8 + 6 + k] = beside[k]


def filter_kernel(parts, planes, across, spot, meta, received, swapped, out, grid, once):
    member = spot[0]
    depth = planes + 4
    wide = parts // across
    lane = lanes()
    row = rows()
    group_lane = lane // 16
    zeros = jnp.zeros((8, 128), F32)

    def clear(index, carry):
        grid[index] = zeros
        return carry

    lax.fori_loop(0, depth * 8 * wide, clear, 0, unroll=8)
    begin = member * planes
    half = begin % 16 // 8
    side = jnp.where(begin % 8 == 0, 0, planes + 2) if planes < 8 else half * (planes + 2)

    def place_plane(tile, lane_at, window, code, k, column, tile_x):
        at = (column * 2 + code % 2) % 8
        moved = pltpu.roll(tile, (at * 16 - lane_at + 256) % 128, 1)
        where_to = (window * 8 + code // 2 * 2 + k) * wide + tile_x
        grid[where_to] = jnp.where(group_lane == at, moved, grid[where_to])

    def from_device(column, carry):
        tile_x = column // across
        for e in range(3):
            code = meta[column, 0, 0, 96 + e].astype(I32) - 1

            @pl.when(code >= 0)
            def _(e=e, code=code):
                for k in range(2):
                    tile = received[column * 8 + 2 * e + k]
                    if planes == 8:
                        for p in range(8):
                            place_plane(tile, 16 * p, p + 2, code, k, column, tile_x)
                        other = swapped[column * 8 + 2 * e + k]
                        for p in range(2):
                            place_plane(
                                other,
                                jnp.where(half == 0, 16 * p, 96 + 16 * p),
                                jnp.where(half == 0, 10 + p, p),
                                code,
                                k,
                                column,
                                tile_x,
                            )
                    else:
                        for window in range(depth):
                            p = begin % 8 + window - 2

                            @pl.when((p >= 0) & (p < 8))
                            def _(tile=tile, p=p, window=window, k=k):
                                place_plane(tile, 16 * p, window, code, k, column, tile_x)

        for e in range(3):
            code = meta[column, 0, 0, 99 + e].astype(I32) - 1

            @pl.when(code >= 0)
            def _(e=e, code=code):
                for k in range(2):
                    tile = received[column * 8 + 6 + k]
                    for p in range(2):
                        place_plane(
                            tile, 32 * e + 16 * p, side + p, code, k, column, tile_x
                        )

        return carry

    lax.fori_loop(0, parts, from_device, 0)

    def relax(ref, window, y, x):
        here = (window * 8 + y) * wide + x
        tile = ref[here]
        north = ref[here + wide] if y < 7 else zeros
        south = ref[here - wide] if y > 0 else zeros
        east = ref[here + 1] if x < wide - 1 else zeros
        west = ref[here - 1] if x > 0 else zeros
        near = ref[here + 8 * wide] + ref[here - 8 * wide]
        near = near + pltpu.roll(jnp.where(row == 0, north, tile), 7, 0)
        near = near + pltpu.roll(jnp.where(row == 7, south, tile), 1, 0)
        near = near + pltpu.roll(jnp.where(lane == 0, east, tile), 127, 1)
        near = near + pltpu.roll(jnp.where(lane == 127, west, tile), 1, 1)
        return (grid[here] + 2.0 * near) * (1.0 / 13.0)

    first = spot[1] == 0
    last = spot[1] == spot[2] - 1

    def sweep_once(window, carry):
        gone = (first & (window < 2)) | (last & (window >= planes + 2))
        keep = jnp.where(gone, 0.0, 1.0).astype(F32)
        for y in range(8):
            for x in range(wide):
                once[(window * 8 + y) * wide + x] = relax(grid, window, y, x) * keep
        return carry

    lax.fori_loop(1, depth - 1, sweep_once, 0)

    def sweep_again(window, carry):
        for y in range(8):
            for x in range(wide):
                out[window - 2, 8 * y : 8 * y + 8, 128 * x : 128 * x + 128] = relax(
                    once, window, y, x
                )
        return carry

    lax.fori_loop(2, depth - 2, sweep_again, 0)


VMEM = pl.BlockSpec(memory_space=pltpu.VMEM)
SMEM = pl.BlockSpec(memory_space=pltpu.SMEM)
ANY = pl.BlockSpec(memory_space=pl.ANY)
BIG = 48 * 1024 * 1024


def meta_of(index):
    return pl.BlockSpec((1, 8, 128), lambda i: (index, 0, 0), memory_space=pltpu.SMEM)


def params():
    return pltpu.CompilerParams(vmem_limit_bytes=BIG)


def tiles(count):
    return jax.ShapeDtypeStruct((count, 8, 128), F32)


def per_device(
    material_fraction, primal_heat_solution, dual_load, dual_prior_design, holder_cube_location
):
    parts = lax.axis_size("ba")
    groups = lax.axis_size("gz")
    member = lax.axis_index("ba")
    group = lax.axis_index("gz")
    planes = 64 // parts
    parity = (member % 2).reshape(1).astype(I32)
    place = holder_cube_location
    fields = [
        field.reshape(128, 1024)
        for field in (material_fraction, primal_heat_solution, dual_load, dual_prior_design)
    ]
    near, far, up, down = pl.pallas_call(
        pack_kernel,
        out_shape=(tiles(X_TILES), tiles(X_TILES), tiles(Z_TILES), tiles(Z_TILES)),
        in_specs=[SMEM, SMEM, VMEM, VMEM, VMEM, VMEM],
        out_specs=(VMEM, VMEM, VMEM, VMEM),
        compiler_params=params(),
        name="pack",
    )(place, parity, *fields)
    inner = [(i, i ^ 1) for i in range(parts)]
    outer = [(i, i + 1 if i % 2 else i - 1) for i in range(1, parts - 1)]
    near = lax.ppermute(near, "ba", inner)
    far = lax.ppermute(far, "ba", outer)
    up, down = pl.pallas_call(
        corner_kernel,
        out_shape=(tiles(Z_TILES), tiles(Z_TILES)),
        in_specs=[SMEM, meta_of(X_TILES - 1), meta_of(X_TILES - 1), ANY, ANY, ANY, ANY],
        out_specs=(ANY, ANY),
        input_output_aliases={5: 0, 6: 1},
        scratch_shapes=[pltpu.VMEM((8, 128), F32), pltpu.SemaphoreType.DMA((38,))],
        grid=(1,),
        compiler_params=params(),
        name="corners",
    )(place, near, far, near, far, up, down)
    rising = [(i, i + 1) for i in range(groups - 1)]
    falling = [(i + 1, i) for i in range(groups - 1)]
    from_below = lax.ppermute(up, "gz", rising)
    from_above = lax.ppermute(down, "gz", falling)
    meta_z = meta_of(Z_TILES - 1)
    meta_x = meta_of(X_TILES - 1)
    field_tiles = pltpu.VMEM((TILES, 8, 128), F32)
    dual, chunks = pl.pallas_call(
        functools.partial(main_kernel, parts),
        out_shape=(jax.ShapeDtypeStruct((128, 1024), F32), tiles(8 * parts)),
        in_specs=[SMEM, SMEM, meta_x, meta_x, meta_z, meta_z] + [VMEM] * 8,
        out_specs=(VMEM, VMEM),
        scratch_shapes=[
            pltpu.SMEM((145,), I32),
            pltpu.SMEM((22 * 8,), I32),
            pltpu.SMEM((44 * 8,), I32),
            field_tiles,
            field_tiles,
            field_tiles,
            field_tiles,
            field_tiles,
            field_tiles,
            pltpu.VMEM((6 * TILES, 8, 128), F32),
            field_tiles,
            pltpu.VMEM((176, 1024), F32),
            pltpu.VMEM((176, 128), F32),
            pltpu.VMEM((22, 8, 128), F32),
        ],
        grid=(1,),
        compiler_params=params(),
        name="sweeps",
    )(
        place,
        parity,
        near,
        far,
        from_above,
        from_below,
        *fields,
        near,
        far,
        from_above,
        from_below,
    )
    received = lax.all_to_all(chunks, "ba", split_axis=0, concat_axis=0, tiled=True)
    swapped = lax.ppermute(received, "ba", inner) if planes == 8 else received
    spot = jnp.stack([member, group * parts + member, jnp.int32(groups * parts)]).astype(I32)
    wide = 32 * parts // 128
    filtered = pl.pallas_call(
        functools.partial(filter_kernel, parts, planes, 4),
        out_shape=jax.ShapeDtypeStruct((planes, 64, 32 * parts), F32),
        in_specs=[
            SMEM,
            pl.BlockSpec(
                (parts, 1, 8, 128), lambda i: (0, 6, 0, 0), memory_space=pltpu.SMEM
            ),
            VMEM,
            VMEM,
        ],
        out_specs=VMEM,
        scratch_shapes=[
            pltpu.VMEM(((planes + 4) * 8 * wide, 8, 128), F32),
            pltpu.VMEM(((planes + 4) * 8 * wide, 8, 128), F32),
        ],
        grid=(1,),
        compiler_params=params(),
        name="smooth",
    )(spot, received.reshape(parts, 8, 8, 128), received, swapped)
    return (dual.reshape(material_fraction.shape), filtered)


def solution(mesh):
    spec = P(("gz", "ba"), None, None)
    return jax.shard_map(
        per_device,
        mesh=mesh,
        in_specs=(spec, spec, spec, spec, P(("gz", "ba"))),
        out_specs=(spec, spec),
        check_vma=False,
    )
```

```python
import functools

import jax
import jax.numpy as jnp
from jax import lax
from jax.experimental import pallas as pl
from jax.experimental.pallas import tpu as pltpu
from jax.sharding import PartitionSpec as P

SLOTS = 4
KMIN = 0.01
HEAT = 0.05
F32 = jnp.float32
I32 = jnp.int32

E_SLAB = 128
E_ZERO = 160
E_TILES = 192
L_INNER = 32
L_UP = 64
L_DOWN = 88
L_SLAB = 112
L_ZERO = 140
L_TILES = 148
X_TILES = 33
Z_SLABS = 72
Z_TILES = 85
DUMMY = 29


def lanes():
    return lax.broadcasted_iota(I32, (8, 128), 1)


def rows():
    return lax.broadcasted_iota(I32, (8, 128), 0)


def take(tile, index):
    return jnp.take_along_axis(tile, index, axis=1)


def row_of(values):
    lane = lanes()
    result = jnp.zeros((8, 128), F32)
    for index, value in enumerate(values):
        result = jnp.where(lane == index, (value + 1).astype(F32), result)
    return result


def position_at(meta, index):
    return meta[0, 0, index].astype(I32) - 1


def as_int(flag):
    return jnp.where(flag, 1, 0).astype(I32)


def pack_kernel(
    place,
    parity_ref,
    mat_in,
    heat_in,
    load_in,
    prior_in,
    near,
    far,
    mat,
    heat,
    load,
    prior,
    sems,
):
    pairs = ((mat_in, mat), (prior_in, prior), (load_in, load), (heat_in, heat))
    fetches = [
        [
            pltpu.make_async_copy(
                source.at[pl.ds(32 * s, 32)], target.at[pl.ds(32 * s, 32)], sems.at[k, s]
            )
            for k, (source, target) in enumerate(pairs)
        ]
        for s in range(SLOTS)
    ]
    for slot_fetches in fetches:
        for fetch in slot_fetches:
            fetch.start()
    parity = parity_ref[0]
    lane = lanes()
    depth = lane // 32
    inside = 32 * (lane % 4)
    pick = (lane % 32) // 4
    mirror = parity == 0
    sides = []
    for out, flip in ((near, mirror), (far, jnp.logical_not(mirror))):
        base = jnp.where(flip, inside + 31, inside)
        sign = jnp.where(flip, -1, 1)
        sides.append(
            (
                out,
                base + sign * depth,
                base,
                base + sign * jnp.maximum(depth - 2, 0),
            )
        )

    def slab(unit, carry):
        row = pl.multiple_of(unit * 8, 8)

        def gather(ref, index):
            tile = take(ref[pl.ds(row, 8), 0:128], index)
            for j in range(1, 8):
                got = take(ref[pl.ds(row, 8), 128 * j : 128 * j + 128], index)
                tile = jnp.where(pick == j, got, tile)
            return tile

        for out, at_depth, at_face, at_load in sides:
            fraction = gather(mat, at_depth)
            warm = gather(heat, at_face)
            dual = gather(prior, at_depth)
            given = gather(load, at_load)
            own = conductivity(fraction)
            third = conduct(own, pltpu.roll(own, 96, 1)) * pltpu.roll(dual, 96, 1)
            given = given + jnp.where(depth == 3, pltpu.roll(third, 64, 1), 0.0)
            out[unit] = jnp.where(depth == 3, warm, fraction)
            out[16 + unit] = jnp.where(depth < 2, dual, given)
        return carry

    for s in range(SLOTS):
        for fetch in fetches[s]:
            fetch.wait()
        lax.fori_loop(4 * s, 4 * s + 4, slab, 0, unroll=2)
    meta = row_of([place[s] for s in range(SLOTS)])
    near[X_TILES - 1] = meta
    far[X_TILES - 1] = meta


def corner_kernel(
    place, near_meta, far_meta, mat, heat, load, prior, near, far, up, down
):
    values = [place[s] for s in range(SLOTS)]
    start = as_int(values[SLOTS - 1] >= 0)
    row = rows()

    def layer(out, to, at, j, rising):
        fraction, warm, given, dual = (
            ref[pl.ds(at, 8), 128 * j : 128 * j + 128] for ref in (mat, heat, load, prior)
        )
        step = 1 if rising else 7
        own = conductivity(fraction)
        beyond = conduct(own, pltpu.roll(own, step, 0)) * pltpu.roll(dual, step, 0)
        given = given + jnp.where(row == (2 if rising else 5), beyond, 0.0)
        spare, two = ((row == 0, row < 2) if rising else (row == 7, row > 5))
        a, b, c = ((5, 4, 2) if rising else (7, 5, 3))
        out[to] = jnp.where(spare, pltpu.roll(warm, a, 0), fraction)
        out[to + 24] = jnp.where(two, pltpu.roll(warm, b, 0), dual)
        out[to + 48] = jnp.where(two, pltpu.roll(warm, c, 0), given)

    for i in range(3):
        top = pl.multiple_of((start + i) * 32 + 24, 8)
        for j in range(8):
            layer(up, 8 * i + j, top, j, True)
            layer(down, 8 * i + j, 32 * i, j, False)
    for b, (meta, source) in enumerate(((near_meta, near), (far_meta, far))):
        listed = [position_at(meta, s) for s in range(SLOTS)]
        values = values + listed
        start = as_int(listed[SLOTS - 1] >= 0)
        for field in range(2):
            for i in range(3):
                to = Z_SLABS + b * 6 + field * 3 + i
                up[to] = source[field * 16 + (start + i) * 4 + 3]
                down[to] = source[field * 16 + i * 4]
    meta_tile = row_of(values)
    up[Z_TILES - 1] = meta_tile
    down[Z_TILES - 1] = meta_tile


def conduct(own, beside):
    return (2.0 * own) * beside / jnp.maximum(own + beside, KMIN)


def conductivity(fraction):
    return KMIN + (1.0 - KMIN) * fraction * fraction * fraction


def cell_of(x, y, z):
    return ((z + 1) * 6 + y + 1) * 4 + x + 1


def clear_cells(cells, zero):
    def clear(index, carry):
        cells[index] = zero
        return carry

    lax.fori_loop(0, 144, clear, 0, unroll=16)


def enter(cells, position, wanted, x, z, tile):
    here = jnp.where(wanted, cell_of(x, position // 2 % 4, z), 144)
    cells[here] = tile
    return jnp.where(wanted, here, DUMMY)


def fill(table, unit, values):
    for k, value in enumerate(values):
        table[unit * 8 + k] = value


class Stencil:
    def __init__(self, weights, stride):
        self.lane = lanes()
        row = rows()
        self.top_row = row == 0
        self.last_row = row == 7
        self.x_cell = self.lane % 32
        self.y_block = self.lane // 32
        self.face_block = self.lane // 4
        self.face_lane = 32 * (self.lane % 4)
        self.weights = weights
        self.stride = stride

    def above(self, tile, other):
        return pltpu.roll(jnp.where(self.top_row, other, tile), 7, 0)

    def below(self, tile, other):
        return pltpu.roll(jnp.where(self.last_row, other, tile), 1, 0)

    def brick(self, table, unit):
        base, up, down, north, south, east, west, px = (table[unit * 8 + k] for k in range(8))
        lane, x_cell = (self.lane, self.x_cell)
        inner = 1 - px
        east_index = jnp.where(px == 1, self.y_block, jnp.maximum(lane - 31, 0))
        west_index = jnp.where(px == 0, self.y_block, jnp.minimum(lane + 31, 127))

        def around(ref, j):
            tile = ref[base + j]
            after = ref[base + j + 1] if j < 7 else ref[north]
            before = ref[base + j - 1] if j > 0 else ref[south + 7]
            over = take(ref[east + inner * j], east_index + 4 * j * px)
            under = take(ref[west + px * j], west_index + 4 * j * inner)
            return tile, (
                jnp.where(x_cell == 31, over, pltpu.roll(tile, 127, 1)),
                jnp.where(x_cell == 0, under, pltpu.roll(tile, 1, 1)),
                pltpu.roll(jnp.where(lane < 32, after, tile), 96, 1),
                pltpu.roll(jnp.where(lane >= 96, before, tile), 32, 1),
                self.above(tile, ref[up + j]),
                self.below(tile, ref[down + j]),
            )

        return base, around

    def slab(self, table, unit):
        at, up, down, north, south, face, column = (table[unit * 8 + k] for k in range(7))
        lane, x_cell = (self.lane, self.x_cell)
        index = self.face_lane + column

        def around(ref):
            tile = ref[at]
            edge = take(ref[face], index)
            for j in range(1, 8):
                edge = jnp.where(self.face_block == j, take(ref[face + j], index), edge)
            return tile, (
                pltpu.roll(tile, 96, 1),
                jnp.where(lane < 32, edge, pltpu.roll(tile, 32, 1)),
                jnp.where(x_cell == 31, pltpu.roll(ref[north], 31, 1), pltpu.roll(tile, 127, 1)),
                jnp.where(x_cell == 0, pltpu.roll(ref[south], 97, 1), pltpu.roll(tile, 1, 1)),
                self.above(tile, ref[up]),
                self.below(tile, ref[down]),
            )

        return at, around

    def first(self, t, source, inverse, dual1, own_kappa, beside_kappa, beside):
        total = jnp.full((8, 128), HEAT, F32)
        flux = source[t]
        for k in range(6):
            weight = conduct(own_kappa, beside_kappa[k])
            self.weights[k * self.stride + t] = weight
            total = total + weight
            flux = flux + weight * beside[k]
        scale = 1.0 / total
        inverse[t] = scale
        dual1[t] = flux * scale

    def later(self, t, source, inverse, beside):
        flux = source[t]
        for k in range(6):
            flux = flux + self.weights[k * self.stride + t] * beside[k]
        return flux * inverse[t]

    def sensitivity(self, t, warm, warms, dual, duals):
        total = jnp.zeros((8, 128), F32)
        for k in range(6):
            total = total + jnp.where(
                self.weights[k * self.stride + t] > 0,
                (warms[k] - warm) * (duals[k] - dual),
                0.0,
            )
        return total


def factor_of(fraction):
    return (-1.5 * (1.0 - KMIN)) * fraction * fraction


def spread(to, first, second, kappa, temperature, source, dual0):
    kappa[to] = conductivity(first)
    dual0[to] = jnp.where(lanes() < 64, second, 0.0)
    source[to] = pltpu.roll(second, 64, 1)
    temperature[to] = pltpu.roll(first, 32, 1)


def shrink_table():
    cell = lax.broadcasted_iota(I32, (512, 128), 0)
    coarse = lax.broadcasted_iota(I32, (512, 128), 1)
    matches = (cell // 64 == coarse // 16) & (cell % 32 // 2 == coarse % 16)
    return jnp.where(matches, 0.125, 0.0).astype(F32)


def restrict(sens, summed, out, count):
    shrink = shrink_table()
    for half in range(2):
        summed[...] = jnp.dot(
            sens[:, 512 * half : 512 * half + 512],
            shrink,
            precision=lax.Precision.HIGHEST,
            preferred_element_type=F32,
        )
        for r in range(count):
            out[half, 8 * r : 8 * r + 8, :] = (
                summed[pl.ds(16 * r, 8, stride=2), :] + summed[pl.ds(16 * r + 1, 8, stride=2), :]
            )


def early_kernel(
    place,
    parity_ref,
    near_meta,
    far_meta,
    mat,
    heat,
    load,
    prior,
    near,
    far,
    dual1,
    dual2,
    coarse,
    cells,
    brick_table,
    slab_table,
    kappa,
    temperature,
    source,
    dual0,
    weights,
    inverse,
    sens,
    summed,
):
    parity = parity_ref[0]
    clear_cells(cells, E_ZERO)
    own = [place[s] for s in range(SLOTS)]
    own_cell = [enter(cells, q, q >= 0, q % 2, q // 8, 32 * s) for s, q in enumerate(own)]
    slab_cell = []
    slab_live = []
    for b, meta in enumerate((near_meta, far_meta)):
        east = parity == b
        column = jnp.where(east, 0, 1)
        x = jnp.where(east, 2, -1)
        for s in range(SLOTS):
            q = position_at(meta, s)
            wanted = (q >= 0) & (q % 2 == column)
            slab_live.append((wanted, q))
            slab_cell.append(
                enter(cells, q, wanted, x, q // 8, E_SLAB + 16 * b + 4 * s)
            )
    for s in range(SLOTS):
        here = own_cell[s]
        px = jnp.where(own[s] >= 0, own[s] % 2, 0)
        lift = jnp.where(own[s] >= 8, 24, 0)
        north, south = (cells[here + 4], cells[here - 4])
        east, west = (cells[here + 1], cells[here - 1])
        above, below = (cells[here + 24], cells[here - 24] + lift)
        for c in range(4):
            base = s * 32 + c * 8
            fill(
                brick_table,
                s * 4 + c,
                (
                    base,
                    base + 8 if c < 3 else above,
                    base - 8 if c > 0 else below,
                    north + 8 * c,
                    south + 8 * c,
                    east + jnp.where(px == 1, c, 8 * c),
                    west + jnp.where(px == 0, c, 8 * c),
                    px,
                ),
            )
    for b in range(2):
        inward = jnp.where(parity == b, -1, 1)
        column = jnp.where(parity == b, 31, 0)
        for s in range(SLOTS):
            here = slab_cell[4 * b + s]
            wanted, q = slab_live[4 * b + s]
            lift = jnp.where(q >= 8, 3, 0)
            north, south = (cells[here + 4], cells[here - 4])
            above, below = (cells[here + 24], cells[here - 24] + lift)
            face = cells[here + inward]
            live = as_int(wanted)
            for c in range(4):
                unit = 16 * b + 4 * s + c
                fill(
                    slab_table,
                    unit,
                    (
                        E_SLAB + unit,
                        E_SLAB + unit + 1 if c < 3 else above,
                        E_SLAB + unit - 1 if c > 0 else below,
                        north + c,
                        south + c,
                        face + 8 * c,
                        column,
                        live,
                    ),
                )

    zeros = jnp.zeros((8, 128), F32)
    for ref in (kappa, temperature, dual0, dual1, dual2):
        for t in range(32):
            ref[E_ZERO + t] = zeros

    def own_unit(unit, carry):
        at = pl.multiple_of(unit * 8, 8)
        active = place[unit // 4] >= 0
        for j in range(8):
            span = slice(128 * j, 128 * j + 128)
            t = unit * 8 + j
            kappa[t] = jnp.where(active, conductivity(mat[pl.ds(at, 8), span]), 0.0)
            source[t] = jnp.where(active, load[pl.ds(at, 8), span], 0.0)
            dual0[t] = prior[pl.ds(at, 8), span]
            temperature[t] = heat[pl.ds(at, 8), span]
        return carry

    lax.fori_loop(0, 16, own_unit, 0)
    for b, message in enumerate((near, far)):
        for t in range(16):
            to = E_SLAB + 16 * b + t
            spread(to, message[t], message[t + 16], kappa, temperature, source, dual0)

    stencil = Stencil(weights, E_TILES)

    def slabs(body):
        def slot(index, carry):
            @pl.when(slab_table[index * 32 + 7] > 0)
            def _():
                for c in range(4):
                    body(*stencil.slab(slab_table, index * 4 + c))

            return carry

        lax.fori_loop(0, 8, slot, 0)

    def bricks(body):
        def two(step, carry):
            for k in range(2):
                unit = 2 * step + k
                base, around = stencil.brick(brick_table, unit)
                for j in range(8):
                    body(unit, base, around, j)
            return carry

        lax.fori_loop(0, 8, two, 0)

    def brick_first(unit, base, around, j):
        own_kappa, beside_kappa = around(kappa, j)
        stencil.first(
            base + j, source, inverse, dual1, own_kappa, beside_kappa, around(dual0, j)[1]
        )

    def slab_first(t, around):
        own_kappa, beside_kappa = around(kappa)
        stencil.first(t, source, inverse, dual1, own_kappa, beside_kappa, around(dual0)[1])

    def brick_second(unit, base, around, j):
        dual2[base + j] = stencil.later(base + j, source, inverse, around(dual1, j)[1])

    def slab_second(t, around):
        dual2[t] = stencil.later(t, source, inverse, around(dual1)[1])

    def brick_third(unit, base, around, j):
        at = pl.multiple_of(unit * 8, 8)
        dual, duals = around(dual2, j)
        warm, warms = around(temperature, j)
        total = stencil.sensitivity(base + j, warm, warms, dual, duals)
        span = slice(128 * j, 128 * j + 128)
        sens[pl.ds(at, 8), span] = factor_of(mat[pl.ds(at, 8), span]) * total

    bricks(brick_first)
    slabs(slab_first)
    bricks(brick_second)
    slabs(slab_second)
    bricks(brick_third)
    restrict(sens, summed, coarse, 8)


def late_kernel(
    parts,
    place,
    parity_ref,
    near_meta,
    far_meta,
    up_meta,
    down_meta,
    mat,
    heat,
    load,
    prior,
    near,
    far,
    z_up,
    z_down,
    early1,
    early2,
    coarse,
    dual_out,
    chunks,
    dual_rows,
    dual_sem,
    cells,
    brick_table,
    slab_table,
    brick_list,
    slab_list,
    kappa,
    temperature,
    source,
    dual0,
    dual1,
    dual2,
    weights,
    inverse,
    factor,
    sens,
    summed,
    edge,
    whole,
    turned,
):
    parity = parity_ref[0]
    lane = lanes()
    row = rows()
    clear_cells(cells, L_ZERO)
    own = [place[s] for s in range(SLOTS)]

    def at_edge(q):
        return ((q >= 0) & (q < 8)) | (q >= 24)

    own_cell = [
        enter(cells, q, at_edge(q), q % 2, q // 8, 8 * s) for s, q in enumerate(own)
    ]
    lists_up = [[position_at(up_meta, 4 * k + s) for s in range(SLOTS)] for k in range(3)]
    lists_down = [[position_at(down_meta, 4 * k + s) for s in range(SLOTS)] for k in range(3)]

    def shifted(listed):
        full = listed[SLOTS - 1] >= 0
        return [jnp.where(full, listed[i + 1], listed[i]) for i in range(3)]

    ups = [listed[:3] for listed in lists_up]
    downs = [shifted(listed) for listed in lists_down]
    brick_live = [at_edge(q) for q in own]
    brick_live += [(q >= 0) & (q < 8) for q in ups[0]]
    brick_live += [q >= 24 for q in downs[0]]
    halo_cell = [
        enter(cells, q, brick_live[4 + i], q % 2, 4, L_UP + 8 * i) for i, q in enumerate(ups[0])
    ]
    halo_cell += [
        enter(cells, q, brick_live[7 + i], q % 2, -1, L_DOWN + 8 * i)
        for i, q in enumerate(downs[0])
    ]
    slab_cell = []
    slab_live = []
    slab_own = []
    for b, meta in enumerate((near_meta, far_meta)):
        east = parity == b
        column = jnp.where(east, 0, 1)
        x = jnp.where(east, 2, -1)
        base = L_SLAB + 14 * b
        mine = [position_at(meta, s) for s in range(SLOTS)]
        slab_own.append(mine)
        tests = [at_edge(q) & (q % 2 == column) for q in mine]
        tests += [(q >= 0) & (q < 8) & (q % 2 == column) for q in ups[1 + b]]
        tests += [(q >= 24) & (q % 2 == column) for q in downs[1 + b]]
        slab_live += tests
        for k, q in enumerate(mine + ups[1 + b] + downs[1 + b]):
            z = q // 8 if k < 4 else 4 if k < 7 else -1
            slab_cell.append(enter(cells, q, tests[k], x, z, base + (k if k < 4 else 4 + k)))

    high = [as_int(q >= 24) for q in own]
    for s in range(SLOTS):
        here = own_cell[s]
        px = jnp.where(own[s] >= 0, own[s] % 2, 0)
        inner = L_INNER + 8 * s
        fill(
            brick_table,
            s,
            (
                jnp.int32(8 * s),
                jnp.where(high[s] == 1, cells[here + 24], inner),
                jnp.where(high[s] == 1, inner, cells[here - 24]),
                cells[here + 4],
                cells[here - 4],
                cells[here + 1],
                cells[here - 1],
                px,
            ),
        )
    for i in range(6):
        here = halo_cell[i]
        q = (ups[0] + downs[0])[i]
        px = jnp.where(q >= 0, q % 2, 0)
        fill(
            brick_table,
            4 + i,
            (
                jnp.int32(L_UP + 8 * i),
                jnp.int32(L_ZERO) if i < 3 else cells[here + 24],
                cells[here - 24] if i < 3 else jnp.int32(L_ZERO),
                cells[here + 4],
                cells[here - 4],
                cells[here + 1],
                cells[here - 1],
                px,
            ),
        )
    for b in range(2):
        inward = jnp.where(parity == b, -1, 1)
        column = jnp.where(parity == b, 31, 0)
        base = L_SLAB + 14 * b
        for k in range(10):
            here = slab_cell[10 * b + k]
            above, below = (cells[here + 24], cells[here - 24])
            if k < 4:
                top = slab_own[b][k] >= 24
                inner = base + 4 + k
                above, below = (jnp.where(top, above, inner), jnp.where(top, inner, below))
            elif k < 7:
                above = jnp.int32(L_ZERO)
            else:
                below = jnp.int32(L_ZERO)
            fill(
                slab_table,
                10 * b + k,
                (
                    jnp.int32(base + (k if k < 4 else 4 + k)),
                    above,
                    below,
                    cells[here + 4],
                    cells[here - 4],
                    cells[here + inward],
                    column,
                ),
            )

    def listed(target, flags):
        count = jnp.int32(0)
        for index, flag in enumerate(flags):
            target[count] = index
            count = count + as_int(flag)
        last = target[jnp.maximum(count - 1, 0)]
        for k in range(3):
            target[count + k] = last
        return count

    brick_count = listed(brick_list, brick_live)
    slab_count = listed(slab_list, slab_live)

    zeros = jnp.zeros((8, 128), F32)
    for ref in (kappa, temperature, dual0, dual1, dual2):
        for t in range(8):
            ref[L_ZERO + t] = zeros

    for s in range(SLOTS):
        active = own[s] >= 0
        for to, chunk in ((8 * s, 3 * high[s]), (L_INNER + 8 * s, 1 + high[s])):
            at = pl.multiple_of(s * 32 + 8 * chunk, 8)
            for j in range(8):
                span = slice(128 * j, 128 * j + 128)
                fraction = mat[pl.ds(at, 8), span]
                kappa[to + j] = jnp.where(active, conductivity(fraction), 0.0)
                dual0[to + j] = prior[pl.ds(at, 8), span]
                temperature[to + j] = heat[pl.ds(at, 8), span]
                if to < L_INNER:
                    source[to + j] = load[pl.ds(at, 8), span]
                    factor[to + j] = factor_of(fraction)
                else:
                    dual1[to + j] = early1[32 * s + 8 * chunk + j]
                    dual2[to + j] = early2[32 * s + 8 * chunk + j]

    for k, message in enumerate((z_up, z_down)):
        for i in range(3):

            @pl.when(brick_live[4 + 3 * k + i])
            def _(k=k, i=i, message=message):
                for j in range(8):
                    t = 8 * i + j
                    to = L_UP + 24 * k + t
                    one, two, three = (message[t], message[24 + t], message[48 + t])
                    a, b, c = ((3, 4, 6) if k else (1, 3, 5))
                    kappa[to] = conductivity(one)
                    dual0[to] = jnp.where(row >= 2 if k else row < 6, two, 0.0)
                    source[to] = three
                    temperature[to] = jnp.where(
                        row == 3 if k else row == 0,
                        pltpu.roll(one, a, 0),
                        jnp.where(
                            row < 6 if k else row < 3,
                            pltpu.roll(two, b, 0),
                            pltpu.roll(three, c, 0),
                        ),
                    )
                    factor[to] = factor_of(one)

    def slab_tile(to, message, at, step):
        spread(to, message[at], message[at + step], kappa, temperature, source, dual0)

    for b, message in enumerate((near, far)):
        base = L_SLAB + 14 * b
        for s in range(SLOTS):
            top = as_int(slab_own[b][s] >= 24)
            slab_tile(base + s, message, 4 * s + 3 * top, 16)
            inner = 4 * s + 1 + top
            slab_tile(base + 4 + s, message, inner, 16)
            dual1[base + 4 + s] = early1[E_SLAB + 16 * b + inner]
            dual2[base + 4 + s] = early2[E_SLAB + 16 * b + inner]
        for i in range(3):
            slab_tile(base + 8 + i, z_up, Z_SLABS + 6 * b + i, 3)
            slab_tile(base + 11 + i, z_down, Z_SLABS + 6 * b + i, 3)

    stencil = Stencil(weights, L_TILES)

    def bricks(body):
        def two(step, carry):
            for k in range(2):
                unit = brick_list[2 * step + k]
                base, around = stencil.brick(brick_table, unit)
                for j in range(8):
                    body(base, around, j)
            return carry

        lax.fori_loop(0, (brick_count + 1) // 2, two, 0)

    def slabs(body):
        def four(step, carry):
            for k in range(4):
                body(*stencil.slab(slab_table, slab_list[4 * step + k]))
            return carry

        lax.fori_loop(0, (slab_count + 3) // 4, four, 0)

    def brick_first(base, around, j):
        own_kappa, beside_kappa = around(kappa, j)
        stencil.first(
            base + j, source, inverse, dual1, own_kappa, beside_kappa, around(dual0, j)[1]
        )

    def slab_first(t, around):
        own_kappa, beside_kappa = around(kappa)
        stencil.first(t, source, inverse, dual1, own_kappa, beside_kappa, around(dual0)[1])

    def brick_second(base, around, j):
        dual2[base + j] = stencil.later(base + j, source, inverse, around(dual1, j)[1])

    def slab_second(t, around):
        dual2[t] = stencil.later(t, source, inverse, around(dual1)[1])

    def brick_third(base, around, j):
        dual, duals = around(dual2, j)
        warm, warms = around(temperature, j)
        total = stencil.sensitivity(base + j, warm, warms, dual, duals)
        at = jnp.where(base < L_INNER, base, base - 32)
        sens[pl.ds(pl.multiple_of(at, 8), 8), 128 * j : 128 * j + 128] = factor[base + j] * total

    bricks(brick_first)
    slabs(slab_first)
    bricks(brick_second)
    slabs(slab_second)
    for s in range(SLOTS):
        for c in range(4):
            for j in range(8):
                dual_rows[32 * s + 8 * c : 32 * s + 8 * c + 8, 128 * j : 128 * j + 128] = early2[
                    32 * s + 8 * c + j
                ]

        @pl.when(brick_live[s])
        def _(s=s):
            at = pl.multiple_of(32 * s + 24 * high[s], 8)
            for j in range(8):
                dual_rows[pl.ds(at, 8), 128 * j : 128 * j + 128] = dual2[8 * s + j]

    writing = pltpu.make_async_copy(dual_rows, dual_out, dual_sem)
    writing.start()
    bricks(brick_third)

    restrict(sens, summed, edge, 5)
    for half in range(2):
        whole[...] = coarse[half]
        for s in range(SLOTS):

            @pl.when(brick_live[s])
            def _(s=s):
                whole[pl.ds(16 * s + 12 * high[s], 4), :] = edge[half, 4 * s : 4 * s + 4, :]

        for r in range(11):
            if r < 8:
                tile = whole[8 * r : 8 * r + 8, :]
            else:
                tile = edge[half, 8 * r - 48 : 8 * r - 40, :]
            for bit in (1, 2, 4):
                low_row = (row & bit) == 0
                low_lane = (lane & (16 * bit)) == 0
                swap_a = pltpu.roll(pltpu.roll(tile, 8 - bit, 0), 16 * bit, 1)
                swap_b = pltpu.roll(pltpu.roll(tile, bit, 0), 128 - 16 * bit, 1)
                tile = jnp.where(low_row == low_lane, tile, jnp.where(low_row, swap_a, swap_b))
            turned[2 * r + half] = tile

    y_block = lane // 32

    planes = 64 // parts
    level = [jnp.where(q >= 0, q // 8, 9) for q in own]

    def count(test):
        return functools.reduce(lambda a, b: a + b, [as_int(test(v)) for v in level])

    before = [count(lambda v, z=z: v < z) for z in range(5)]

    def nth(z, e):
        index = before[z] + e
        valid = index < before[z + 1]
        slot = jnp.minimum(index, SLOTS - 1)
        code = jnp.where(valid, place[slot] - 8 * z, -1)
        return slot, code

    for d in range(parts):
        z = d * planes // 16
        half = d * planes % 16 // 8
        codes = []
        for e in range(3):
            slot, code = nth(z, e)
            codes.append(code)
            for k in range(2):
                chunks[d * 8 + 2 * e + k] = turned[(slot * 2 + half) * 2 + k]
        start = d * planes % 8 == 0
        end = (d + 1) * planes % 8 == 0
        if planes >= 8:
            outside = -1 if half == 0 else 1
        else:
            outside = -1 if start else 1 if end else 0
        beyond = half + outside
        beside = [zeros, zeros]
        for e in range(3):
            if outside == 0:
                tile_at, lane_at, code = (0, 0, jnp.int32(-1))
            elif beyond in (0, 1):
                slot, code = nth(z, e)
                tile_at, lane_at = (slot * 2 + beyond, 96 if outside < 0 else 0)
            elif 0 <= z + outside <= 3:
                slot, code = nth(z + outside, e)
                tile_at, lane_at = (slot * 2 + (1 if outside < 0 else 0), 96 if outside < 0 else 0)
            elif outside < 0:
                q = downs[0][e]
                code = jnp.where(q >= 24, q - 24, -1)
                tile_at, lane_at = (8 + (3 + e) // 2, 64 * ((3 + e) % 2) + 32)
            else:
                q = ups[0][e]
                code = jnp.where((q >= 0) & (q < 8), q, -1)
                tile_at, lane_at = (8 + e // 2, 64 * (e % 2))
            codes.append(code)
            for k in range(2):
                tile = turned[tile_at * 2 + k]
                shift = (32 * e - lane_at) % 128
                if shift:
                    tile = pltpu.roll(tile, shift, 1)
                beside[k] = jnp.where(y_block == e, tile, beside[k])
        for e, code in enumerate(codes):
            beside[0] = jnp.where(lane == 96 + e, (code + 1).astype(F32), beside[0])
        for k in range(2):
            chunks[d * 8 + 6 + k] = beside[k]
    writing.wait()


def filter_kernel(parts, planes, across, spot, meta, received, swapped, out, grid, once):
    member = spot[0]
    depth = planes + 4
    wide = parts // across
    lane = lanes()
    row = rows()
    group_lane = lane // 16
    zeros = jnp.zeros((8, 128), F32)

    def clear(index, carry):
        grid[index] = zeros
        return carry

    lax.fori_loop(0, depth * 8 * wide, clear, 0, unroll=8)
    begin = member * planes
    half = begin % 16 // 8
    side = jnp.where(begin % 8 == 0, 0, planes + 2) if planes < 8 else half * (planes + 2)

    def place_plane(tile, lane_at, window, code, k, column, tile_x):
        at = (column * 2 + code % 2) % 8
        moved = pltpu.roll(tile, (at * 16 - lane_at + 256) % 128, 1)
        where_to = (window * 8 + code // 2 * 2 + k) * wide + tile_x
        grid[where_to] = jnp.where(group_lane == at, moved, grid[where_to])

    def from_device(column, carry):
        tile_x = column // across
        for e in range(3):
            code = meta[column, 0, 0, 96 + e].astype(I32) - 1

            @pl.when(code >= 0)
            def _(e=e, code=code):
                for k in range(2):
                    tile = received[column * 8 + 2 * e + k]
                    if planes == 8:
                        for p in range(8):
                            place_plane(tile, 16 * p, p + 2, code, k, column, tile_x)
                        other = swapped[column * 8 + 2 * e + k]
                        for p in range(2):
                            place_plane(
                                other,
                                jnp.where(half == 0, 16 * p, 96 + 16 * p),
                                jnp.where(half == 0, 10 + p, p),
                                code,
                                k,
                                column,
                                tile_x,
                            )
                    else:
                        for window in range(depth):
                            p = begin % 8 + window - 2

                            @pl.when((p >= 0) & (p < 8))
                            def _(tile=tile, p=p, window=window, k=k):
                                place_plane(tile, 16 * p, window, code, k, column, tile_x)

        for e in range(3):
            code = meta[column, 0, 0, 99 + e].astype(I32) - 1

            @pl.when(code >= 0)
            def _(e=e, code=code):
                for k in range(2):
                    tile = received[column * 8 + 6 + k]
                    for p in range(2):
                        place_plane(
                            tile, 32 * e + 16 * p, side + p, code, k, column, tile_x
                        )

        return carry

    lax.fori_loop(0, parts, from_device, 0)

    def relax(ref, window, y, x):
        here = (window * 8 + y) * wide + x
        tile = ref[here]
        north = ref[here + wide] if y < 7 else zeros
        south = ref[here - wide] if y > 0 else zeros
        east = ref[here + 1] if x < wide - 1 else zeros
        west = ref[here - 1] if x > 0 else zeros
        near = ref[here + 8 * wide] + ref[here - 8 * wide]
        near = near + pltpu.roll(jnp.where(row == 0, north, tile), 7, 0)
        near = near + pltpu.roll(jnp.where(row == 7, south, tile), 1, 0)
        near = near + pltpu.roll(jnp.where(lane == 0, east, tile), 127, 1)
        near = near + pltpu.roll(jnp.where(lane == 127, west, tile), 1, 1)
        return (grid[here] + 2.0 * near) * (1.0 / 13.0)

    first = spot[1] == 0
    last = spot[1] == spot[2] - 1

    def sweep_once(window, carry):
        gone = (first & (window < 2)) | (last & (window >= planes + 2))
        keep = jnp.where(gone, 0.0, 1.0).astype(F32)
        for y in range(8):
            for x in range(wide):
                once[(window * 8 + y) * wide + x] = relax(grid, window, y, x) * keep
        return carry

    lax.fori_loop(1, depth - 1, sweep_once, 0)

    def sweep_again(window, carry):
        for y in range(8):
            for x in range(wide):
                out[window - 2, 8 * y : 8 * y + 8, 128 * x : 128 * x + 128] = relax(
                    once, window, y, x
                )
        return carry

    lax.fori_loop(2, depth - 2, sweep_again, 0)


VMEM = pl.BlockSpec(memory_space=pltpu.VMEM)
SMEM = pl.BlockSpec(memory_space=pltpu.SMEM)
HBM = pl.BlockSpec(memory_space=pltpu.HBM)
BIG = 32 * 1024 * 1024
WHOLE = 60 * 1024 * 1024


def meta_of(index):
    return pl.BlockSpec((1, 8, 128), lambda i: (index, 0, 0), memory_space=pltpu.SMEM)


def params(limit=BIG):
    return pltpu.CompilerParams(vmem_limit_bytes=limit)


def tiles(count):
    return jax.ShapeDtypeStruct((count, 8, 128), F32)


def per_device(
    material_fraction, primal_heat_solution, dual_load, dual_prior_design, holder_cube_location
):
    parts = lax.axis_size("ba")
    groups = lax.axis_size("gz")
    member = lax.axis_index("ba")
    group = lax.axis_index("gz")
    planes = 64 // parts
    parity = (member % 2).reshape(1).astype(I32)
    place = holder_cube_location
    fields = [
        field.reshape(128, 1024)
        for field in (material_fraction, primal_heat_solution, dual_load, dual_prior_design)
    ]
    near, far = pl.pallas_call(
        pack_kernel,
        out_shape=(tiles(X_TILES), tiles(X_TILES)),
        in_specs=[SMEM, SMEM, HBM, HBM, HBM, HBM],
        out_specs=(VMEM, VMEM),
        scratch_shapes=[pltpu.VMEM((128, 1024), F32)] * 4 + [pltpu.SemaphoreType.DMA((4, 4))],
        compiler_params=params(WHOLE),
        name="pack",
    )(place, parity, *fields)
    inner = [(i, i ^ 1) for i in range(parts)]
    outer = [(i, i + 1 if i % 2 else i - 1) for i in range(1, parts - 1)]
    near = lax.ppermute(near, "ba", inner)
    far = lax.ppermute(far, "ba", outer)
    up, down = pl.pallas_call(
        corner_kernel,
        out_shape=(tiles(Z_TILES), tiles(Z_TILES)),
        in_specs=[SMEM, meta_of(X_TILES - 1), meta_of(X_TILES - 1)] + [VMEM] * 6,
        out_specs=(VMEM, VMEM),
        grid=(1,),
        compiler_params=params(),
        name="corners",
    )(place, near, far, *fields, near, far)
    rising = [(i, i + 1) for i in range(groups - 1)]
    falling = [(i + 1, i) for i in range(groups - 1)]
    from_below = lax.ppermute(up, "gz", rising)
    from_above = lax.ppermute(down, "gz", falling)
    meta_z = meta_of(Z_TILES - 1)
    meta_x = meta_of(X_TILES - 1)
    early = pltpu.VMEM((E_TILES, 8, 128), F32)
    dual1, dual2, coarse = pl.pallas_call(
        early_kernel,
        out_shape=(tiles(E_TILES), tiles(E_TILES), jax.ShapeDtypeStruct((2, 64, 128), F32)),
        in_specs=[SMEM, SMEM, meta_x, meta_x] + [VMEM] * 6,
        out_specs=(VMEM, VMEM, VMEM),
        scratch_shapes=[
            pltpu.SMEM((145,), I32),
            pltpu.SMEM((16 * 8,), I32),
            pltpu.SMEM((32 * 8,), I32),
            early,
            early,
            early,
            early,
            pltpu.VMEM((6 * E_TILES, 8, 128), F32),
            early,
            pltpu.VMEM((128, 1024), F32),
            pltpu.VMEM((128, 128), F32),
        ],
        grid=(1,),
        cost_estimate=pl.CostEstimate(flops=10**9, bytes_accessed=3 * 10**7, transcendentals=0),
        compiler_params=params(),
        name="early",
    )(place, parity, near, far, *fields, near, far)
    late = pltpu.VMEM((L_TILES, 8, 128), F32)
    dual, chunks = pl.pallas_call(
        functools.partial(late_kernel, parts),
        out_shape=(jax.ShapeDtypeStruct((128, 1024), F32), tiles(8 * parts)),
        in_specs=[SMEM, SMEM, meta_x, meta_x, meta_z, meta_z] + [VMEM] * 11,
        out_specs=(HBM, VMEM),
        scratch_shapes=[
            pltpu.VMEM((128, 1024), F32),
            pltpu.SemaphoreType.DMA,
            pltpu.SMEM((145,), I32),
            pltpu.SMEM((10 * 8,), I32),
            pltpu.SMEM((20 * 8,), I32),
            pltpu.SMEM((16,), I32),
            pltpu.SMEM((24,), I32),
            late,
            late,
            late,
            late,
            late,
            late,
            pltpu.VMEM((6 * L_TILES, 8, 128), F32),
            late,
            pltpu.VMEM((L_SLAB, 8, 128), F32),
            pltpu.VMEM((80, 1024), F32),
            pltpu.VMEM((80, 128), F32),
            pltpu.VMEM((2, 40, 128), F32),
            pltpu.VMEM((64, 128), F32),
            pltpu.VMEM((22, 8, 128), F32),
        ],
        grid=(1,),
        compiler_params=params(),
        name="late",
    )(
        place,
        parity,
        near,
        far,
        from_above,
        from_below,
        *fields,
        near,
        far,
        from_above,
        from_below,
        dual1,
        dual2,
        coarse,
    )
    received = lax.all_to_all(chunks, "ba", split_axis=0, concat_axis=0, tiled=True)
    swapped = lax.ppermute(received, "ba", inner) if planes == 8 else received
    spot = jnp.stack([member, group * parts + member, jnp.int32(groups * parts)]).astype(I32)
    wide = 32 * parts // 128
    filtered = pl.pallas_call(
        functools.partial(filter_kernel, parts, planes, 4),
        out_shape=jax.ShapeDtypeStruct((planes, 64, 32 * parts), F32),
        in_specs=[
            SMEM,
            pl.BlockSpec(
                (parts, 1, 8, 128), lambda i: (0, 6, 0, 0), memory_space=pltpu.SMEM
            ),
            VMEM,
            VMEM,
        ],
        out_specs=VMEM,
        scratch_shapes=[
            pltpu.VMEM(((planes + 4) * 8 * wide, 8, 128), F32),
            pltpu.VMEM(((planes + 4) * 8 * wide, 8, 128), F32),
        ],
        grid=(1,),
        compiler_params=params(),
        name="smooth",
    )(spot, received.reshape(parts, 8, 8, 128), received, swapped)
    return (dual.reshape(material_fraction.shape), filtered)


def solution(mesh):
    spec = P(("gz", "ba"), None, None)
    return jax.shard_map(
        per_device,
        mesh=mesh,
        in_specs=(spec, spec, spec, spec, P(("gz", "ba"))),
        out_specs=(spec, spec),
        check_vma=False,
    )
```

```python
import functools

import jax
import jax.numpy as jnp
from jax import lax
from jax.experimental import pallas as pl
from jax.experimental.pallas import tpu as pltpu
from jax.sharding import PartitionSpec as P

SLOTS = 4
KMIN = 0.01
HEAT = 0.05
F32 = jnp.float32
I32 = jnp.int32

E_SLAB = 128
E_ZERO = 160
E_TILES = 192
L_INNER = 32
L_UP = 64
L_DOWN = 88
L_SLAB = 112
L_ZERO = 140
L_TILES = 148
X_TILES = 33
Z_SLABS = 72
Z_TILES = 85
DUMMY = 29


def lanes():
    return lax.broadcasted_iota(I32, (8, 128), 1)


def rows():
    return lax.broadcasted_iota(I32, (8, 128), 0)


def take(tile, index):
    return jnp.take_along_axis(tile, index, axis=1)


def row_of(values):
    lane = lanes()
    result = jnp.zeros((8, 128), F32)
    for index, value in enumerate(values):
        result = jnp.where(lane == index, (value + 1).astype(F32), result)
    return result


def position_at(meta, index):
    return meta[0, 0, index].astype(I32) - 1


def as_int(flag):
    return jnp.where(flag, 1, 0).astype(I32)


def pack_kernel(
    place,
    parity_ref,
    mat_in,
    heat_in,
    load_in,
    prior_in,
    near,
    far,
    mat,
    heat,
    load,
    prior,
    parts,
    sems,
):
    pairs = ((mat_in, mat), (heat_in, heat), (prior_in, prior), (load_in, load))
    fetches = [
        [
            pltpu.make_async_copy(
                source.at[pl.ds(32 * s, 32)], target.at[pl.ds(32 * s, 32)], sems.at[k, s]
            )
            for k, (source, target) in enumerate(pairs)
        ]
        for s in range(SLOTS)
    ]
    for slot_fetches in fetches:
        for fetch in slot_fetches:
            fetch.start()
    cell = lax.broadcasted_iota(I32, (1024, 256), 0)
    column = lax.broadcasted_iota(I32, (1024, 256), 1)
    deep = column % 128 // 32
    flipped = (column // 128) != parity_ref[0]
    wanted = 32 * (column % 32) + jnp.where(flipped, deep, 31 - deep)
    pick = jnp.where(cell == wanted, 1.0, 0.0).astype(jnp.bfloat16)
    depth = lanes() // 32
    for s in range(SLOTS):
        for fetch in fetches[s]:
            fetch.wait()
        for k, ref in enumerate((mat, heat, prior, load)):
            rest = ref[32 * s : 32 * s + 32, :]
            for third in range(3):
                part = rest.astype(jnp.bfloat16)
                at = (3 * k + third) * 32
                parts[at : at + 32, :] = part
                rest = rest - part.astype(F32)
        moved = jnp.dot(parts[...], pick, preferred_element_type=F32)
        for side, out in enumerate((near, far)):
            for c in range(4):

                def field(k):
                    high, mid, low = (
                        moved[
                            (3 * k + third) * 32 + 8 * c : (3 * k + third) * 32 + 8 * c + 8,
                            128 * side : 128 * side + 128,
                        ]
                        for third in range(3)
                    )
                    return (high + mid) + low

                fraction, warm, dual, given = (field(k) for k in range(4))
                own = conductivity(fraction)
                beyond = conduct(own, pltpu.roll(own, 96, 1)) * pltpu.roll(dual, 96, 1)
                given = pltpu.roll(given + jnp.where(depth == 1, beyond, 0.0), 64, 1)
                unit = 4 * s + c
                out[unit] = jnp.where(depth == 3, pltpu.roll(warm, 96, 1), fraction)
                out[16 + unit] = jnp.where(depth < 2, dual, given)
    meta = row_of([place[s] for s in range(SLOTS)])
    near[X_TILES - 1] = meta
    far[X_TILES - 1] = meta


def corner_kernel(
    place, near_meta, far_meta, mat, heat, load, prior, near, far, up, down
):
    values = [place[s] for s in range(SLOTS)]
    start = as_int(values[SLOTS - 1] >= 0)
    row = rows()

    def layer(out, to, at, j, rising):
        fraction, warm, given, dual = (
            ref[pl.ds(at, 8), 128 * j : 128 * j + 128] for ref in (mat, heat, load, prior)
        )
        step = 1 if rising else 7
        own = conductivity(fraction)
        beyond = conduct(own, pltpu.roll(own, step, 0)) * pltpu.roll(dual, step, 0)
        given = given + jnp.where(row == (2 if rising else 5), beyond, 0.0)
        spare, two = ((row == 0, row < 2) if rising else (row == 7, row > 5))
        a, b, c = ((5, 4, 2) if rising else (7, 5, 3))
        out[to] = jnp.where(spare, pltpu.roll(warm, a, 0), fraction)
        out[to + 24] = jnp.where(two, pltpu.roll(warm, b, 0), dual)
        out[to + 48] = jnp.where(two, pltpu.roll(warm, c, 0), given)

    for i in range(3):
        top = pl.multiple_of((start + i) * 32 + 24, 8)
        for j in range(8):
            layer(up, 8 * i + j, top, j, True)
            layer(down, 8 * i + j, 32 * i, j, False)
    for b, (meta, source) in enumerate(((near_meta, near), (far_meta, far))):
        listed = [position_at(meta, s) for s in range(SLOTS)]
        values = values + listed
        start = as_int(listed[SLOTS - 1] >= 0)
        for field in range(2):
            for i in range(3):
                to = Z_SLABS + b * 6 + field * 3 + i
                up[to] = source[field * 16 + (start + i) * 4 + 3]
                down[to] = source[field * 16 + i * 4]
    meta_tile = row_of(values)
    up[Z_TILES - 1] = meta_tile
    down[Z_TILES - 1] = meta_tile


def conduct(own, beside):
    return (2.0 * own) * beside / jnp.maximum(own + beside, KMIN)


def conductivity(fraction):
    return KMIN + (1.0 - KMIN) * fraction * fraction * fraction


def cell_of(x, y, z):
    return ((z + 1) * 6 + y + 1) * 4 + x + 1


def clear_cells(cells, zero):
    def clear(index, carry):
        cells[index] = zero
        return carry

    lax.fori_loop(0, 144, clear, 0, unroll=16)


def enter(cells, position, wanted, x, z, tile):
    here = jnp.where(wanted, cell_of(x, position // 2 % 4, z), 144)
    cells[here] = tile
    return jnp.where(wanted, here, DUMMY)


def fill(table, unit, values):
    for k, value in enumerate(values):
        table[unit * 8 + k] = value


class Stencil:
    def __init__(self, weights, stride):
        self.lane = lanes()
        row = rows()
        self.top_row = row == 0
        self.last_row = row == 7
        self.x_cell = self.lane % 32
        self.y_block = self.lane // 32
        self.face_block = self.lane // 4
        self.face_lane = 32 * (self.lane % 4)
        self.weights = weights
        self.stride = stride

    def above(self, tile, other):
        return pltpu.roll(jnp.where(self.top_row, other, tile), 7, 0)

    def below(self, tile, other):
        return pltpu.roll(jnp.where(self.last_row, other, tile), 1, 0)

    def brick(self, table, unit):
        base, up, down, north, south, east, west, px = (table[unit * 8 + k] for k in range(8))
        lane, x_cell = (self.lane, self.x_cell)
        own_lane = 31 * px
        brick_at = jnp.where(px == 1, west, east)
        slab_at = jnp.where(px == 1, east, west)
        from_brick = x_cell == own_lane
        to_brick = x_cell == 31 - own_lane
        index = jnp.where(to_brick, 32 * self.y_block + own_lane, self.y_block)
        step = jnp.where(to_brick, 0, 4)

        def around(ref, j):
            tile = ref[base + j]
            after = ref[base + j + 1] if j < 7 else ref[north]
            before = ref[base + j - 1] if j > 0 else ref[south + 7]
            beside = ref[slab_at]
            moved = 0
            if j == 0:
                beside, moved = (pltpu.roll(beside, 4, 1), 1)
            elif j == 7:
                beside, moved = (jnp.where(px == 1, pltpu.roll(beside, 4, 1), beside), px)
            both = jnp.where(from_brick, ref[brick_at + j], beside)
            edge = take(both, index + step * (j + moved))
            return tile, (
                jnp.where(x_cell == 31, edge, pltpu.roll(tile, 127, 1)),
                jnp.where(x_cell == 0, edge, pltpu.roll(tile, 1, 1)),
                pltpu.roll(jnp.where(lane < 32, after, tile), 96, 1),
                pltpu.roll(jnp.where(lane >= 96, before, tile), 32, 1),
                self.above(tile, ref[up + j]),
                self.below(tile, ref[down + j]),
            )

        return base, around

    def slab(self, table, unit):
        at, up, down, north, south, face, column = (table[unit * 8 + k] for k in range(7))
        lane, x_cell = (self.lane, self.x_cell)
        index = self.face_lane + column

        def around(ref):
            tile = ref[at]
            edge = take(ref[face], index)
            for j in range(1, 8):
                edge = jnp.where(self.face_block == j, take(ref[face + j], index), edge)
            return tile, (
                pltpu.roll(tile, 96, 1),
                jnp.where(lane < 32, edge, pltpu.roll(tile, 32, 1)),
                jnp.where(x_cell == 31, pltpu.roll(ref[north], 31, 1), pltpu.roll(tile, 127, 1)),
                jnp.where(x_cell == 0, pltpu.roll(ref[south], 97, 1), pltpu.roll(tile, 1, 1)),
                self.above(tile, ref[up]),
                self.below(tile, ref[down]),
            )

        return at, around

    def first(self, t, source, inverse, dual1, own_kappa, beside_kappa, beside):
        total = jnp.full((8, 128), HEAT, F32)
        flux = source[t]
        for k in range(6):
            weight = conduct(own_kappa, beside_kappa[k])
            self.weights[k * self.stride + t] = weight
            total = total + weight
            flux = flux + weight * beside[k]
        scale = 1.0 / total
        inverse[t] = scale
        dual1[t] = flux * scale

    def later(self, t, source, inverse, beside):
        flux = source[t]
        for k in range(6):
            flux = flux + self.weights[k * self.stride + t] * beside[k]
        return flux * inverse[t]

    def sensitivity(self, t, warm, warms, dual, duals):
        total = jnp.zeros((8, 128), F32)
        for k in range(6):
            total = total + jnp.where(
                self.weights[k * self.stride + t] > 0,
                (warms[k] - warm) * (duals[k] - dual),
                0.0,
            )
        return total


def factor_of(fraction):
    return (-1.5 * (1.0 - KMIN)) * fraction * fraction


def spread(to, first, second, kappa, temperature, source, dual0):
    kappa[to] = conductivity(first)
    dual0[to] = jnp.where(lanes() < 64, second, 0.0)
    source[to] = pltpu.roll(second, 64, 1)
    temperature[to] = pltpu.roll(first, 32, 1)


def shrink_table():
    cell = lax.broadcasted_iota(I32, (512, 128), 0)
    coarse = lax.broadcasted_iota(I32, (512, 128), 1)
    matches = (cell // 64 == coarse // 16) & (cell % 32 // 2 == coarse % 16)
    return jnp.where(matches, 0.125, 0.0).astype(F32)


def restrict(sens, summed, out, count):
    shrink = shrink_table()
    for half in range(2):
        summed[...] = jnp.dot(
            sens[:, 512 * half : 512 * half + 512],
            shrink,
            precision=lax.Precision.HIGHEST,
            preferred_element_type=F32,
        )
        for r in range(count):
            out[half, 8 * r : 8 * r + 8, :] = (
                summed[pl.ds(16 * r, 8, stride=2), :] + summed[pl.ds(16 * r + 1, 8, stride=2), :]
            )


def early_kernel(
    place,
    parity_ref,
    near_meta,
    far_meta,
    mat,
    heat,
    load,
    prior,
    near,
    far,
    dual1,
    dual2,
    coarse,
    cells,
    brick_table,
    slab_table,
    kappa,
    temperature,
    source,
    dual0,
    weights,
    inverse,
    sens,
    summed,
):
    parity = parity_ref[0]
    clear_cells(cells, E_ZERO)
    own = [place[s] for s in range(SLOTS)]
    own_cell = [enter(cells, q, q >= 0, q % 2, q // 8, 32 * s) for s, q in enumerate(own)]
    slab_cell = []
    slab_live = []
    for b, meta in enumerate((near_meta, far_meta)):
        east = parity == b
        column = jnp.where(east, 0, 1)
        x = jnp.where(east, 2, -1)
        for s in range(SLOTS):
            q = position_at(meta, s)
            wanted = (q >= 0) & (q % 2 == column)
            slab_live.append((wanted, q))
            slab_cell.append(
                enter(cells, q, wanted, x, q // 8, E_SLAB + 16 * b + 4 * s)
            )
    for s in range(SLOTS):
        here = own_cell[s]
        px = jnp.where(own[s] >= 0, own[s] % 2, 0)
        lift = jnp.where(own[s] >= 8, 24, 0)
        north, south = (cells[here + 4], cells[here - 4])
        east, west = (cells[here + 1], cells[here - 1])
        above, below = (cells[here + 24], cells[here - 24] + lift)
        for c in range(4):
            base = s * 32 + c * 8
            fill(
                brick_table,
                s * 4 + c,
                (
                    base,
                    base + 8 if c < 3 else above,
                    base - 8 if c > 0 else below,
                    north + 8 * c,
                    south + 8 * c,
                    east + jnp.where(px == 1, c, 8 * c),
                    west + jnp.where(px == 0, c, 8 * c),
                    px,
                ),
            )
    for b in range(2):
        inward = jnp.where(parity == b, -1, 1)
        column = jnp.where(parity == b, 31, 0)
        for s in range(SLOTS):
            here = slab_cell[4 * b + s]
            wanted, q = slab_live[4 * b + s]
            lift = jnp.where(q >= 8, 3, 0)
            north, south = (cells[here + 4], cells[here - 4])
            above, below = (cells[here + 24], cells[here - 24] + lift)
            face = cells[here + inward]
            live = as_int(wanted)
            for c in range(4):
                unit = 16 * b + 4 * s + c
                fill(
                    slab_table,
                    unit,
                    (
                        E_SLAB + unit,
                        E_SLAB + unit + 1 if c < 3 else above,
                        E_SLAB + unit - 1 if c > 0 else below,
                        north + c,
                        south + c,
                        face + 8 * c,
                        column,
                        live,
                    ),
                )

    zeros = jnp.zeros((8, 128), F32)
    for ref in (kappa, temperature, dual0, dual1, dual2):
        for t in range(32):
            ref[E_ZERO + t] = zeros

    def own_unit(unit, carry):
        at = pl.multiple_of(unit * 8, 8)
        active = place[unit // 4] >= 0
        for j in range(8):
            span = slice(128 * j, 128 * j + 128)
            t = unit * 8 + j
            kappa[t] = jnp.where(active, conductivity(mat[pl.ds(at, 8), span]), 0.0)
            source[t] = jnp.where(active, load[pl.ds(at, 8), span], 0.0)
            dual0[t] = prior[pl.ds(at, 8), span]
            temperature[t] = heat[pl.ds(at, 8), span]
        return carry

    lax.fori_loop(0, 16, own_unit, 0)
    for b, message in enumerate((near, far)):
        for t in range(16):
            to = E_SLAB + 16 * b + t
            spread(to, message[t], message[t + 16], kappa, temperature, source, dual0)

    stencil = Stencil(weights, E_TILES)

    def slabs(body):
        def slot(index, carry):
            @pl.when(slab_table[index * 32 + 7] > 0)
            def _():
                for c in range(4):
                    body(*stencil.slab(slab_table, index * 4 + c))

            return carry

        lax.fori_loop(0, 8, slot, 0)

    def bricks(body):
        def four(step, carry):
            for k in range(4):
                unit = 4 * step + k
                base, around = stencil.brick(brick_table, unit)
                for j in range(8):
                    body(unit, base, around, j)
            return carry

        lax.fori_loop(0, 4, four, 0)

    def brick_first(unit, base, around, j):
        own_kappa, beside_kappa = around(kappa, j)
        stencil.first(
            base + j, source, inverse, dual1, own_kappa, beside_kappa, around(dual0, j)[1]
        )

    def slab_first(t, around):
        own_kappa, beside_kappa = around(kappa)
        stencil.first(t, source, inverse, dual1, own_kappa, beside_kappa, around(dual0)[1])

    def brick_second(unit, base, around, j):
        dual2[base + j] = stencil.later(base + j, source, inverse, around(dual1, j)[1])

    def slab_second(t, around):
        dual2[t] = stencil.later(t, source, inverse, around(dual1)[1])

    def brick_third(unit, base, around, j):
        at = pl.multiple_of(unit * 8, 8)
        dual, duals = around(dual2, j)
        warm, warms = around(temperature, j)
        total = stencil.sensitivity(base + j, warm, warms, dual, duals)
        span = slice(128 * j, 128 * j + 128)
        sens[pl.ds(at, 8), span] = factor_of(mat[pl.ds(at, 8), span]) * total

    bricks(brick_first)
    slabs(slab_first)
    bricks(brick_second)
    slabs(slab_second)
    bricks(brick_third)
    restrict(sens, summed, coarse, 8)


def late_kernel(
    parts,
    place,
    parity_ref,
    near_meta,
    far_meta,
    up_meta,
    down_meta,
    mat,
    heat,
    load,
    prior,
    near,
    far,
    z_up,
    z_down,
    early1,
    early2,
    coarse,
    dual_out,
    chunks,
    dual_rows,
    dual_sem,
    cells,
    brick_table,
    slab_table,
    brick_list,
    slab_list,
    kappa,
    temperature,
    source,
    dual0,
    dual1,
    dual2,
    weights,
    inverse,
    factor,
    sens,
    summed,
    edge,
    whole,
    turned,
):
    parity = parity_ref[0]
    lane = lanes()
    row = rows()
    clear_cells(cells, L_ZERO)
    own = [place[s] for s in range(SLOTS)]

    def at_edge(q):
        return ((q >= 0) & (q < 8)) | (q >= 24)

    own_cell = [
        enter(cells, q, at_edge(q), q % 2, q // 8, 8 * s) for s, q in enumerate(own)
    ]
    lists_up = [[position_at(up_meta, 4 * k + s) for s in range(SLOTS)] for k in range(3)]
    lists_down = [[position_at(down_meta, 4 * k + s) for s in range(SLOTS)] for k in range(3)]

    def shifted(listed):
        full = listed[SLOTS - 1] >= 0
        return [jnp.where(full, listed[i + 1], listed[i]) for i in range(3)]

    ups = [listed[:3] for listed in lists_up]
    downs = [shifted(listed) for listed in lists_down]
    brick_live = [at_edge(q) for q in own]
    brick_live += [(q >= 0) & (q < 8) for q in ups[0]]
    brick_live += [q >= 24 for q in downs[0]]
    halo_cell = [
        enter(cells, q, brick_live[4 + i], q % 2, 4, L_UP + 8 * i) for i, q in enumerate(ups[0])
    ]
    halo_cell += [
        enter(cells, q, brick_live[7 + i], q % 2, -1, L_DOWN + 8 * i)
        for i, q in enumerate(downs[0])
    ]
    slab_cell = []
    slab_live = []
    slab_own = []
    for b, meta in enumerate((near_meta, far_meta)):
        east = parity == b
        column = jnp.where(east, 0, 1)
        x = jnp.where(east, 2, -1)
        base = L_SLAB + 14 * b
        mine = [position_at(meta, s) for s in range(SLOTS)]
        slab_own.append(mine)
        tests = [at_edge(q) & (q % 2 == column) for q in mine]
        tests += [(q >= 0) & (q < 8) & (q % 2 == column) for q in ups[1 + b]]
        tests += [(q >= 24) & (q % 2 == column) for q in downs[1 + b]]
        slab_live += tests
        for k, q in enumerate(mine + ups[1 + b] + downs[1 + b]):
            z = q // 8 if k < 4 else 4 if k < 7 else -1
            slab_cell.append(enter(cells, q, tests[k], x, z, base + (k if k < 4 else 4 + k)))

    high = [as_int(q >= 24) for q in own]
    for s in range(SLOTS):
        here = own_cell[s]
        px = jnp.where(own[s] >= 0, own[s] % 2, 0)
        inner = L_INNER + 8 * s
        fill(
            brick_table,
            s,
            (
                jnp.int32(8 * s),
                jnp.where(high[s] == 1, cells[here + 24], inner),
                jnp.where(high[s] == 1, inner, cells[here - 24]),
                cells[here + 4],
                cells[here - 4],
                cells[here + 1],
                cells[here - 1],
                px,
            ),
        )
    for i in range(6):
        here = halo_cell[i]
        q = (ups[0] + downs[0])[i]
        px = jnp.where(q >= 0, q % 2, 0)
        fill(
            brick_table,
            4 + i,
            (
                jnp.int32(L_UP + 8 * i),
                jnp.int32(L_ZERO) if i < 3 else cells[here + 24],
                cells[here - 24] if i < 3 else jnp.int32(L_ZERO),
                cells[here + 4],
                cells[here - 4],
                cells[here + 1],
                cells[here - 1],
                px,
            ),
        )
    for b in range(2):
        inward = jnp.where(parity == b, -1, 1)
        column = jnp.where(parity == b, 31, 0)
        base = L_SLAB + 14 * b
        for k in range(10):
            here = slab_cell[10 * b + k]
            above, below = (cells[here + 24], cells[here - 24])
            if k < 4:
                top = slab_own[b][k] >= 24
                inner = base + 4 + k
                above, below = (jnp.where(top, above, inner), jnp.where(top, inner, below))
            elif k < 7:
                above = jnp.int32(L_ZERO)
            else:
                below = jnp.int32(L_ZERO)
            fill(
                slab_table,
                10 * b + k,
                (
                    jnp.int32(base + (k if k < 4 else 4 + k)),
                    above,
                    below,
                    cells[here + 4],
                    cells[here - 4],
                    cells[here + inward],
                    column,
                ),
            )

    def listed(target, flags):
        count = jnp.int32(0)
        for index, flag in enumerate(flags):
            target[count] = index
            count = count + as_int(flag)
        last = target[jnp.maximum(count - 1, 0)]
        for k in range(3):
            target[count + k] = last
        return count

    brick_count = listed(brick_list, brick_live)
    slab_count = listed(slab_list, slab_live)

    zeros = jnp.zeros((8, 128), F32)
    for ref in (kappa, temperature, dual0, dual1, dual2):
        for t in range(8):
            ref[L_ZERO + t] = zeros

    for s in range(SLOTS):
        active = own[s] >= 0
        for to, chunk in ((8 * s, 3 * high[s]), (L_INNER + 8 * s, 1 + high[s])):
            at = pl.multiple_of(s * 32 + 8 * chunk, 8)
            for j in range(8):
                span = slice(128 * j, 128 * j + 128)
                fraction = mat[pl.ds(at, 8), span]
                kappa[to + j] = jnp.where(active, conductivity(fraction), 0.0)
                dual0[to + j] = prior[pl.ds(at, 8), span]
                temperature[to + j] = heat[pl.ds(at, 8), span]
                if to < L_INNER:
                    source[to + j] = load[pl.ds(at, 8), span]
                    factor[to + j] = factor_of(fraction)
                else:
                    dual1[to + j] = early1[32 * s + 8 * chunk + j]
                    dual2[to + j] = early2[32 * s + 8 * chunk + j]

    for k, message in enumerate((z_up, z_down)):
        for i in range(3):

            @pl.when(brick_live[4 + 3 * k + i])
            def _(k=k, i=i, message=message):
                for j in range(8):
                    t = 8 * i + j
                    to = L_UP + 24 * k + t
                    one, two, three = (message[t], message[24 + t], message[48 + t])
                    a, b, c = ((3, 4, 6) if k else (1, 3, 5))
                    kappa[to] = conductivity(one)
                    dual0[to] = jnp.where(row >= 2 if k else row < 6, two, 0.0)
                    source[to] = three
                    temperature[to] = jnp.where(
                        row == 3 if k else row == 0,
                        pltpu.roll(one, a, 0),
                        jnp.where(
                            row < 6 if k else row < 3,
                            pltpu.roll(two, b, 0),
                            pltpu.roll(three, c, 0),
                        ),
                    )
                    factor[to] = factor_of(one)

    def slab_tile(to, message, at, step):
        spread(to, message[at], message[at + step], kappa, temperature, source, dual0)

    for b, message in enumerate((near, far)):
        base = L_SLAB + 14 * b
        for s in range(SLOTS):
            top = as_int(slab_own[b][s] >= 24)
            slab_tile(base + s, message, 4 * s + 3 * top, 16)
            inner = 4 * s + 1 + top
            slab_tile(base + 4 + s, message, inner, 16)
            dual1[base + 4 + s] = early1[E_SLAB + 16 * b + inner]
            dual2[base + 4 + s] = early2[E_SLAB + 16 * b + inner]
        for i in range(3):
            slab_tile(base + 8 + i, z_up, Z_SLABS + 6 * b + i, 3)
            slab_tile(base + 11 + i, z_down, Z_SLABS + 6 * b + i, 3)

    stencil = Stencil(weights, L_TILES)

    def bricks(body):
        def two(step, carry):
            for k in range(2):
                unit = brick_list[2 * step + k]
                base, around = stencil.brick(brick_table, unit)
                for j in range(8):
                    body(base, around, j)
            return carry

        lax.fori_loop(0, (brick_count + 1) // 2, two, 0)

    def slabs(body):
        def four(step, carry):
            for k in range(4):
                body(*stencil.slab(slab_table, slab_list[4 * step + k]))
            return carry

        lax.fori_loop(0, (slab_count + 3) // 4, four, 0)

    def brick_first(base, around, j):
        own_kappa, beside_kappa = around(kappa, j)
        stencil.first(
            base + j, source, inverse, dual1, own_kappa, beside_kappa, around(dual0, j)[1]
        )

    def slab_first(t, around):
        own_kappa, beside_kappa = around(kappa)
        stencil.first(t, source, inverse, dual1, own_kappa, beside_kappa, around(dual0)[1])

    def brick_second(base, around, j):
        dual2[base + j] = stencil.later(base + j, source, inverse, around(dual1, j)[1])

    def slab_second(t, around):
        dual2[t] = stencil.later(t, source, inverse, around(dual1)[1])

    def brick_third(base, around, j):
        dual, duals = around(dual2, j)
        warm, warms = around(temperature, j)
        total = stencil.sensitivity(base + j, warm, warms, dual, duals)
        at = jnp.where(base < L_INNER, base, base - 32)
        sens[pl.ds(pl.multiple_of(at, 8), 8), 128 * j : 128 * j + 128] = factor[base + j] * total

    bricks(brick_first)
    slabs(slab_first)
    bricks(brick_second)
    slabs(slab_second)
    for s in range(SLOTS):
        for c in range(4):
            for j in range(8):
                dual_rows[32 * s + 8 * c : 32 * s + 8 * c + 8, 128 * j : 128 * j + 128] = early2[
                    32 * s + 8 * c + j
                ]

        @pl.when(brick_live[s])
        def _(s=s):
            at = pl.multiple_of(32 * s + 24 * high[s], 8)
            for j in range(8):
                dual_rows[pl.ds(at, 8), 128 * j : 128 * j + 128] = dual2[8 * s + j]

    writing = pltpu.make_async_copy(dual_rows, dual_out, dual_sem)
    writing.start()
    bricks(brick_third)

    restrict(sens, summed, edge, 5)
    for half in range(2):
        whole[...] = coarse[half]
        for s in range(SLOTS):

            @pl.when(brick_live[s])
            def _(s=s):
                whole[pl.ds(16 * s + 12 * high[s], 4), :] = edge[half, 4 * s : 4 * s + 4, :]

        for r in range(11):
            if r < 8:
                tile = whole[8 * r : 8 * r + 8, :]
            else:
                tile = edge[half, 8 * r - 48 : 8 * r - 40, :]
            for bit in (1, 2, 4):
                low_row = (row & bit) == 0
                low_lane = (lane & (16 * bit)) == 0
                swap_a = pltpu.roll(pltpu.roll(tile, 8 - bit, 0), 16 * bit, 1)
                swap_b = pltpu.roll(pltpu.roll(tile, bit, 0), 128 - 16 * bit, 1)
                tile = jnp.where(low_row == low_lane, tile, jnp.where(low_row, swap_a, swap_b))
            turned[2 * r + half] = tile

    y_block = lane // 32

    planes = 64 // parts
    level = [jnp.where(q >= 0, q // 8, 9) for q in own]

    def count(test):
        return functools.reduce(lambda a, b: a + b, [as_int(test(v)) for v in level])

    before = [count(lambda v, z=z: v < z) for z in range(5)]

    def nth(z, e):
        index = before[z] + e
        valid = index < before[z + 1]
        slot = jnp.minimum(index, SLOTS - 1)
        code = jnp.where(valid, place[slot] - 8 * z, -1)
        return slot, code

    for d in range(parts):
        z = d * planes // 16
        half = d * planes % 16 // 8
        codes = []
        for e in range(3):
            slot, code = nth(z, e)
            codes.append(code)
            for k in range(2):
                chunks[d * 8 + 2 * e + k] = turned[(slot * 2 + half) * 2 + k]
        start = d * planes % 8 == 0
        end = (d + 1) * planes % 8 == 0
        if planes >= 8:
            outside = -1 if half == 0 else 1
        else:
            outside = -1 if start else 1 if end else 0
        beyond = half + outside
        beside = [zeros, zeros]
        for e in range(3):
            if outside == 0:
                tile_at, lane_at, code = (0, 0, jnp.int32(-1))
            elif beyond in (0, 1):
                slot, code = nth(z, e)
                tile_at, lane_at = (slot * 2 + beyond, 96 if outside < 0 else 0)
            elif 0 <= z + outside <= 3:
                slot, code = nth(z + outside, e)
                tile_at, lane_at = (slot * 2 + (1 if outside < 0 else 0), 96 if outside < 0 else 0)
            elif outside < 0:
                q = downs[0][e]
                code = jnp.where(q >= 24, q - 24, -1)
                tile_at, lane_at = (8 + (3 + e) // 2, 64 * ((3 + e) % 2) + 32)
            else:
                q = ups[0][e]
                code = jnp.where((q >= 0) & (q < 8), q, -1)
                tile_at, lane_at = (8 + e // 2, 64 * (e % 2))
            codes.append(code)
            for k in range(2):
                tile = turned[tile_at * 2 + k]
                shift = (32 * e - lane_at) % 128
                if shift:
                    tile = pltpu.roll(tile, shift, 1)
                beside[k] = jnp.where(y_block == e, tile, beside[k])
        for e, code in enumerate(codes):
            beside[0] = jnp.where(lane == 96 + e, (code + 1).astype(F32), beside[0])
        for k in range(2):
            chunks[d * 8 + 6 + k] = beside[k]
    writing.wait()


def filter_kernel(parts, planes, across, spot, meta, received, swapped, out, grid, once):
    member = spot[0]
    depth = planes + 4
    wide = parts // across
    lane = lanes()
    row = rows()
    group_lane = lane // 16
    zeros = jnp.zeros((8, 128), F32)

    def clear(index, carry):
        grid[index] = zeros
        return carry

    lax.fori_loop(0, depth * 8 * wide, clear, 0, unroll=8)
    begin = member * planes
    half = begin % 16 // 8
    side = jnp.where(begin % 8 == 0, 0, planes + 2) if planes < 8 else half * (planes + 2)

    def place_plane(tile, lane_at, window, code, k, column, tile_x):
        at = (column * 2 + code % 2) % 8
        moved = pltpu.roll(tile, (at * 16 - lane_at + 256) % 128, 1)
        where_to = (window * 8 + code // 2 * 2 + k) * wide + tile_x
        grid[where_to] = jnp.where(group_lane == at, moved, grid[where_to])

    def from_device(column, carry):
        tile_x = column // across
        for e in range(3):
            code = meta[column, 0, 0, 96 + e].astype(I32) - 1

            @pl.when(code >= 0)
            def _(e=e, code=code):
                for k in range(2):
                    tile = received[column * 8 + 2 * e + k]
                    if planes == 8:
                        for p in range(8):
                            place_plane(tile, 16 * p, p + 2, code, k, column, tile_x)
                        other = swapped[column * 8 + 2 * e + k]
                        for p in range(2):
                            place_plane(
                                other,
                                jnp.where(half == 0, 16 * p, 96 + 16 * p),
                                jnp.where(half == 0, 10 + p, p),
                                code,
                                k,
                                column,
                                tile_x,
                            )
                    else:
                        for window in range(depth):
                            p = begin % 8 + window - 2

                            @pl.when((p >= 0) & (p < 8))
                            def _(tile=tile, p=p, window=window, k=k):
                                place_plane(tile, 16 * p, window, code, k, column, tile_x)

        for e in range(3):
            code = meta[column, 0, 0, 99 + e].astype(I32) - 1

            @pl.when(code >= 0)
            def _(e=e, code=code):
                for k in range(2):
                    tile = received[column * 8 + 6 + k]
                    for p in range(2):
                        place_plane(
                            tile, 32 * e + 16 * p, side + p, code, k, column, tile_x
                        )

        return carry

    lax.fori_loop(0, parts, from_device, 0)

    def relax(ref, window, y, x):
        here = (window * 8 + y) * wide + x
        tile = ref[here]
        north = ref[here + wide] if y < 7 else zeros
        south = ref[here - wide] if y > 0 else zeros
        east = ref[here + 1] if x < wide - 1 else zeros
        west = ref[here - 1] if x > 0 else zeros
        near = ref[here + 8 * wide] + ref[here - 8 * wide]
        near = near + pltpu.roll(jnp.where(row == 0, north, tile), 7, 0)
        near = near + pltpu.roll(jnp.where(row == 7, south, tile), 1, 0)
        near = near + pltpu.roll(jnp.where(lane == 0, east, tile), 127, 1)
        near = near + pltpu.roll(jnp.where(lane == 127, west, tile), 1, 1)
        return (grid[here] + 2.0 * near) * (1.0 / 13.0)

    first = spot[1] == 0
    last = spot[1] == spot[2] - 1

    def sweep_once(window, carry):
        gone = (first & (window < 2)) | (last & (window >= planes + 2))
        keep = jnp.where(gone, 0.0, 1.0).astype(F32)
        for y in range(8):
            for x in range(wide):
                once[(window * 8 + y) * wide + x] = relax(grid, window, y, x) * keep
        return carry

    lax.fori_loop(1, depth - 1, sweep_once, 0, unroll=2)

    def sweep_again(window, carry):
        for y in range(8):
            for x in range(wide):
                out[window - 2, 8 * y : 8 * y + 8, 128 * x : 128 * x + 128] = relax(
                    once, window, y, x
                )
        return carry

    lax.fori_loop(2, depth - 2, sweep_again, 0, unroll=2)


VMEM = pl.BlockSpec(memory_space=pltpu.VMEM)
SMEM = pl.BlockSpec(memory_space=pltpu.SMEM)
HBM = pl.BlockSpec(memory_space=pltpu.HBM)
BIG = 32 * 1024 * 1024
WHOLE = 60 * 1024 * 1024


def meta_of(index):
    return pl.BlockSpec((1, 8, 128), lambda i: (index, 0, 0), memory_space=pltpu.SMEM)


def params(limit=BIG):
    return pltpu.CompilerParams(vmem_limit_bytes=limit)


def tiles(count):
    return jax.ShapeDtypeStruct((count, 8, 128), F32)


def per_device(
    material_fraction, primal_heat_solution, dual_load, dual_prior_design, holder_cube_location
):
    parts = lax.axis_size("ba")
    groups = lax.axis_size("gz")
    member = lax.axis_index("ba")
    group = lax.axis_index("gz")
    planes = 64 // parts
    parity = (member % 2).reshape(1).astype(I32)
    place = holder_cube_location
    fields = [
        field.reshape(128, 1024)
        for field in (material_fraction, primal_heat_solution, dual_load, dual_prior_design)
    ]
    near, far = pl.pallas_call(
        pack_kernel,
        out_shape=(tiles(X_TILES), tiles(X_TILES)),
        in_specs=[SMEM, SMEM, HBM, HBM, HBM, HBM],
        out_specs=(VMEM, VMEM),
        scratch_shapes=[pltpu.VMEM((128, 1024), F32)] * 4
        + [pltpu.VMEM((384, 1024), jnp.bfloat16), pltpu.SemaphoreType.DMA((4, 4))],
        compiler_params=params(WHOLE),
        name="pack",
    )(place, parity, *fields)
    inner = [(i, i ^ 1) for i in range(parts)]
    outer = [(i, i + 1 if i % 2 else i - 1) for i in range(1, parts - 1)]
    near = lax.ppermute(near, "ba", inner)
    far = lax.ppermute(far, "ba", outer)
    up, down = pl.pallas_call(
        corner_kernel,
        out_shape=(tiles(Z_TILES), tiles(Z_TILES)),
        in_specs=[SMEM, meta_of(X_TILES - 1), meta_of(X_TILES - 1)] + [VMEM] * 6,
        out_specs=(VMEM, VMEM),
        grid=(1,),
        compiler_params=params(),
        name="corners",
    )(place, near, far, *fields, near, far)
    rising = [(i, i + 1) for i in range(groups - 1)]
    falling = [(i + 1, i) for i in range(groups - 1)]
    from_below = lax.ppermute(up, "gz", rising)
    from_above = lax.ppermute(down, "gz", falling)
    meta_z = meta_of(Z_TILES - 1)
    meta_x = meta_of(X_TILES - 1)
    early = pltpu.VMEM((E_TILES, 8, 128), F32)
    dual1, dual2, coarse = pl.pallas_call(
        early_kernel,
        out_shape=(tiles(E_TILES), tiles(E_TILES), jax.ShapeDtypeStruct((2, 64, 128), F32)),
        in_specs=[SMEM, SMEM, meta_x, meta_x] + [VMEM] * 6,
        out_specs=(VMEM, VMEM, VMEM),
        scratch_shapes=[
            pltpu.SMEM((145,), I32),
            pltpu.SMEM((16 * 8,), I32),
            pltpu.SMEM((32 * 8,), I32),
            early,
            early,
            early,
            early,
            pltpu.VMEM((6 * E_TILES, 8, 128), F32),
            early,
            pltpu.VMEM((128, 1024), F32),
            pltpu.VMEM((128, 128), F32),
        ],
        grid=(1,),
        cost_estimate=pl.CostEstimate(flops=10**9, bytes_accessed=3 * 10**7, transcendentals=0),
        compiler_params=params(),
        name="early",
    )(place, parity, near, far, *fields, near, far)
    late = pltpu.VMEM((L_TILES, 8, 128), F32)
    dual, chunks = pl.pallas_call(
        functools.partial(late_kernel, parts),
        out_shape=(jax.ShapeDtypeStruct((128, 1024), F32), tiles(8 * parts)),
        in_specs=[SMEM, SMEM, meta_x, meta_x, meta_z, meta_z] + [VMEM] * 11,
        out_specs=(HBM, VMEM),
        scratch_shapes=[
            pltpu.VMEM((128, 1024), F32),
            pltpu.SemaphoreType.DMA,
            pltpu.SMEM((145,), I32),
            pltpu.SMEM((10 * 8,), I32),
            pltpu.SMEM((20 * 8,), I32),
            pltpu.SMEM((16,), I32),
            pltpu.SMEM((24,), I32),
            late,
            late,
            late,
            late,
            late,
            late,
            pltpu.VMEM((6 * L_TILES, 8, 128), F32),
            late,
            pltpu.VMEM((L_SLAB, 8, 128), F32),
            pltpu.VMEM((80, 1024), F32),
            pltpu.VMEM((80, 128), F32),
            pltpu.VMEM((2, 40, 128), F32),
            pltpu.VMEM((64, 128), F32),
            pltpu.VMEM((22, 8, 128), F32),
        ],
        grid=(1,),
        compiler_params=params(),
        name="late",
    )(
        place,
        parity,
        near,
        far,
        from_above,
        from_below,
        *fields,
        near,
        far,
        from_above,
        from_below,
        dual1,
        dual2,
        coarse,
    )
    received = lax.all_to_all(chunks, "ba", split_axis=0, concat_axis=0, tiled=True)
    swapped = lax.ppermute(received, "ba", inner) if planes == 8 else received
    spot = jnp.stack([member, group * parts + member, jnp.int32(groups * parts)]).astype(I32)
    wide = 32 * parts // 128
    filtered = pl.pallas_call(
        functools.partial(filter_kernel, parts, planes, 4),
        out_shape=jax.ShapeDtypeStruct((planes, 64, 32 * parts), F32),
        in_specs=[
            SMEM,
            pl.BlockSpec(
                (parts, 1, 8, 128), lambda i: (0, 6, 0, 0), memory_space=pltpu.SMEM
            ),
            VMEM,
            VMEM,
        ],
        out_specs=VMEM,
        scratch_shapes=[
            pltpu.VMEM(((planes + 4) * 8 * wide, 8, 128), F32),
            pltpu.VMEM(((planes + 4) * 8 * wide, 8, 128), F32),
        ],
        grid=(1,),
        compiler_params=params(),
        name="smooth",
    )(spot, received.reshape(parts, 8, 8, 128), received, swapped)
    return (dual.reshape(material_fraction.shape), filtered)


def solution(mesh):
    spec = P(("gz", "ba"), None, None)
    return jax.shard_map(
        per_device,
        mesh=mesh,
        in_specs=(spec, spec, spec, spec, P(("gz", "ba"))),
        out_specs=(spec, spec),
        check_vma=False,
    )
```

```python
import functools

import jax
import jax.numpy as jnp
from jax import lax
from jax.experimental import pallas as pl
from jax.experimental.pallas import tpu as pltpu
from jax.sharding import PartitionSpec as P

SLOTS = 4
KMIN = 0.01
HEAT = 0.05
F32 = jnp.float32
I32 = jnp.int32

E_SLAB = 128
E_ZERO = 160
E_TILES = 192
L_INNER = 32
L_UP = 64
L_DOWN = 88
L_SLAB = 112
L_ZERO = 140
L_TILES = 148
X_TILES = 33
Z_SLABS = 72
Z_TILES = 85
DUMMY = 29
GROUP = 4


def lanes():
    return lax.broadcasted_iota(I32, (8, 128), 1)


def rows():
    return lax.broadcasted_iota(I32, (8, 128), 0)


def take(tile, index):
    return jnp.take_along_axis(tile, index, axis=1)


def row_of(values):
    lane = lanes()
    result = jnp.zeros((8, 128), F32)
    for index, value in enumerate(values):
        result = jnp.where(lane == index, (value + 1).astype(F32), result)
    return result


def position_at(meta, index):
    return meta[0, 0, index].astype(I32) - 1


def as_int(flag):
    return jnp.where(flag, 1, 0).astype(I32)


def pack_kernel(
    place,
    parity_ref,
    mat_in,
    heat_in,
    load_in,
    prior_in,
    near,
    far,
    mat,
    heat,
    load,
    prior,
    parts,
    sems,
):
    pairs = ((mat_in, mat), (heat_in, heat), (prior_in, prior), (load_in, load))
    fetches = [
        [
            pltpu.make_async_copy(
                source.at[pl.ds(32 * s, 32)], target.at[pl.ds(32 * s, 32)], sems.at[k, s]
            )
            for k, (source, target) in enumerate(pairs)
        ]
        for s in range(SLOTS)
    ]
    for slot_fetches in fetches:
        for fetch in slot_fetches:
            fetch.start()
    cell = lax.broadcasted_iota(I32, (1024, 256), 0)
    column = lax.broadcasted_iota(I32, (1024, 256), 1)
    deep = column % 128 // 32
    flipped = (column // 128) != parity_ref[0]
    wanted = 32 * (column % 32) + jnp.where(flipped, deep, 31 - deep)
    pick = jnp.where(cell == wanted, 1.0, 0.0).astype(jnp.bfloat16)
    depth = lanes() // 32
    def field(moved, k, lead, c, side):
        high, mid, low = (
            moved[
                384 * lead + (3 * k + third) * 32 + 8 * c : 384 * lead + (3 * k + third) * 32 + 8 * c + 8,
                128 * side : 128 * side + 128,
            ]
            for third in range(3)
        )
        return (high + mid) + low

    for s in range(SLOTS):
        for fetch in fetches[s]:
            fetch.wait()
        lead = s % GROUP
        for k, ref in enumerate((mat, heat, prior, load)):
            rest = ref[32 * s : 32 * s + 32, :]
            for third in range(3):
                part = rest.astype(jnp.bfloat16)
                at = 384 * lead + (3 * k + third) * 32
                parts[at : at + 32, :] = part
                rest = rest - part.astype(F32)
        if lead < GROUP - 1:
            continue
        moved = jnp.dot(parts[...], pick, preferred_element_type=F32)
        for lead in range(GROUP):
            slot = s - GROUP + 1 + lead
            for side, out in enumerate((near, far)):
                for c in range(4):
                    fraction, warm, dual, given = (
                        field(moved, k, lead, c, side) for k in range(4)
                    )
                    own = conductivity(fraction)
                    beyond = conduct(own, pltpu.roll(own, 96, 1)) * pltpu.roll(dual, 96, 1)
                    given = pltpu.roll(given + jnp.where(depth == 1, beyond, 0.0), 64, 1)
                    unit = 4 * slot + c
                    out[unit] = jnp.where(depth == 3, pltpu.roll(warm, 96, 1), fraction)
                    out[16 + unit] = jnp.where(depth < 2, dual, given)
    meta = row_of([place[s] for s in range(SLOTS)])
    near[X_TILES - 1] = meta
    far[X_TILES - 1] = meta


def corner_kernel(
    place, near_meta, far_meta, mat, heat, load, prior, near, far, up, down
):
    values = [place[s] for s in range(SLOTS)]
    start = as_int(values[SLOTS - 1] >= 0)
    row = rows()

    def layer(out, to, at, j, rising):
        fraction, warm, given, dual = (
            ref[pl.ds(at, 8), 128 * j : 128 * j + 128] for ref in (mat, heat, load, prior)
        )
        step = 1 if rising else 7
        own = conductivity(fraction)
        beyond = conduct(own, pltpu.roll(own, step, 0)) * pltpu.roll(dual, step, 0)
        given = given + jnp.where(row == (2 if rising else 5), beyond, 0.0)
        spare, two = ((row == 0, row < 2) if rising else (row == 7, row > 5))
        a, b, c = ((5, 4, 2) if rising else (7, 5, 3))
        out[to] = jnp.where(spare, pltpu.roll(warm, a, 0), fraction)
        out[to + 24] = jnp.where(two, pltpu.roll(warm, b, 0), dual)
        out[to + 48] = jnp.where(two, pltpu.roll(warm, c, 0), given)

    for i in range(3):
        top = pl.multiple_of((start + i) * 32 + 24, 8)
        for j in range(8):
            layer(up, 8 * i + j, top, j, True)
            layer(down, 8 * i + j, 32 * i, j, False)
    for b, (meta, source) in enumerate(((near_meta, near), (far_meta, far))):
        listed = [position_at(meta, s) for s in range(SLOTS)]
        values = values + listed
        start = as_int(listed[SLOTS - 1] >= 0)
        for field in range(2):
            for i in range(3):
                to = Z_SLABS + b * 6 + field * 3 + i
                up[to] = source[field * 16 + (start + i) * 4 + 3]
                down[to] = source[field * 16 + i * 4]
    meta_tile = row_of(values)
    up[Z_TILES - 1] = meta_tile
    down[Z_TILES - 1] = meta_tile


def conduct(own, beside):
    return (2.0 * own) * beside / jnp.maximum(own + beside, KMIN)


def conductivity(fraction):
    return KMIN + (1.0 - KMIN) * fraction * fraction * fraction


def cell_of(x, y, z):
    return ((z + 1) * 6 + y + 1) * 4 + x + 1


def clear_cells(cells, zero):
    def clear(index, carry):
        cells[index] = zero
        return carry

    lax.fori_loop(0, 144, clear, 0, unroll=16)


def enter(cells, position, wanted, x, z, tile):
    here = jnp.where(wanted, cell_of(x, position // 2 % 4, z), 144)
    cells[here] = tile
    return jnp.where(wanted, here, DUMMY)


def fill(table, unit, values):
    for k, value in enumerate(values):
        table[unit * 8 + k] = value


class Stencil:
    def __init__(self, weights, stride):
        self.lane = lanes()
        row = rows()
        self.top_row = row == 0
        self.last_row = row == 7
        self.x_cell = self.lane % 32
        self.y_block = self.lane // 32
        self.face_block = self.lane // 4
        self.face_lane = 32 * (self.lane % 4)
        self.weights = weights
        self.stride = stride

    def above(self, tile, other):
        return pltpu.roll(jnp.where(self.top_row, other, tile), 7, 0)

    def below(self, tile, other):
        return pltpu.roll(jnp.where(self.last_row, other, tile), 1, 0)

    def brick(self, table, unit):
        base, up, down, north, south, east, west, px = (table[unit * 8 + k] for k in range(8))
        lane, x_cell = (self.lane, self.x_cell)
        own_lane = 31 * px
        brick_at = jnp.where(px == 1, west, east)
        slab_at = jnp.where(px == 1, east, west)
        from_brick = x_cell == own_lane
        to_brick = x_cell == 31 - own_lane
        index = jnp.where(to_brick, 32 * self.y_block + own_lane, self.y_block)
        step = jnp.where(to_brick, 0, 4)

        def around(ref, j):
            tile = ref[base + j]
            after = ref[base + j + 1] if j < 7 else ref[north]
            before = ref[base + j - 1] if j > 0 else ref[south + 7]
            beside = ref[slab_at]
            moved = 0
            if j == 0:
                beside, moved = (pltpu.roll(beside, 4, 1), 1)
            elif j == 7:
                beside, moved = (jnp.where(px == 1, pltpu.roll(beside, 4, 1), beside), px)
            both = jnp.where(from_brick, ref[brick_at + j], beside)
            edge = take(both, index + step * (j + moved))
            return tile, (
                jnp.where(x_cell == 31, edge, pltpu.roll(tile, 127, 1)),
                jnp.where(x_cell == 0, edge, pltpu.roll(tile, 1, 1)),
                pltpu.roll(jnp.where(lane < 32, after, tile), 96, 1),
                pltpu.roll(jnp.where(lane >= 96, before, tile), 32, 1),
                self.above(tile, ref[up + j]),
                self.below(tile, ref[down + j]),
            )

        return base, around

    def slab(self, table, unit):
        at, up, down, north, south, face, column = (table[unit * 8 + k] for k in range(7))
        lane, x_cell = (self.lane, self.x_cell)
        index = self.face_lane + column

        def around(ref):
            tile = ref[at]
            edge = take(ref[face], index)
            for j in range(1, 8):
                edge = jnp.where(self.face_block == j, take(ref[face + j], index), edge)
            return tile, (
                pltpu.roll(tile, 96, 1),
                jnp.where(lane < 32, edge, pltpu.roll(tile, 32, 1)),
                jnp.where(x_cell == 31, pltpu.roll(ref[north], 31, 1), pltpu.roll(tile, 127, 1)),
                jnp.where(x_cell == 0, pltpu.roll(ref[south], 97, 1), pltpu.roll(tile, 1, 1)),
                self.above(tile, ref[up]),
                self.below(tile, ref[down]),
            )

        return at, around

    def first(self, t, source, inverse, dual1, own_kappa, beside_kappa, beside):
        total = jnp.full((8, 128), HEAT, F32)
        flux = source[t]
        for k in range(6):
            weight = conduct(own_kappa, beside_kappa[k])
            self.weights[k * self.stride + t] = weight
            total = total + weight
            flux = flux + weight * beside[k]
        scale = 1.0 / total
        inverse[t] = scale
        dual1[t] = flux * scale

    def later(self, t, source, inverse, beside):
        flux = source[t]
        for k in range(6):
            flux = flux + self.weights[k * self.stride + t] * beside[k]
        return flux * inverse[t]

    def sensitivity(self, t, warm, warms, dual, duals):
        total = jnp.zeros((8, 128), F32)
        for k in range(6):
            total = total + jnp.where(
                self.weights[k * self.stride + t] > 0,
                (warms[k] - warm) * (duals[k] - dual),
                0.0,
            )
        return total


def factor_of(fraction):
    return (-1.5 * (1.0 - KMIN)) * fraction * fraction


def spread(to, first, second, kappa, temperature, source, dual0):
    kappa[to] = conductivity(first)
    dual0[to] = jnp.where(lanes() < 64, second, 0.0)
    source[to] = pltpu.roll(second, 64, 1)
    temperature[to] = pltpu.roll(first, 32, 1)


def shrink_table():
    cell = lax.broadcasted_iota(I32, (512, 128), 0)
    coarse = lax.broadcasted_iota(I32, (512, 128), 1)
    matches = (cell // 64 == coarse // 16) & (cell % 32 // 2 == coarse % 16)
    return jnp.where(matches, 0.125, 0.0).astype(F32)


def restrict(sens, summed, out, count):
    shrink = shrink_table()
    for half in range(2):
        summed[...] = jnp.dot(
            sens[:, 512 * half : 512 * half + 512],
            shrink,
            precision=lax.Precision.HIGHEST,
            preferred_element_type=F32,
        )
        for r in range(count):
            out[half, 8 * r : 8 * r + 8, :] = (
                summed[pl.ds(16 * r, 8, stride=2), :] + summed[pl.ds(16 * r + 1, 8, stride=2), :]
            )


def early_kernel(
    place,
    parity_ref,
    near_meta,
    far_meta,
    mat,
    heat,
    load,
    prior,
    near,
    far,
    dual1,
    dual2,
    coarse,
    cells,
    brick_table,
    slab_table,
    kappa,
    temperature,
    source,
    dual0,
    weights,
    inverse,
    sens,
    summed,
):
    parity = parity_ref[0]
    clear_cells(cells, E_ZERO)
    own = [place[s] for s in range(SLOTS)]
    own_cell = [enter(cells, q, q >= 0, q % 2, q // 8, 32 * s) for s, q in enumerate(own)]
    slab_cell = []
    slab_live = []
    for b, meta in enumerate((near_meta, far_meta)):
        east = parity == b
        column = jnp.where(east, 0, 1)
        x = jnp.where(east, 2, -1)
        for s in range(SLOTS):
            q = position_at(meta, s)
            wanted = (q >= 0) & (q % 2 == column)
            slab_live.append((wanted, q))
            slab_cell.append(
                enter(cells, q, wanted, x, q // 8, E_SLAB + 16 * b + 4 * s)
            )
    for s in range(SLOTS):
        here = own_cell[s]
        px = jnp.where(own[s] >= 0, own[s] % 2, 0)
        lift = jnp.where(own[s] >= 8, 24, 0)
        north, south = (cells[here + 4], cells[here - 4])
        east, west = (cells[here + 1], cells[here - 1])
        above, below = (cells[here + 24], cells[here - 24] + lift)
        for c in range(4):
            base = s * 32 + c * 8
            fill(
                brick_table,
                s * 4 + c,
                (
                    base,
                    base + 8 if c < 3 else above,
                    base - 8 if c > 0 else below,
                    north + 8 * c,
                    south + 8 * c,
                    east + jnp.where(px == 1, c, 8 * c),
                    west + jnp.where(px == 0, c, 8 * c),
                    px,
                ),
            )
    for b in range(2):
        inward = jnp.where(parity == b, -1, 1)
        column = jnp.where(parity == b, 31, 0)
        for s in range(SLOTS):
            here = slab_cell[4 * b + s]
            wanted, q = slab_live[4 * b + s]
            lift = jnp.where(q >= 8, 3, 0)
            north, south = (cells[here + 4], cells[here - 4])
            above, below = (cells[here + 24], cells[here - 24] + lift)
            face = cells[here + inward]
            live = as_int(wanted)
            for c in range(4):
                unit = 16 * b + 4 * s + c
                fill(
                    slab_table,
                    unit,
                    (
                        E_SLAB + unit,
                        E_SLAB + unit + 1 if c < 3 else above,
                        E_SLAB + unit - 1 if c > 0 else below,
                        north + c,
                        south + c,
                        face + 8 * c,
                        column,
                        live,
                    ),
                )

    zeros = jnp.zeros((8, 128), F32)
    for ref in (kappa, temperature, dual0, dual1, dual2):
        for t in range(32):
            ref[E_ZERO + t] = zeros

    def own_unit(unit, carry):
        at = pl.multiple_of(unit * 8, 8)
        active = place[unit // 4] >= 0
        for j in range(8):
            span = slice(128 * j, 128 * j + 128)
            t = unit * 8 + j
            kappa[t] = jnp.where(active, conductivity(mat[pl.ds(at, 8), span]), 0.0)
            source[t] = jnp.where(active, load[pl.ds(at, 8), span], 0.0)
            dual0[t] = prior[pl.ds(at, 8), span]
            temperature[t] = heat[pl.ds(at, 8), span]
        return carry

    lax.fori_loop(0, 16, own_unit, 0)
    for b, message in enumerate((near, far)):
        for t in range(16):
            to = E_SLAB + 16 * b + t
            spread(to, message[t], message[t + 16], kappa, temperature, source, dual0)

    stencil = Stencil(weights, E_TILES)

    def slabs(body):
        def slot(index, carry):
            @pl.when(slab_table[index * 32 + 7] > 0)
            def _():
                for c in range(4):
                    body(*stencil.slab(slab_table, index * 4 + c))

            return carry

        lax.fori_loop(0, 8, slot, 0)

    def bricks(body):
        def four(step, carry):
            for k in range(4):
                unit = 4 * step + k
                base, around = stencil.brick(brick_table, unit)
                for j in range(8):
                    body(unit, base, around, j)
            return carry

        lax.fori_loop(0, 4, four, 0)

    def brick_first(unit, base, around, j):
        own_kappa, beside_kappa = around(kappa, j)
        stencil.first(
            base + j, source, inverse, dual1, own_kappa, beside_kappa, around(dual0, j)[1]
        )

    def slab_first(t, around):
        own_kappa, beside_kappa = around(kappa)
        stencil.first(t, source, inverse, dual1, own_kappa, beside_kappa, around(dual0)[1])

    def brick_second(unit, base, around, j):
        dual2[base + j] = stencil.later(base + j, source, inverse, around(dual1, j)[1])

    def slab_second(t, around):
        dual2[t] = stencil.later(t, source, inverse, around(dual1)[1])

    def brick_third(unit, base, around, j):
        at = pl.multiple_of(unit * 8, 8)
        dual, duals = around(dual2, j)
        warm, warms = around(temperature, j)
        total = stencil.sensitivity(base + j, warm, warms, dual, duals)
        span = slice(128 * j, 128 * j + 128)
        sens[pl.ds(at, 8), span] = factor_of(mat[pl.ds(at, 8), span]) * total

    bricks(brick_first)
    slabs(slab_first)
    bricks(brick_second)
    slabs(slab_second)
    bricks(brick_third)
    restrict(sens, summed, coarse, 8)


def late_kernel(
    parts,
    place,
    parity_ref,
    near_meta,
    far_meta,
    up_meta,
    down_meta,
    mat,
    heat,
    load,
    prior,
    near,
    far,
    z_up,
    z_down,
    early1,
    early2,
    coarse,
    dual_out,
    chunks,
    dual_rows,
    dual_sem,
    cells,
    brick_table,
    slab_table,
    brick_list,
    slab_list,
    kappa,
    temperature,
    source,
    dual0,
    dual1,
    dual2,
    weights,
    inverse,
    factor,
    sens,
    summed,
    edge,
    whole,
    turned,
):
    parity = parity_ref[0]
    lane = lanes()
    row = rows()
    clear_cells(cells, L_ZERO)
    own = [place[s] for s in range(SLOTS)]

    def at_edge(q):
        return ((q >= 0) & (q < 8)) | (q >= 24)

    own_cell = [
        enter(cells, q, at_edge(q), q % 2, q // 8, 8 * s) for s, q in enumerate(own)
    ]
    lists_up = [[position_at(up_meta, 4 * k + s) for s in range(SLOTS)] for k in range(3)]
    lists_down = [[position_at(down_meta, 4 * k + s) for s in range(SLOTS)] for k in range(3)]

    def shifted(listed):
        full = listed[SLOTS - 1] >= 0
        return [jnp.where(full, listed[i + 1], listed[i]) for i in range(3)]

    ups = [listed[:3] for listed in lists_up]
    downs = [shifted(listed) for listed in lists_down]
    brick_live = [at_edge(q) for q in own]
    brick_live += [(q >= 0) & (q < 8) for q in ups[0]]
    brick_live += [q >= 24 for q in downs[0]]
    halo_cell = [
        enter(cells, q, brick_live[4 + i], q % 2, 4, L_UP + 8 * i) for i, q in enumerate(ups[0])
    ]
    halo_cell += [
        enter(cells, q, brick_live[7 + i], q % 2, -1, L_DOWN + 8 * i)
        for i, q in enumerate(downs[0])
    ]
    slab_cell = []
    slab_live = []
    slab_own = []
    for b, meta in enumerate((near_meta, far_meta)):
        east = parity == b
        column = jnp.where(east, 0, 1)
        x = jnp.where(east, 2, -1)
        base = L_SLAB + 14 * b
        mine = [position_at(meta, s) for s in range(SLOTS)]
        slab_own.append(mine)
        tests = [at_edge(q) & (q % 2 == column) for q in mine]
        tests += [(q >= 0) & (q < 8) & (q % 2 == column) for q in ups[1 + b]]
        tests += [(q >= 24) & (q % 2 == column) for q in downs[1 + b]]
        slab_live += tests
        for k, q in enumerate(mine + ups[1 + b] + downs[1 + b]):
            z = q // 8 if k < 4 else 4 if k < 7 else -1
            slab_cell.append(enter(cells, q, tests[k], x, z, base + (k if k < 4 else 4 + k)))

    high = [as_int(q >= 24) for q in own]
    for s in range(SLOTS):
        here = own_cell[s]
        px = jnp.where(own[s] >= 0, own[s] % 2, 0)
        inner = L_INNER + 8 * s
        fill(
            brick_table,
            s,
            (
                jnp.int32(8 * s),
                jnp.where(high[s] == 1, cells[here + 24], inner),
                jnp.where(high[s] == 1, inner, cells[here - 24]),
                cells[here + 4],
                cells[here - 4],
                cells[here + 1],
                cells[here - 1],
                px,
            ),
        )
    for i in range(6):
        here = halo_cell[i]
        q = (ups[0] + downs[0])[i]
        px = jnp.where(q >= 0, q % 2, 0)
        fill(
            brick_table,
            4 + i,
            (
                jnp.int32(L_UP + 8 * i),
                jnp.int32(L_ZERO) if i < 3 else cells[here + 24],
                cells[here - 24] if i < 3 else jnp.int32(L_ZERO),
                cells[here + 4],
                cells[here - 4],
                cells[here + 1],
                cells[here - 1],
                px,
            ),
        )
    for b in range(2):
        inward = jnp.where(parity == b, -1, 1)
        column = jnp.where(parity == b, 31, 0)
        base = L_SLAB + 14 * b
        for k in range(10):
            here = slab_cell[10 * b + k]
            above, below = (cells[here + 24], cells[here - 24])
            if k < 4:
                top = slab_own[b][k] >= 24
                inner = base + 4 + k
                above, below = (jnp.where(top, above, inner), jnp.where(top, inner, below))
            elif k < 7:
                above = jnp.int32(L_ZERO)
            else:
                below = jnp.int32(L_ZERO)
            fill(
                slab_table,
                10 * b + k,
                (
                    jnp.int32(base + (k if k < 4 else 4 + k)),
                    above,
                    below,
                    cells[here + 4],
                    cells[here - 4],
                    cells[here + inward],
                    column,
                ),
            )

    def listed(target, flags):
        count = jnp.int32(0)
        for index, flag in enumerate(flags):
            target[count] = index
            count = count + as_int(flag)
        last = target[jnp.maximum(count - 1, 0)]
        for k in range(3):
            target[count + k] = last
        return count

    brick_count = listed(brick_list, brick_live)
    slab_count = listed(slab_list, slab_live)

    zeros = jnp.zeros((8, 128), F32)
    for ref in (kappa, temperature, dual0, dual1, dual2):
        for t in range(8):
            ref[L_ZERO + t] = zeros

    for s in range(SLOTS):
        active = own[s] >= 0
        for to, chunk in ((8 * s, 3 * high[s]), (L_INNER + 8 * s, 1 + high[s])):
            at = pl.multiple_of(s * 32 + 8 * chunk, 8)
            for j in range(8):
                span = slice(128 * j, 128 * j + 128)
                fraction = mat[pl.ds(at, 8), span]
                kappa[to + j] = jnp.where(active, conductivity(fraction), 0.0)
                dual0[to + j] = prior[pl.ds(at, 8), span]
                temperature[to + j] = heat[pl.ds(at, 8), span]
                if to < L_INNER:
                    source[to + j] = load[pl.ds(at, 8), span]
                    factor[to + j] = factor_of(fraction)
                else:
                    dual1[to + j] = early1[32 * s + 8 * chunk + j]
                    dual2[to + j] = early2[32 * s + 8 * chunk + j]

    for k, message in enumerate((z_up, z_down)):
        for i in range(3):

            @pl.when(brick_live[4 + 3 * k + i])
            def _(k=k, i=i, message=message):
                for j in range(8):
                    t = 8 * i + j
                    to = L_UP + 24 * k + t
                    one, two, three = (message[t], message[24 + t], message[48 + t])
                    a, b, c = ((3, 4, 6) if k else (1, 3, 5))
                    kappa[to] = conductivity(one)
                    dual0[to] = jnp.where(row >= 2 if k else row < 6, two, 0.0)
                    source[to] = three
                    temperature[to] = jnp.where(
                        row == 3 if k else row == 0,
                        pltpu.roll(one, a, 0),
                        jnp.where(
                            row < 6 if k else row < 3,
                            pltpu.roll(two, b, 0),
                            pltpu.roll(three, c, 0),
                        ),
                    )
                    factor[to] = factor_of(one)

    def slab_tile(to, message, at, step):
        spread(to, message[at], message[at + step], kappa, temperature, source, dual0)

    for b, message in enumerate((near, far)):
        base = L_SLAB + 14 * b
        for s in range(SLOTS):
            top = as_int(slab_own[b][s] >= 24)
            slab_tile(base + s, message, 4 * s + 3 * top, 16)
            inner = 4 * s + 1 + top
            slab_tile(base + 4 + s, message, inner, 16)
            dual1[base + 4 + s] = early1[E_SLAB + 16 * b + inner]
            dual2[base + 4 + s] = early2[E_SLAB + 16 * b + inner]
        for i in range(3):
            slab_tile(base + 8 + i, z_up, Z_SLABS + 6 * b + i, 3)
            slab_tile(base + 11 + i, z_down, Z_SLABS + 6 * b + i, 3)

    stencil = Stencil(weights, L_TILES)

    def bricks(body):
        def two(step, carry):
            for k in range(2):
                unit = brick_list[2 * step + k]
                base, around = stencil.brick(brick_table, unit)
                for j in range(8):
                    body(base, around, j)
            return carry

        lax.fori_loop(0, (brick_count + 1) // 2, two, 0)

    def slabs(body):
        def four(step, carry):
            for k in range(4):
                body(*stencil.slab(slab_table, slab_list[4 * step + k]))
            return carry

        lax.fori_loop(0, (slab_count + 3) // 4, four, 0)

    def brick_first(base, around, j):
        own_kappa, beside_kappa = around(kappa, j)
        stencil.first(
            base + j, source, inverse, dual1, own_kappa, beside_kappa, around(dual0, j)[1]
        )

    def slab_first(t, around):
        own_kappa, beside_kappa = around(kappa)
        stencil.first(t, source, inverse, dual1, own_kappa, beside_kappa, around(dual0)[1])

    def brick_second(base, around, j):
        dual2[base + j] = stencil.later(base + j, source, inverse, around(dual1, j)[1])

    def slab_second(t, around):
        dual2[t] = stencil.later(t, source, inverse, around(dual1)[1])

    def brick_third(base, around, j):
        dual, duals = around(dual2, j)
        warm, warms = around(temperature, j)
        total = stencil.sensitivity(base + j, warm, warms, dual, duals)
        at = jnp.where(base < L_INNER, base, base - 32)
        sens[pl.ds(pl.multiple_of(at, 8), 8), 128 * j : 128 * j + 128] = factor[base + j] * total

    bricks(brick_first)
    slabs(slab_first)
    bricks(brick_second)
    slabs(slab_second)
    for s in range(SLOTS):
        for c in range(4):
            for j in range(8):
                dual_rows[32 * s + 8 * c : 32 * s + 8 * c + 8, 128 * j : 128 * j + 128] = early2[
                    32 * s + 8 * c + j
                ]

        @pl.when(brick_live[s])
        def _(s=s):
            at = pl.multiple_of(32 * s + 24 * high[s], 8)
            for j in range(8):
                dual_rows[pl.ds(at, 8), 128 * j : 128 * j + 128] = dual2[8 * s + j]

    writing = pltpu.make_async_copy(dual_rows, dual_out, dual_sem)
    writing.start()
    bricks(brick_third)

    restrict(sens, summed, edge, 5)
    for half in range(2):
        whole[...] = coarse[half]
        for s in range(SLOTS):

            @pl.when(brick_live[s])
            def _(s=s):
                whole[pl.ds(16 * s + 12 * high[s], 4), :] = edge[half, 4 * s : 4 * s + 4, :]

        for r in range(11):
            if r < 8:
                tile = whole[8 * r : 8 * r + 8, :]
            else:
                tile = edge[half, 8 * r - 48 : 8 * r - 40, :]
            for bit in (1, 2, 4):
                low_row = (row & bit) == 0
                low_lane = (lane & (16 * bit)) == 0
                swap_a = pltpu.roll(pltpu.roll(tile, 8 - bit, 0), 16 * bit, 1)
                swap_b = pltpu.roll(pltpu.roll(tile, bit, 0), 128 - 16 * bit, 1)
                tile = jnp.where(low_row == low_lane, tile, jnp.where(low_row, swap_a, swap_b))
            turned[2 * r + half] = tile

    y_block = lane // 32

    planes = 64 // parts
    level = [jnp.where(q >= 0, q // 8, 9) for q in own]

    def count(test):
        return functools.reduce(lambda a, b: a + b, [as_int(test(v)) for v in level])

    before = [count(lambda v, z=z: v < z) for z in range(5)]

    def nth(z, e):
        index = before[z] + e
        valid = index < before[z + 1]
        slot = jnp.minimum(index, SLOTS - 1)
        code = jnp.where(valid, place[slot] - 8 * z, -1)
        return slot, code

    for d in range(parts):
        z = d * planes // 16
        half = d * planes % 16 // 8
        codes = []
        for e in range(3):
            slot, code = nth(z, e)
            codes.append(code)
            for k in range(2):
                chunks[d * 8 + 2 * e + k] = turned[(slot * 2 + half) * 2 + k]
        start = d * planes % 8 == 0
        end = (d + 1) * planes % 8 == 0
        if planes >= 8:
            outside = -1 if half == 0 else 1
        else:
            outside = -1 if start else 1 if end else 0
        beyond = half + outside
        beside = [zeros, zeros]
        for e in range(3):
            if outside == 0:
                tile_at, lane_at, code = (0, 0, jnp.int32(-1))
            elif beyond in (0, 1):
                slot, code = nth(z, e)
                tile_at, lane_at = (slot * 2 + beyond, 96 if outside < 0 else 0)
            elif 0 <= z + outside <= 3:
                slot, code = nth(z + outside, e)
                tile_at, lane_at = (slot * 2 + (1 if outside < 0 else 0), 96 if outside < 0 else 0)
            elif outside < 0:
                q = downs[0][e]
                code = jnp.where(q >= 24, q - 24, -1)
                tile_at, lane_at = (8 + (3 + e) // 2, 64 * ((3 + e) % 2) + 32)
            else:
                q = ups[0][e]
                code = jnp.where((q >= 0) & (q < 8), q, -1)
                tile_at, lane_at = (8 + e // 2, 64 * (e % 2))
            codes.append(code)
            for k in range(2):
                tile = turned[tile_at * 2 + k]
                shift = (32 * e - lane_at) % 128
                if shift:
                    tile = pltpu.roll(tile, shift, 1)
                beside[k] = jnp.where(y_block == e, tile, beside[k])
        for e, code in enumerate(codes):
            beside[0] = jnp.where(lane == 96 + e, (code + 1).astype(F32), beside[0])
        for k in range(2):
            chunks[d * 8 + 6 + k] = beside[k]
    writing.wait()


class Placer:
    def __init__(self, grid, size, wide, across, code, column):
        self.grid = grid
        self.stride = 8 * wide
        self.wide = wide
        self.to = jnp.where(code >= 0, 0, size) + lax.div(column, across)
        code = jnp.maximum(code, 0)
        self.to = self.to + (code >> 1) * (2 * wide)
        self.at = (column * 2 + (code & 1)) & 7
        self.here = lanes() // 16 == self.at

    def planes(self, tile, k, windows, first, moved=0):
        found = []
        for p, window in enumerate(windows):
            shift = (self.at * 16 + moved + (-first - 16 * p) % 128) & 127
            to = self.to + k * self.wide + window * self.stride
            found.append((to, pltpu.roll(tile, shift, 1)))
        return found

    def put(self, planes):
        old = [self.grid[to] for to, _ in planes]
        for (to, moved), before in zip(planes, old):
            self.grid[to] = jnp.where(self.here, moved, before)


def code_of(meta, column, index):
    return meta[column, 0, 0, 96 + index].astype(I32) - 1


def filter_kernel(parts, planes, across, spot, meta, received, swapped, out, grid, once):
    depth = planes + 4
    wide = parts // across
    lane = lanes()
    row = rows()
    zeros = jnp.zeros((8, 128), F32)

    def clear(index, carry):
        grid[index] = zeros
        return carry

    lax.fori_loop(0, depth * 8 * wide, clear, 0, unroll=16)
    begin = spot[0] * planes
    half = begin % 16 // 8
    side = jnp.where(begin % 8 == 0, 0, planes + 2) if planes < 8 else half * (planes + 2)

    def from_device(column, carry):
        work = []
        for e in range(3):
            placer = Placer(grid, depth * 8 * wide, wide, across, code_of(meta, column, e), column)
            pair = [received[column * 8 + 2 * e + k] for k in range(2)]
            if planes == 8:
                found = []
                for k in range(2):
                    found += placer.planes(pair[k], k, range(2, 10), 0)
                    found += placer.planes(
                        swapped[column * 8 + 2 * e + k],
                        k,
                        [jnp.where(half == 0, 10 + p, p) for p in range(2)],
                        0,
                        jnp.where(half == 0, 0, 32),
                    )
                work.append((placer, found))
            else:
                for window in range(depth):
                    p = begin % 8 + window - 2

                    @pl.when((p >= 0) & (p < 8))
                    def _(p=p, window=window, pair=pair, placer=placer):
                        found = []
                        for k in range(2):
                            found += placer.planes(pair[k], k, [window], 0, 128 - 16 * p)
                        placer.put(found)

        for e in range(3):
            code = code_of(meta, column, 3 + e)
            placer = Placer(grid, depth * 8 * wide, wide, across, code, column)
            found = []
            for k in range(2):
                found += placer.planes(received[column * 8 + 6 + k], k, [side, side + 1], 32 * e)
            work.append((placer, found))
        for placer, found in work:
            placer.put(found)
        return carry

    lax.fori_loop(0, parts, from_device, 0)

    def relax(ref, window, y, x):
        here = (window * 8 + y) * wide + x
        tile = ref[here]
        north = ref[here + wide] if y < 7 else zeros
        south = ref[here - wide] if y > 0 else zeros
        east = ref[here + 1] if x < wide - 1 else zeros
        west = ref[here - 1] if x > 0 else zeros
        near = ref[here + 8 * wide] + ref[here - 8 * wide]
        near = near + pltpu.roll(jnp.where(row == 0, north, tile), 7, 0)
        near = near + pltpu.roll(jnp.where(row == 7, south, tile), 1, 0)
        near = near + pltpu.roll(jnp.where(lane == 0, east, tile), 127, 1)
        near = near + pltpu.roll(jnp.where(lane == 127, west, tile), 1, 1)
        return (grid[here] + 2.0 * near) * (1.0 / 13.0)

    first = spot[1] == 0
    last = spot[1] == spot[2] - 1

    def sweep_once(window, carry):
        gone = (first & (window < 2)) | (last & (window >= planes + 2))
        keep = jnp.where(gone, 0.0, 1.0).astype(F32)
        for y in range(8):
            for x in range(wide):
                once[(window * 8 + y) * wide + x] = relax(grid, window, y, x) * keep
        return carry

    lax.fori_loop(1, depth - 1, sweep_once, 0, unroll=5)

    def sweep_again(window, carry):
        for y in range(8):
            for x in range(wide):
                out[window - 2, 8 * y : 8 * y + 8, 128 * x : 128 * x + 128] = relax(
                    once, window, y, x
                )
        return carry

    lax.fori_loop(2, depth - 2, sweep_again, 0, unroll=4)


VMEM = pl.BlockSpec(memory_space=pltpu.VMEM)
SMEM = pl.BlockSpec(memory_space=pltpu.SMEM)
HBM = pl.BlockSpec(memory_space=pltpu.HBM)
BIG = 32 * 1024 * 1024
WHOLE = 60 * 1024 * 1024


def meta_of(index):
    return pl.BlockSpec((1, 8, 128), lambda i: (index, 0, 0), memory_space=pltpu.SMEM)


def params(limit=BIG):
    return pltpu.CompilerParams(vmem_limit_bytes=limit)


def tiles(count):
    return jax.ShapeDtypeStruct((count, 8, 128), F32)


def per_device(
    material_fraction, primal_heat_solution, dual_load, dual_prior_design, holder_cube_location
):
    parts = lax.axis_size("ba")
    groups = lax.axis_size("gz")
    member = lax.axis_index("ba")
    group = lax.axis_index("gz")
    planes = 64 // parts
    parity = (member % 2).reshape(1).astype(I32)
    place = holder_cube_location
    fields = [
        field.reshape(128, 1024)
        for field in (material_fraction, primal_heat_solution, dual_load, dual_prior_design)
    ]
    near, far = pl.pallas_call(
        pack_kernel,
        out_shape=(tiles(X_TILES), tiles(X_TILES)),
        in_specs=[SMEM, SMEM, HBM, HBM, HBM, HBM],
        out_specs=(VMEM, VMEM),
        scratch_shapes=[pltpu.VMEM((128, 1024), F32)] * 4
        + [pltpu.VMEM((384 * GROUP, 1024), jnp.bfloat16), pltpu.SemaphoreType.DMA((4, 4))],
        compiler_params=params(WHOLE),
        name="pack",
    )(place, parity, *fields)
    inner = [(i, i ^ 1) for i in range(parts)]
    outer = [(i, i + 1 if i % 2 else i - 1) for i in range(1, parts - 1)]
    near = lax.ppermute(near, "ba", inner)
    far = lax.ppermute(far, "ba", outer)
    up, down = pl.pallas_call(
        corner_kernel,
        out_shape=(tiles(Z_TILES), tiles(Z_TILES)),
        in_specs=[SMEM, meta_of(X_TILES - 1), meta_of(X_TILES - 1)] + [VMEM] * 6,
        out_specs=(VMEM, VMEM),
        grid=(1,),
        compiler_params=params(),
        name="corners",
    )(place, near, far, *fields, near, far)
    rising = [(i, i + 1) for i in range(groups - 1)]
    falling = [(i + 1, i) for i in range(groups - 1)]
    from_below = lax.ppermute(up, "gz", rising)
    from_above = lax.ppermute(down, "gz", falling)
    meta_z = meta_of(Z_TILES - 1)
    meta_x = meta_of(X_TILES - 1)
    early = pltpu.VMEM((E_TILES, 8, 128), F32)
    dual1, dual2, coarse = pl.pallas_call(
        early_kernel,
        out_shape=(tiles(E_TILES), tiles(E_TILES), jax.ShapeDtypeStruct((2, 64, 128), F32)),
        in_specs=[SMEM, SMEM, meta_x, meta_x] + [VMEM] * 6,
        out_specs=(VMEM, VMEM, VMEM),
        scratch_shapes=[
            pltpu.SMEM((145,), I32),
            pltpu.SMEM((16 * 8,), I32),
            pltpu.SMEM((32 * 8,), I32),
            early,
            early,
            early,
            early,
            pltpu.VMEM((6 * E_TILES, 8, 128), F32),
            early,
            pltpu.VMEM((128, 1024), F32),
            pltpu.VMEM((128, 128), F32),
        ],
        grid=(1,),
        cost_estimate=pl.CostEstimate(flops=10**9, bytes_accessed=3 * 10**7, transcendentals=0),
        compiler_params=params(),
        name="early",
    )(place, parity, near, far, *fields, near, far)
    late = pltpu.VMEM((L_TILES, 8, 128), F32)
    dual, chunks = pl.pallas_call(
        functools.partial(late_kernel, parts),
        out_shape=(jax.ShapeDtypeStruct((128, 1024), F32), tiles(8 * parts)),
        in_specs=[SMEM, SMEM, meta_x, meta_x, meta_z, meta_z] + [VMEM] * 11,
        out_specs=(HBM, VMEM),
        scratch_shapes=[
            pltpu.VMEM((128, 1024), F32),
            pltpu.SemaphoreType.DMA,
            pltpu.SMEM((145,), I32),
            pltpu.SMEM((10 * 8,), I32),
            pltpu.SMEM((20 * 8,), I32),
            pltpu.SMEM((16,), I32),
            pltpu.SMEM((24,), I32),
            late,
            late,
            late,
            late,
            late,
            late,
            pltpu.VMEM((6 * L_TILES, 8, 128), F32),
            late,
            pltpu.VMEM((L_SLAB, 8, 128), F32),
            pltpu.VMEM((80, 1024), F32),
            pltpu.VMEM((80, 128), F32),
            pltpu.VMEM((2, 40, 128), F32),
            pltpu.VMEM((64, 128), F32),
            pltpu.VMEM((22, 8, 128), F32),
        ],
        grid=(1,),
        compiler_params=params(),
        name="late",
    )(
        place,
        parity,
        near,
        far,
        from_above,
        from_below,
        *fields,
        near,
        far,
        from_above,
        from_below,
        dual1,
        dual2,
        coarse,
    )
    received = lax.all_to_all(chunks, "ba", split_axis=0, concat_axis=0, tiled=True)
    swapped = lax.ppermute(received, "ba", inner) if planes == 8 else received
    spot = jnp.stack([member, group * parts + member, jnp.int32(groups * parts)]).astype(I32)
    wide = 32 * parts // 128
    codes = received.reshape(parts, 8, 8, 128)
    codes_spec = pl.BlockSpec((parts, 1, 8, 128), lambda i: (0, 6, 0, 0), memory_space=pltpu.SMEM)
    window = (planes + 4) * 8 * wide
    filtered = pl.pallas_call(
        functools.partial(filter_kernel, parts, planes, 4),
        out_shape=jax.ShapeDtypeStruct((planes, 64, 32 * parts), F32),
        in_specs=[SMEM, codes_spec, VMEM, VMEM],
        out_specs=VMEM,
        scratch_shapes=[pltpu.VMEM((2 * window, 8, 128), F32), pltpu.VMEM((window, 8, 128), F32)],
        grid=(1,),
        compiler_params=params(),
        name="smooth",
    )(spot, codes, received, swapped)
    return (dual.reshape(material_fraction.shape), filtered)


def solution(mesh):
    spec = P(("gz", "ba"), None, None)
    return jax.shard_map(
        per_device,
        mesh=mesh,
        in_specs=(spec, spec, spec, spec, P(("gz", "ba"))),
        out_specs=(spec, spec),
        check_vma=False,
    )
```

```python
import functools

import jax
import jax.numpy as jnp
from jax import lax
from jax.experimental import pallas as pl
from jax.experimental.pallas import tpu as pltpu
from jax.sharding import PartitionSpec as P

SLOTS = 4
KMIN = 0.01
HEAT = 0.05
F32 = jnp.float32
I32 = jnp.int32

E_SLAB = 128
E_ZERO = 160
E_TILES = 192
L_INNER = 32
L_UP = 64
L_DOWN = 88
L_SLAB = 112
L_ZERO = 140
L_TILES = 148
X_TILES = 33
Z_SLABS = 72
Z_TILES = 85
DUMMY = 29
GROUP = 4


def lanes():
    return lax.broadcasted_iota(I32, (8, 128), 1)


def rows():
    return lax.broadcasted_iota(I32, (8, 128), 0)


def take(tile, index):
    return jnp.take_along_axis(tile, index, axis=1)


def row_of(values):
    lane = lanes()
    result = jnp.zeros((8, 128), F32)
    for index, value in enumerate(values):
        result = jnp.where(lane == index, (value + 1).astype(F32), result)
    return result


def position_at(meta, index):
    return meta[0, 0, index].astype(I32) - 1


def as_int(flag):
    return jnp.where(flag, 1, 0).astype(I32)


def pack_kernel(
    place,
    parity_ref,
    mat_in,
    heat_in,
    load_in,
    prior_in,
    near,
    far,
    mat,
    heat,
    load,
    prior,
    parts,
    sems,
):
    pairs = ((mat_in, mat), (heat_in, heat), (prior_in, prior), (load_in, load))
    fetches = [
        [
            pltpu.make_async_copy(
                source.at[pl.ds(32 * s, 32)], target.at[pl.ds(32 * s, 32)], sems.at[k, s]
            )
            for k, (source, target) in enumerate(pairs)
        ]
        for s in range(SLOTS)
    ]
    for slot_fetches in fetches:
        for fetch in slot_fetches:
            fetch.start()
    cell = lax.broadcasted_iota(I32, (1024, 256), 0)
    column = lax.broadcasted_iota(I32, (1024, 256), 1)
    deep = column % 128 // 32
    flipped = (column // 128) != parity_ref[0]
    wanted = 32 * (column % 32) + jnp.where(flipped, deep, 31 - deep)
    pick = jnp.where(cell == wanted, 1.0, 0.0).astype(jnp.bfloat16)
    depth = lanes() // 32
    def field(moved, k, lead, c, side):
        high, mid, low = (
            moved[
                384 * lead + (3 * k + third) * 32 + 8 * c : 384 * lead + (3 * k + third) * 32 + 8 * c + 8,
                128 * side : 128 * side + 128,
            ]
            for third in range(3)
        )
        return (high + mid) + low

    for s in range(SLOTS):
        for fetch in fetches[s]:
            fetch.wait()
        lead = s % GROUP
        for k, ref in enumerate((mat, heat, prior, load)):
            rest = ref[32 * s : 32 * s + 32, :]
            for third in range(3):
                part = rest.astype(jnp.bfloat16)
                at = 384 * lead + (3 * k + third) * 32
                parts[at : at + 32, :] = part
                rest = rest - part.astype(F32)
        if lead < GROUP - 1:
            continue
        moved = jnp.dot(parts[...], pick, preferred_element_type=F32)
        for lead in range(GROUP):
            slot = s - GROUP + 1 + lead
            for side, out in enumerate((near, far)):
                for c in range(4):
                    fraction, warm, dual, given = (
                        field(moved, k, lead, c, side) for k in range(4)
                    )
                    own = conductivity(fraction)
                    beyond = conduct(own, pltpu.roll(own, 96, 1)) * pltpu.roll(dual, 96, 1)
                    given = pltpu.roll(given + jnp.where(depth == 1, beyond, 0.0), 64, 1)
                    unit = 4 * slot + c
                    out[unit] = jnp.where(depth == 3, pltpu.roll(warm, 96, 1), fraction)
                    out[16 + unit] = jnp.where(depth < 2, dual, given)
    meta = row_of([place[s] for s in range(SLOTS)])
    near[X_TILES - 1] = meta
    far[X_TILES - 1] = meta


def corner_kernel(
    place, near_meta, far_meta, mat, heat, load, prior, near, far, up, down
):
    values = [place[s] for s in range(SLOTS)]
    start = as_int(values[SLOTS - 1] >= 0)
    row = rows()

    def layer(out, to, at, j, rising):
        fraction, warm, given, dual = (
            ref[pl.ds(at, 8), 128 * j : 128 * j + 128] for ref in (mat, heat, load, prior)
        )
        step = 1 if rising else 7
        own = conductivity(fraction)
        beyond = conduct(own, pltpu.roll(own, step, 0)) * pltpu.roll(dual, step, 0)
        given = given + jnp.where(row == (2 if rising else 5), beyond, 0.0)
        spare, two = ((row == 0, row < 2) if rising else (row == 7, row > 5))
        a, b, c = ((5, 4, 2) if rising else (7, 5, 3))
        out[to] = jnp.where(spare, pltpu.roll(warm, a, 0), fraction)
        out[to + 24] = jnp.where(two, pltpu.roll(warm, b, 0), dual)
        out[to + 48] = jnp.where(two, pltpu.roll(warm, c, 0), given)

    for i in range(3):
        top = pl.multiple_of((start + i) * 32 + 24, 8)
        for j in range(8):
            layer(up, 8 * i + j, top, j, True)
            layer(down, 8 * i + j, 32 * i, j, False)
    for b, (meta, source) in enumerate(((near_meta, near), (far_meta, far))):
        listed = [position_at(meta, s) for s in range(SLOTS)]
        values = values + listed
        start = as_int(listed[SLOTS - 1] >= 0)
        for field in range(2):
            for i in range(3):
                to = Z_SLABS + b * 6 + field * 3 + i
                up[to] = source[field * 16 + (start + i) * 4 + 3]
                down[to] = source[field * 16 + i * 4]
    meta_tile = row_of(values)
    up[Z_TILES - 1] = meta_tile
    down[Z_TILES - 1] = meta_tile


def conduct(own, beside):
    return (2.0 * own) * beside / jnp.maximum(own + beside, KMIN)


def conductivity(fraction):
    return KMIN + (1.0 - KMIN) * fraction * fraction * fraction


def cell_of(x, y, z):
    return ((z + 1) * 6 + y + 1) * 4 + x + 1


def clear_cells(cells, zero):
    def clear(index, carry):
        cells[index] = zero
        return carry

    lax.fori_loop(0, 144, clear, 0, unroll=16)


def enter(cells, position, wanted, x, z, tile):
    here = jnp.where(wanted, cell_of(x, position // 2 % 4, z), 144)
    cells[here] = tile
    return jnp.where(wanted, here, DUMMY)


def fill(table, unit, values):
    for k, value in enumerate(values):
        table[unit * 8 + k] = value


class Stencil:
    def __init__(self, weights, stride):
        self.lane = lanes()
        row = rows()
        self.top_row = row == 0
        self.last_row = row == 7
        self.x_cell = self.lane % 32
        self.y_block = self.lane // 32
        self.face_block = self.lane // 4
        self.face_lane = 32 * (self.lane % 4)
        self.weights = weights
        self.stride = stride

    def above(self, tile, other):
        return pltpu.roll(jnp.where(self.top_row, other, tile), 7, 0)

    def below(self, tile, other):
        return pltpu.roll(jnp.where(self.last_row, other, tile), 1, 0)

    def brick(self, table, unit):
        base, up, down, north, south, east, west, px = (table[unit * 8 + k] for k in range(8))
        lane, x_cell = (self.lane, self.x_cell)
        own_lane = 31 * px
        brick_at = jnp.where(px == 1, west, east)
        slab_at = jnp.where(px == 1, east, west)
        from_brick = x_cell == own_lane
        to_brick = x_cell == 31 - own_lane
        index = jnp.where(to_brick, 32 * self.y_block + own_lane, self.y_block)
        step = jnp.where(to_brick, 0, 4)

        def around(ref, j):
            tile = ref[base + j]
            after = ref[base + j + 1] if j < 7 else ref[north]
            before = ref[base + j - 1] if j > 0 else ref[south + 7]
            beside = ref[slab_at]
            moved = 0
            if j == 0:
                beside, moved = (pltpu.roll(beside, 4, 1), 1)
            elif j == 7:
                beside, moved = (jnp.where(px == 1, pltpu.roll(beside, 4, 1), beside), px)
            both = jnp.where(from_brick, ref[brick_at + j], beside)
            edge = take(both, index + step * (j + moved))
            return tile, (
                jnp.where(x_cell == 31, edge, pltpu.roll(tile, 127, 1)),
                jnp.where(x_cell == 0, edge, pltpu.roll(tile, 1, 1)),
                pltpu.roll(jnp.where(lane < 32, after, tile), 96, 1),
                pltpu.roll(jnp.where(lane >= 96, before, tile), 32, 1),
                self.above(tile, ref[up + j]),
                self.below(tile, ref[down + j]),
            )

        return base, around

    def slab(self, table, unit):
        at, up, down, north, south, face, column = (table[unit * 8 + k] for k in range(7))
        lane, x_cell = (self.lane, self.x_cell)
        index = self.face_lane + column

        def around(ref):
            tile = ref[at]
            edge = take(ref[face], index)
            for j in range(1, 8):
                edge = jnp.where(self.face_block == j, take(ref[face + j], index), edge)
            return tile, (
                pltpu.roll(tile, 96, 1),
                jnp.where(lane < 32, edge, pltpu.roll(tile, 32, 1)),
                jnp.where(x_cell == 31, pltpu.roll(ref[north], 31, 1), pltpu.roll(tile, 127, 1)),
                jnp.where(x_cell == 0, pltpu.roll(ref[south], 97, 1), pltpu.roll(tile, 1, 1)),
                self.above(tile, ref[up]),
                self.below(tile, ref[down]),
            )

        return at, around

    def first(self, t, source, inverse, dual1, own_kappa, beside_kappa, beside):
        total = jnp.full((8, 128), HEAT, F32)
        flux = source[t]
        for k in range(6):
            weight = conduct(own_kappa, beside_kappa[k])
            self.weights[k * self.stride + t] = weight
            total = total + weight
            flux = flux + weight * beside[k]
        scale = 1.0 / total
        inverse[t] = scale
        dual1[t] = flux * scale

    def later(self, t, source, inverse, beside):
        flux = source[t]
        for k in range(6):
            flux = flux + self.weights[k * self.stride + t] * beside[k]
        return flux * inverse[t]

    def sensitivity(self, t, warm, warms, dual, duals):
        total = jnp.zeros((8, 128), F32)
        for k in range(6):
            total = total + jnp.where(
                self.weights[k * self.stride + t] > 0,
                (warms[k] - warm) * (duals[k] - dual),
                0.0,
            )
        return total


def factor_of(fraction):
    return (-1.5 * (1.0 - KMIN)) * fraction * fraction


def spread(to, first, second, kappa, temperature, source, dual0):
    kappa[to] = conductivity(first)
    dual0[to] = jnp.where(lanes() < 64, second, 0.0)
    source[to] = pltpu.roll(second, 64, 1)
    temperature[to] = pltpu.roll(first, 32, 1)


def shrink_table():
    cell = lax.broadcasted_iota(I32, (512, 128), 0)
    coarse = lax.broadcasted_iota(I32, (512, 128), 1)
    matches = (cell // 64 == coarse // 16) & (cell % 32 // 2 == coarse % 16)
    return jnp.where(matches, 0.125, 0.0).astype(F32)


def restrict(sens, summed, out, count):
    shrink = shrink_table()
    for half in range(2):
        summed[...] = jnp.dot(
            sens[:, 512 * half : 512 * half + 512],
            shrink,
            precision=lax.Precision.HIGHEST,
            preferred_element_type=F32,
        )
        for r in range(count):
            out[half, 8 * r : 8 * r + 8, :] = (
                summed[pl.ds(16 * r, 8, stride=2), :] + summed[pl.ds(16 * r + 1, 8, stride=2), :]
            )


def early_kernel(
    place,
    parity_ref,
    near_meta,
    far_meta,
    mat,
    heat,
    load,
    prior,
    near,
    far,
    dual1,
    dual2,
    coarse,
    cells,
    brick_table,
    slab_table,
    kappa,
    temperature,
    source,
    dual0,
    weights,
    inverse,
    sens,
    summed,
):
    parity = parity_ref[0]
    clear_cells(cells, E_ZERO)
    own = [place[s] for s in range(SLOTS)]
    own_cell = [enter(cells, q, q >= 0, q % 2, q // 8, 32 * s) for s, q in enumerate(own)]
    slab_cell = []
    slab_live = []
    for b, meta in enumerate((near_meta, far_meta)):
        east = parity == b
        column = jnp.where(east, 0, 1)
        x = jnp.where(east, 2, -1)
        for s in range(SLOTS):
            q = position_at(meta, s)
            wanted = (q >= 0) & (q % 2 == column)
            slab_live.append((wanted, q))
            slab_cell.append(
                enter(cells, q, wanted, x, q // 8, E_SLAB + 16 * b + 4 * s)
            )
    for s in range(SLOTS):
        here = own_cell[s]
        px = jnp.where(own[s] >= 0, own[s] % 2, 0)
        lift = jnp.where(own[s] >= 8, 24, 0)
        north, south = (cells[here + 4], cells[here - 4])
        east, west = (cells[here + 1], cells[here - 1])
        above, below = (cells[here + 24], cells[here - 24] + lift)
        for c in range(4):
            base = s * 32 + c * 8
            fill(
                brick_table,
                s * 4 + c,
                (
                    base,
                    base + 8 if c < 3 else above,
                    base - 8 if c > 0 else below,
                    north + 8 * c,
                    south + 8 * c,
                    east + jnp.where(px == 1, c, 8 * c),
                    west + jnp.where(px == 0, c, 8 * c),
                    px,
                ),
            )
    for b in range(2):
        inward = jnp.where(parity == b, -1, 1)
        column = jnp.where(parity == b, 31, 0)
        for s in range(SLOTS):
            here = slab_cell[4 * b + s]
            wanted, q = slab_live[4 * b + s]
            lift = jnp.where(q >= 8, 3, 0)
            north, south = (cells[here + 4], cells[here - 4])
            above, below = (cells[here + 24], cells[here - 24] + lift)
            face = cells[here + inward]
            live = as_int(wanted)
            for c in range(4):
                unit = 16 * b + 4 * s + c
                fill(
                    slab_table,
                    unit,
                    (
                        E_SLAB + unit,
                        E_SLAB + unit + 1 if c < 3 else above,
                        E_SLAB + unit - 1 if c > 0 else below,
                        north + c,
                        south + c,
                        face + 8 * c,
                        column,
                        live,
                    ),
                )

    zeros = jnp.zeros((8, 128), F32)
    for ref in (kappa, temperature, dual0, dual1, dual2):
        for t in range(32):
            ref[E_ZERO + t] = zeros

    def own_unit(unit, carry):
        at = pl.multiple_of(unit * 8, 8)
        active = place[unit // 4] >= 0
        for j in range(8):
            span = slice(128 * j, 128 * j + 128)
            t = unit * 8 + j
            kappa[t] = jnp.where(active, conductivity(mat[pl.ds(at, 8), span]), 0.0)
            source[t] = jnp.where(active, load[pl.ds(at, 8), span], 0.0)
            dual0[t] = prior[pl.ds(at, 8), span]
            temperature[t] = heat[pl.ds(at, 8), span]
        return carry

    lax.fori_loop(0, 16, own_unit, 0)
    for b, message in enumerate((near, far)):
        for t in range(16):
            to = E_SLAB + 16 * b + t
            spread(to, message[t], message[t + 16], kappa, temperature, source, dual0)

    stencil = Stencil(weights, E_TILES)

    def slabs(body):
        def slot(index, carry):
            @pl.when(slab_table[index * 32 + 7] > 0)
            def _():
                for c in range(4):
                    body(*stencil.slab(slab_table, index * 4 + c))

            return carry

        lax.fori_loop(0, 8, slot, 0)

    def bricks(body):
        def four(step, carry):
            for k in range(4):
                unit = 4 * step + k
                base, around = stencil.brick(brick_table, unit)
                for j in range(8):
                    body(unit, base, around, j)
            return carry

        lax.fori_loop(0, 4, four, 0)

    def brick_first(unit, base, around, j):
        own_kappa, beside_kappa = around(kappa, j)
        stencil.first(
            base + j, source, inverse, dual1, own_kappa, beside_kappa, around(dual0, j)[1]
        )

    def slab_first(t, around):
        own_kappa, beside_kappa = around(kappa)
        stencil.first(t, source, inverse, dual1, own_kappa, beside_kappa, around(dual0)[1])

    def brick_second(unit, base, around, j):
        dual2[base + j] = stencil.later(base + j, source, inverse, around(dual1, j)[1])

    def slab_second(t, around):
        dual2[t] = stencil.later(t, source, inverse, around(dual1)[1])

    def brick_third(unit, base, around, j):
        at = pl.multiple_of(unit * 8, 8)
        dual, duals = around(dual2, j)
        warm, warms = around(temperature, j)
        total = stencil.sensitivity(base + j, warm, warms, dual, duals)
        span = slice(128 * j, 128 * j + 128)
        sens[pl.ds(at, 8), span] = factor_of(mat[pl.ds(at, 8), span]) * total

    bricks(brick_first)
    slabs(slab_first)
    bricks(brick_second)
    slabs(slab_second)
    bricks(brick_third)
    restrict(sens, summed, coarse, 8)


def late_kernel(
    parts,
    place,
    parity_ref,
    near_meta,
    far_meta,
    up_meta,
    down_meta,
    mat,
    heat,
    load,
    prior,
    near,
    far,
    z_up,
    z_down,
    early1,
    early2,
    coarse,
    dual_out,
    chunks,
    dual_rows,
    dual_sem,
    cells,
    brick_table,
    slab_table,
    brick_list,
    slab_list,
    kappa,
    temperature,
    source,
    dual0,
    dual1,
    dual2,
    weights,
    inverse,
    factor,
    sens,
    summed,
    edge,
    whole,
    turned,
):
    parity = parity_ref[0]
    lane = lanes()
    row = rows()
    clear_cells(cells, L_ZERO)
    own = [place[s] for s in range(SLOTS)]

    def at_edge(q):
        return ((q >= 0) & (q < 8)) | (q >= 24)

    own_cell = [
        enter(cells, q, at_edge(q), q % 2, q // 8, 8 * s) for s, q in enumerate(own)
    ]
    lists_up = [[position_at(up_meta, 4 * k + s) for s in range(SLOTS)] for k in range(3)]
    lists_down = [[position_at(down_meta, 4 * k + s) for s in range(SLOTS)] for k in range(3)]

    def shifted(listed):
        full = listed[SLOTS - 1] >= 0
        return [jnp.where(full, listed[i + 1], listed[i]) for i in range(3)]

    ups = [listed[:3] for listed in lists_up]
    downs = [shifted(listed) for listed in lists_down]
    brick_live = [at_edge(q) for q in own]
    brick_live += [(q >= 0) & (q < 8) for q in ups[0]]
    brick_live += [q >= 24 for q in downs[0]]
    halo_cell = [
        enter(cells, q, brick_live[4 + i], q % 2, 4, L_UP + 8 * i) for i, q in enumerate(ups[0])
    ]
    halo_cell += [
        enter(cells, q, brick_live[7 + i], q % 2, -1, L_DOWN + 8 * i)
        for i, q in enumerate(downs[0])
    ]
    slab_cell = []
    slab_live = []
    slab_own = []
    for b, meta in enumerate((near_meta, far_meta)):
        east = parity == b
        column = jnp.where(east, 0, 1)
        x = jnp.where(east, 2, -1)
        base = L_SLAB + 14 * b
        mine = [position_at(meta, s) for s in range(SLOTS)]
        slab_own.append(mine)
        tests = [at_edge(q) & (q % 2 == column) for q in mine]
        tests += [(q >= 0) & (q < 8) & (q % 2 == column) for q in ups[1 + b]]
        tests += [(q >= 24) & (q % 2 == column) for q in downs[1 + b]]
        slab_live += tests
        for k, q in enumerate(mine + ups[1 + b] + downs[1 + b]):
            z = q // 8 if k < 4 else 4 if k < 7 else -1
            slab_cell.append(enter(cells, q, tests[k], x, z, base + (k if k < 4 else 4 + k)))

    high = [as_int(q >= 24) for q in own]
    for s in range(SLOTS):
        here = own_cell[s]
        px = jnp.where(own[s] >= 0, own[s] % 2, 0)
        inner = L_INNER + 8 * s
        fill(
            brick_table,
            s,
            (
                jnp.int32(8 * s),
                jnp.where(high[s] == 1, cells[here + 24], inner),
                jnp.where(high[s] == 1, inner, cells[here - 24]),
                cells[here + 4],
                cells[here - 4],
                cells[here + 1],
                cells[here - 1],
                px,
            ),
        )
    for i in range(6):
        here = halo_cell[i]
        q = (ups[0] + downs[0])[i]
        px = jnp.where(q >= 0, q % 2, 0)
        fill(
            brick_table,
            4 + i,
            (
                jnp.int32(L_UP + 8 * i),
                jnp.int32(L_ZERO) if i < 3 else cells[here + 24],
                cells[here - 24] if i < 3 else jnp.int32(L_ZERO),
                cells[here + 4],
                cells[here - 4],
                cells[here + 1],
                cells[here - 1],
                px,
            ),
        )
    for b in range(2):
        inward = jnp.where(parity == b, -1, 1)
        column = jnp.where(parity == b, 31, 0)
        base = L_SLAB + 14 * b
        for k in range(10):
            here = slab_cell[10 * b + k]
            above, below = (cells[here + 24], cells[here - 24])
            if k < 4:
                top = slab_own[b][k] >= 24
                inner = base + 4 + k
                above, below = (jnp.where(top, above, inner), jnp.where(top, inner, below))
            elif k < 7:
                above = jnp.int32(L_ZERO)
            else:
                below = jnp.int32(L_ZERO)
            fill(
                slab_table,
                10 * b + k,
                (
                    jnp.int32(base + (k if k < 4 else 4 + k)),
                    above,
                    below,
                    cells[here + 4],
                    cells[here - 4],
                    cells[here + inward],
                    column,
                ),
            )

    def listed(target, flags):
        count = jnp.int32(0)
        for index, flag in enumerate(flags):
            target[count] = index
            count = count + as_int(flag)
        last = target[jnp.maximum(count - 1, 0)]
        for k in range(3):
            target[count + k] = last
        return count

    brick_count = listed(brick_list, brick_live)
    slab_count = listed(slab_list, slab_live)

    zeros = jnp.zeros((8, 128), F32)
    for ref in (kappa, temperature, dual0, dual1, dual2):
        for t in range(8):
            ref[L_ZERO + t] = zeros

    for s in range(SLOTS):
        active = own[s] >= 0
        for to, chunk in ((8 * s, 3 * high[s]), (L_INNER + 8 * s, 1 + high[s])):
            at = pl.multiple_of(s * 32 + 8 * chunk, 8)
            for j in range(8):
                span = slice(128 * j, 128 * j + 128)
                fraction = mat[pl.ds(at, 8), span]
                kappa[to + j] = jnp.where(active, conductivity(fraction), 0.0)
                dual0[to + j] = prior[pl.ds(at, 8), span]
                temperature[to + j] = heat[pl.ds(at, 8), span]
                if to < L_INNER:
                    source[to + j] = load[pl.ds(at, 8), span]
                    factor[to + j] = factor_of(fraction)
                else:
                    dual1[to + j] = early1[32 * s + 8 * chunk + j]
                    dual2[to + j] = early2[32 * s + 8 * chunk + j]

    for k, message in enumerate((z_up, z_down)):
        for t in range(24):
            to = L_UP + 24 * k + t
            one, two, three = (message[t], message[24 + t], message[48 + t])
            a, b, c = ((3, 4, 6) if k else (1, 3, 5))
            kappa[to] = conductivity(one)
            dual0[to] = jnp.where(row >= 2 if k else row < 6, two, 0.0)
            source[to] = three
            temperature[to] = jnp.where(
                row == 3 if k else row == 0,
                pltpu.roll(one, a, 0),
                jnp.where(
                    row < 6 if k else row < 3,
                    pltpu.roll(two, b, 0),
                    pltpu.roll(three, c, 0),
                ),
            )
            factor[to] = factor_of(one)

    def slab_tile(to, message, at, step):
        spread(to, message[at], message[at + step], kappa, temperature, source, dual0)

    for b, message in enumerate((near, far)):
        base = L_SLAB + 14 * b
        for s in range(SLOTS):
            top = as_int(slab_own[b][s] >= 24)
            slab_tile(base + s, message, 4 * s + 3 * top, 16)
            inner = 4 * s + 1 + top
            slab_tile(base + 4 + s, message, inner, 16)
            dual1[base + 4 + s] = early1[E_SLAB + 16 * b + inner]
            dual2[base + 4 + s] = early2[E_SLAB + 16 * b + inner]
        for i in range(3):
            slab_tile(base + 8 + i, z_up, Z_SLABS + 6 * b + i, 3)
            slab_tile(base + 11 + i, z_down, Z_SLABS + 6 * b + i, 3)

    stencil = Stencil(weights, L_TILES)

    def bricks(body):
        def two(step, carry):
            for k in range(2):
                unit = brick_list[2 * step + k]
                base, around = stencil.brick(brick_table, unit)
                for j in range(8):
                    body(base, around, j)
            return carry

        lax.fori_loop(0, (brick_count + 1) // 2, two, 0)

    def slabs(body):
        def four(step, carry):
            for k in range(4):
                body(*stencil.slab(slab_table, slab_list[4 * step + k]))
            return carry

        lax.fori_loop(0, (slab_count + 3) // 4, four, 0)

    def brick_first(base, around, j):
        own_kappa, beside_kappa = around(kappa, j)
        stencil.first(
            base + j, source, inverse, dual1, own_kappa, beside_kappa, around(dual0, j)[1]
        )

    def slab_first(t, around):
        own_kappa, beside_kappa = around(kappa)
        stencil.first(t, source, inverse, dual1, own_kappa, beside_kappa, around(dual0)[1])

    def brick_second(base, around, j):
        dual2[base + j] = stencil.later(base + j, source, inverse, around(dual1, j)[1])

    def slab_second(t, around):
        dual2[t] = stencil.later(t, source, inverse, around(dual1)[1])

    def brick_third(base, around, j):
        dual, duals = around(dual2, j)
        warm, warms = around(temperature, j)
        total = stencil.sensitivity(base + j, warm, warms, dual, duals)
        at = jnp.where(base < L_INNER, base, base - 32)
        sens[pl.ds(pl.multiple_of(at, 8), 8), 128 * j : 128 * j + 128] = factor[base + j] * total

    bricks(brick_first)
    slabs(slab_first)
    bricks(brick_second)
    slabs(slab_second)
    for s in range(SLOTS):
        for c in range(4):
            for j in range(8):
                dual_rows[32 * s + 8 * c : 32 * s + 8 * c + 8, 128 * j : 128 * j + 128] = early2[
                    32 * s + 8 * c + j
                ]
        at = pl.multiple_of(32 * s + 24 * high[s], 8)
        for j in range(8):
            dual_rows[pl.ds(at, 8), 128 * j : 128 * j + 128] = jnp.where(
                brick_live[s], dual2[8 * s + j], early2[32 * s + 24 * high[s] + j]
            )

    writing = pltpu.make_async_copy(dual_rows, dual_out, dual_sem)
    writing.start()
    bricks(brick_third)

    restrict(sens, summed, edge, 5)
    for half in range(2):
        whole[...] = coarse[half]
        for s in range(SLOTS):
            at = 16 * s + 12 * high[s]
            whole[pl.ds(at, 4), :] = jnp.where(
                brick_live[s], edge[half, 4 * s : 4 * s + 4, :], coarse[half, pl.ds(at, 4), :]
            )

        for r in range(11):
            if r < 8:
                tile = whole[8 * r : 8 * r + 8, :]
            else:
                tile = edge[half, 8 * r - 48 : 8 * r - 40, :]
            for bit in (1, 2, 4):
                low_row = (row & bit) == 0
                low_lane = (lane & (16 * bit)) == 0
                swap_a = pltpu.roll(pltpu.roll(tile, 8 - bit, 0), 16 * bit, 1)
                swap_b = pltpu.roll(pltpu.roll(tile, bit, 0), 128 - 16 * bit, 1)
                tile = jnp.where(low_row == low_lane, tile, jnp.where(low_row, swap_a, swap_b))
            turned[2 * r + half] = tile

    y_block = lane // 32

    planes = 64 // parts
    level = [jnp.where(q >= 0, q // 8, 9) for q in own]

    def count(test):
        return functools.reduce(lambda a, b: a + b, [as_int(test(v)) for v in level])

    before = [count(lambda v, z=z: v < z) for z in range(5)]

    def nth(z, e):
        index = before[z] + e
        valid = index < before[z + 1]
        slot = jnp.minimum(index, SLOTS - 1)
        code = jnp.where(valid, place[slot] - 8 * z, -1)
        return slot, code

    for d in range(parts):
        z = d * planes // 16
        half = d * planes % 16 // 8
        codes = []
        for e in range(3):
            slot, code = nth(z, e)
            codes.append(code)
            for k in range(2):
                chunks[d * 8 + 2 * e + k] = turned[(slot * 2 + half) * 2 + k]
        start = d * planes % 8 == 0
        end = (d + 1) * planes % 8 == 0
        if planes >= 8:
            outside = -1 if half == 0 else 1
        else:
            outside = -1 if start else 1 if end else 0
        beyond = half + outside
        beside = [zeros, zeros]
        for e in range(3):
            if outside == 0:
                tile_at, lane_at, code = (0, 0, jnp.int32(-1))
            elif beyond in (0, 1):
                slot, code = nth(z, e)
                tile_at, lane_at = (slot * 2 + beyond, 96 if outside < 0 else 0)
            elif 0 <= z + outside <= 3:
                slot, code = nth(z + outside, e)
                tile_at, lane_at = (slot * 2 + (1 if outside < 0 else 0), 96 if outside < 0 else 0)
            elif outside < 0:
                q = downs[0][e]
                code = jnp.where(q >= 24, q - 24, -1)
                tile_at, lane_at = (8 + (3 + e) // 2, 64 * ((3 + e) % 2) + 32)
            else:
                q = ups[0][e]
                code = jnp.where((q >= 0) & (q < 8), q, -1)
                tile_at, lane_at = (8 + e // 2, 64 * (e % 2))
            codes.append(code)
            for k in range(2):
                tile = turned[tile_at * 2 + k]
                shift = (32 * e - lane_at) % 128
                if shift:
                    tile = pltpu.roll(tile, shift, 1)
                beside[k] = jnp.where(y_block == e, tile, beside[k])
        for e, code in enumerate(codes):
            beside[0] = jnp.where(lane == 96 + e, (code + 1).astype(F32), beside[0])
        for k in range(2):
            chunks[d * 8 + 6 + k] = beside[k]
    writing.wait()


class Placer:
    def __init__(self, grid, size, wide, across, code, column):
        self.grid = grid
        self.stride = 8 * wide
        self.wide = wide
        self.to = jnp.where(code >= 0, 0, size) + lax.div(column, across)
        code = jnp.maximum(code, 0)
        self.to = self.to + (code >> 1) * (2 * wide)
        self.at = (column * 2 + (code & 1)) & 7
        self.here = lanes() // 16 == self.at

    def planes(self, tile, k, windows, first, moved=0):
        found = []
        for p, window in enumerate(windows):
            shift = (self.at * 16 + moved + (-first - 16 * p) % 128) & 127
            to = self.to + k * self.wide + window * self.stride
            found.append((to, pltpu.roll(tile, shift, 1)))
        return found

    def put(self, planes):
        old = [self.grid[to] for to, _ in planes]
        for (to, moved), before in zip(planes, old):
            self.grid[to] = jnp.where(self.here, moved, before)


def code_of(meta, column, index):
    return meta[column, 0, 0, 96 + index].astype(I32) - 1


def filter_kernel(parts, planes, across, spot, meta, received, swapped, out, grid, once):
    depth = planes + 4
    wide = parts // across
    lane = lanes()
    row = rows()
    zeros = jnp.zeros((8, 128), F32)

    def clear(index, carry):
        grid[index] = zeros
        return carry

    lax.fori_loop(0, depth * 8 * wide, clear, 0, unroll=16)
    begin = spot[0] * planes
    half = begin % 16 // 8
    side = jnp.where(begin % 8 == 0, 0, planes + 2) if planes < 8 else half * (planes + 2)

    def from_device(column, carry):
        work = []
        for e in range(3):
            placer = Placer(grid, depth * 8 * wide, wide, across, code_of(meta, column, e), column)
            pair = [received[column * 8 + 2 * e + k] for k in range(2)]
            if planes == 8:
                found = []
                for k in range(2):
                    found += placer.planes(pair[k], k, range(2, 10), 0)
                    found += placer.planes(
                        swapped[column * 8 + 2 * e + k],
                        k,
                        [jnp.where(half == 0, 10 + p, p) for p in range(2)],
                        0,
                        jnp.where(half == 0, 0, 32),
                    )
                work.append((placer, found))
            else:
                for window in range(depth):
                    p = begin % 8 + window - 2

                    @pl.when((p >= 0) & (p < 8))
                    def _(p=p, window=window, pair=pair, placer=placer):
                        found = []
                        for k in range(2):
                            found += placer.planes(pair[k], k, [window], 0, 128 - 16 * p)
                        placer.put(found)

        for e in range(3):
            code = code_of(meta, column, 3 + e)
            placer = Placer(grid, depth * 8 * wide, wide, across, code, column)
            found = []
            for k in range(2):
                found += placer.planes(received[column * 8 + 6 + k], k, [side, side + 1], 32 * e)
            work.append((placer, found))
        for placer, found in work:
            placer.put(found)
        return carry

    lax.fori_loop(0, parts, from_device, 0)

    def relax(ref, window, y, x):
        here = (window * 8 + y) * wide + x
        tile = ref[here]
        north = ref[here + wide] if y < 7 else zeros
        south = ref[here - wide] if y > 0 else zeros
        east = ref[here + 1] if x < wide - 1 else zeros
        west = ref[here - 1] if x > 0 else zeros
        near = ref[here + 8 * wide] + ref[here - 8 * wide]
        near = near + pltpu.roll(jnp.where(row == 0, north, tile), 7, 0)
        near = near + pltpu.roll(jnp.where(row == 7, south, tile), 1, 0)
        near = near + pltpu.roll(jnp.where(lane == 0, east, tile), 127, 1)
        near = near + pltpu.roll(jnp.where(lane == 127, west, tile), 1, 1)
        return (grid[here] + 2.0 * near) * (1.0 / 13.0)

    first = spot[1] == 0
    last = spot[1] == spot[2] - 1

    def sweep_once(window, carry):
        gone = (first & (window < 2)) | (last & (window >= planes + 2))
        keep = jnp.where(gone, 0.0, 1.0).astype(F32)
        for y in range(8):
            for x in range(wide):
                once[(window * 8 + y) * wide + x] = relax(grid, window, y, x) * keep
        return carry

    lax.fori_loop(1, depth - 1, sweep_once, 0, unroll=5)

    def sweep_again(window, carry):
        for y in range(8):
            for x in range(wide):
                out[window - 2, 8 * y : 8 * y + 8, 128 * x : 128 * x + 128] = relax(
                    once, window, y, x
                )
        return carry

    lax.fori_loop(2, depth - 2, sweep_again, 0, unroll=4)


VMEM = pl.BlockSpec(memory_space=pltpu.VMEM)
SMEM = pl.BlockSpec(memory_space=pltpu.SMEM)
HBM = pl.BlockSpec(memory_space=pltpu.HBM)
BIG = 32 * 1024 * 1024
WHOLE = 60 * 1024 * 1024


def meta_of(index):
    return pl.BlockSpec((1, 8, 128), lambda i: (index, 0, 0), memory_space=pltpu.SMEM)


def params(limit=BIG):
    return pltpu.CompilerParams(vmem_limit_bytes=limit)


def tiles(count):
    return jax.ShapeDtypeStruct((count, 8, 128), F32)


def per_device(
    material_fraction, primal_heat_solution, dual_load, dual_prior_design, holder_cube_location
):
    parts = lax.axis_size("ba")
    groups = lax.axis_size("gz")
    member = lax.axis_index("ba")
    group = lax.axis_index("gz")
    planes = 64 // parts
    parity = (member % 2).reshape(1).astype(I32)
    place = holder_cube_location
    fields = [
        field.reshape(128, 1024)
        for field in (material_fraction, primal_heat_solution, dual_load, dual_prior_design)
    ]
    near, far = pl.pallas_call(
        pack_kernel,
        out_shape=(tiles(X_TILES), tiles(X_TILES)),
        in_specs=[SMEM, SMEM, HBM, HBM, HBM, HBM],
        out_specs=(VMEM, VMEM),
        scratch_shapes=[pltpu.VMEM((128, 1024), F32)] * 4
        + [pltpu.VMEM((384 * GROUP, 1024), jnp.bfloat16), pltpu.SemaphoreType.DMA((4, 4))],
        compiler_params=params(WHOLE),
        name="pack",
    )(place, parity, *fields)
    inner = [(i, i ^ 1) for i in range(parts)]
    outer = [(i, i + 1 if i % 2 else i - 1) for i in range(1, parts - 1)]
    near = lax.ppermute(near, "ba", inner)
    far = lax.ppermute(far, "ba", outer)
    up, down = pl.pallas_call(
        corner_kernel,
        out_shape=(tiles(Z_TILES), tiles(Z_TILES)),
        in_specs=[SMEM, meta_of(X_TILES - 1), meta_of(X_TILES - 1)] + [VMEM] * 6,
        out_specs=(VMEM, VMEM),
        grid=(1,),
        compiler_params=params(),
        name="corners",
    )(place, near, far, *fields, near, far)
    rising = [(i, i + 1) for i in range(groups - 1)]
    falling = [(i + 1, i) for i in range(groups - 1)]
    from_below = lax.ppermute(up, "gz", rising)
    from_above = lax.ppermute(down, "gz", falling)
    meta_z = meta_of(Z_TILES - 1)
    meta_x = meta_of(X_TILES - 1)
    early = pltpu.VMEM((E_TILES, 8, 128), F32)
    dual1, dual2, coarse = pl.pallas_call(
        early_kernel,
        out_shape=(tiles(E_TILES), tiles(E_TILES), jax.ShapeDtypeStruct((2, 64, 128), F32)),
        in_specs=[SMEM, SMEM, meta_x, meta_x] + [VMEM] * 6,
        out_specs=(VMEM, VMEM, VMEM),
        scratch_shapes=[
            pltpu.SMEM((145,), I32),
            pltpu.SMEM((16 * 8,), I32),
            pltpu.SMEM((32 * 8,), I32),
            early,
            early,
            early,
            early,
            pltpu.VMEM((6 * E_TILES, 8, 128), F32),
            early,
            pltpu.VMEM((128, 1024), F32),
            pltpu.VMEM((128, 128), F32),
        ],
        grid=(1,),
        cost_estimate=pl.CostEstimate(flops=10**9, bytes_accessed=3 * 10**7, transcendentals=0),
        compiler_params=params(),
        name="early",
    )(place, parity, near, far, *fields, near, far)
    late = pltpu.VMEM((L_TILES, 8, 128), F32)
    dual, chunks = pl.pallas_call(
        functools.partial(late_kernel, parts),
        out_shape=(jax.ShapeDtypeStruct((128, 1024), F32), tiles(8 * parts)),
        in_specs=[SMEM, SMEM, meta_x, meta_x, meta_z, meta_z] + [VMEM] * 11,
        out_specs=(HBM, VMEM),
        scratch_shapes=[
            pltpu.VMEM((128, 1024), F32),
            pltpu.SemaphoreType.DMA,
            pltpu.SMEM((145,), I32),
            pltpu.SMEM((10 * 8,), I32),
            pltpu.SMEM((20 * 8,), I32),
            pltpu.SMEM((16,), I32),
            pltpu.SMEM((24,), I32),
            late,
            late,
            late,
            late,
            late,
            late,
            pltpu.VMEM((6 * L_TILES, 8, 128), F32),
            late,
            pltpu.VMEM((L_SLAB, 8, 128), F32),
            pltpu.VMEM((80, 1024), F32),
            pltpu.VMEM((80, 128), F32),
            pltpu.VMEM((2, 40, 128), F32),
            pltpu.VMEM((64, 128), F32),
            pltpu.VMEM((22, 8, 128), F32),
        ],
        grid=(1,),
        compiler_params=params(),
        name="late",
    )(
        place,
        parity,
        near,
        far,
        from_above,
        from_below,
        *fields,
        near,
        far,
        from_above,
        from_below,
        dual1,
        dual2,
        coarse,
    )
    received = lax.all_to_all(chunks, "ba", split_axis=0, concat_axis=0, tiled=True)
    swapped = lax.ppermute(received, "ba", inner) if planes == 8 else received
    spot = jnp.stack([member, group * parts + member, jnp.int32(groups * parts)]).astype(I32)
    wide = 32 * parts // 128
    codes = received.reshape(parts, 8, 8, 128)
    codes_spec = pl.BlockSpec((parts, 1, 8, 128), lambda i: (0, 6, 0, 0), memory_space=pltpu.SMEM)
    window = (planes + 4) * 8 * wide
    filtered = pl.pallas_call(
        functools.partial(filter_kernel, parts, planes, 4),
        out_shape=jax.ShapeDtypeStruct((planes, 64, 32 * parts), F32),
        in_specs=[SMEM, codes_spec, VMEM, VMEM],
        out_specs=VMEM,
        scratch_shapes=[pltpu.VMEM((2 * window, 8, 128), F32), pltpu.VMEM((window, 8, 128), F32)],
        grid=(1,),
        compiler_params=params(),
        name="smooth",
    )(spot, codes, received, swapped)
    return (dual.reshape(material_fraction.shape), filtered)


def solution(mesh):
    spec = P(("gz", "ba"), None, None)
    return jax.shard_map(
        per_device,
        mesh=mesh,
        in_specs=(spec, spec, spec, spec, P(("gz", "ba"))),
        out_specs=(spec, spec),
        check_vma=False,
    )
```

```python
import functools

import jax
import jax.numpy as jnp
from jax import lax
from jax.experimental import pallas as pl
from jax.experimental.pallas import tpu as pltpu
from jax.sharding import PartitionSpec as P

SLOTS = 4
KMIN = 0.01
HEAT = 0.05
F32 = jnp.float32
I32 = jnp.int32

E_SLAB = 128
E_ZERO = 160
E_TILES = 192
L_INNER = 32
L_UP = 64
L_DOWN = 88
L_SLAB = 112
L_ZERO = 140
L_TILES = 148
X_TILES = 33
Z_SLABS = 72
Z_TILES = 85
DUMMY = 29
GROUP = 4


def lanes():
    return lax.broadcasted_iota(I32, (8, 128), 1)


def rows():
    return lax.broadcasted_iota(I32, (8, 128), 0)


def take(tile, index):
    return jnp.take_along_axis(tile, index, axis=1)


def row_of(values):
    lane = lanes()
    result = jnp.zeros((8, 128), F32)
    for index, value in enumerate(values):
        result = jnp.where(lane == index, (value + 1).astype(F32), result)
    return result


def position_at(meta, index):
    return meta[0, 0, index].astype(I32) - 1


def as_int(flag):
    return jnp.where(flag, 1, 0).astype(I32)


def pack_kernel(
    place,
    parity_ref,
    mat_in,
    heat_in,
    load_in,
    prior_in,
    near,
    far,
    mat,
    heat,
    load,
    prior,
    parts,
    sems,
):
    pairs = ((mat_in, mat), (heat_in, heat), (prior_in, prior), (load_in, load))
    fetches = [
        [
            pltpu.make_async_copy(
                source.at[pl.ds(32 * s, 32)], target.at[pl.ds(32 * s, 32)], sems.at[k, s]
            )
            for k, (source, target) in enumerate(pairs)
        ]
        for s in range(SLOTS)
    ]
    for slot_fetches in fetches:
        for fetch in slot_fetches:
            fetch.start()
    cell = lax.broadcasted_iota(I32, (1024, 256), 0)
    column = lax.broadcasted_iota(I32, (1024, 256), 1)
    deep = column % 128 // 32
    flipped = (column // 128) != parity_ref[0]
    wanted = 32 * (column % 32) + jnp.where(flipped, deep, 31 - deep)
    pick = jnp.where(cell == wanted, 1.0, 0.0).astype(jnp.bfloat16)
    depth = lanes() // 32
    def field(moved, k, lead, c, side):
        high, mid, low = (
            moved[
                384 * lead + (3 * k + third) * 32 + 8 * c : 384 * lead + (3 * k + third) * 32 + 8 * c + 8,
                128 * side : 128 * side + 128,
            ]
            for third in range(3)
        )
        return (high + mid) + low

    for s in range(SLOTS):
        for fetch in fetches[s]:
            fetch.wait()
        lead = s % GROUP
        for k, ref in enumerate((mat, heat, prior, load)):
            rest = ref[32 * s : 32 * s + 32, :]
            for third in range(3):
                part = rest.astype(jnp.bfloat16)
                at = 384 * lead + (3 * k + third) * 32
                parts[at : at + 32, :] = part
                rest = rest - part.astype(F32)
        if lead < GROUP - 1:
            continue
        moved = jnp.dot(parts[...], pick, preferred_element_type=F32)
        for lead in range(GROUP):
            slot = s - GROUP + 1 + lead
            for side, out in enumerate((near, far)):
                for c in range(4):
                    fraction, warm, dual, given = (
                        field(moved, k, lead, c, side) for k in range(4)
                    )
                    own = conductivity(fraction)
                    beyond = conduct(own, pltpu.roll(own, 96, 1)) * pltpu.roll(dual, 96, 1)
                    given = pltpu.roll(given + jnp.where(depth == 1, beyond, 0.0), 64, 1)
                    unit = 4 * slot + c
                    out[unit] = jnp.where(depth == 3, pltpu.roll(warm, 96, 1), fraction)
                    out[16 + unit] = jnp.where(depth < 2, dual, given)
    meta = row_of([place[s] for s in range(SLOTS)])
    near[X_TILES - 1] = meta
    far[X_TILES - 1] = meta


def corner_kernel(
    place, near_meta, far_meta, mat, heat, load, prior, near, far, up, down
):
    values = [place[s] for s in range(SLOTS)]
    start = as_int(values[SLOTS - 1] >= 0)
    row = rows()

    def layer(out, to, at, j, rising):
        fraction, warm, given, dual = (
            ref[pl.ds(at, 8), 128 * j : 128 * j + 128] for ref in (mat, heat, load, prior)
        )
        step = 1 if rising else 7
        own = conductivity(fraction)
        beyond = conduct(own, pltpu.roll(own, step, 0)) * pltpu.roll(dual, step, 0)
        given = given + jnp.where(row == (2 if rising else 5), beyond, 0.0)
        spare, two = ((row == 0, row < 2) if rising else (row == 7, row > 5))
        a, b, c = ((5, 4, 2) if rising else (7, 5, 3))
        out[to] = jnp.where(spare, pltpu.roll(warm, a, 0), fraction)
        out[to + 24] = jnp.where(two, pltpu.roll(warm, b, 0), dual)
        out[to + 48] = jnp.where(two, pltpu.roll(warm, c, 0), given)

    for i in range(3):
        top = pl.multiple_of((start + i) * 32 + 24, 8)
        for j in range(8):
            layer(up, 8 * i + j, top, j, True)
            layer(down, 8 * i + j, 32 * i, j, False)
    for b, (meta, source) in enumerate(((near_meta, near), (far_meta, far))):
        listed = [position_at(meta, s) for s in range(SLOTS)]
        values = values + listed
        start = as_int(listed[SLOTS - 1] >= 0)
        for field in range(2):
            for i in range(3):
                to = Z_SLABS + b * 6 + field * 3 + i
                up[to] = source[field * 16 + (start + i) * 4 + 3]
                down[to] = source[field * 16 + i * 4]
    meta_tile = row_of(values)
    up[Z_TILES - 1] = meta_tile
    down[Z_TILES - 1] = meta_tile


def conduct(own, beside):
    return (2.0 * own) * beside / jnp.maximum(own + beside, KMIN)


def conductivity(fraction):
    return KMIN + (1.0 - KMIN) * fraction * fraction * fraction


def cell_of(x, y, z):
    return ((z + 1) * 6 + y + 1) * 4 + x + 1


def clear_cells(cells, zero):
    def clear(index, carry):
        cells[index] = zero
        return carry

    lax.fori_loop(0, 144, clear, 0, unroll=16)


def enter(cells, position, wanted, x, z, tile):
    here = jnp.where(wanted, cell_of(x, position // 2 % 4, z), 144)
    cells[here] = tile
    return jnp.where(wanted, here, DUMMY)


def fill(table, unit, values):
    for k, value in enumerate(values):
        table[unit * 8 + k] = value


class Stencil:
    def __init__(self, weights, stride):
        self.lane = lanes()
        row = rows()
        self.top_row = row == 0
        self.last_row = row == 7
        self.x_cell = self.lane % 32
        self.y_block = self.lane // 32
        self.face_block = self.lane // 4
        self.face_lane = 32 * (self.lane % 4)
        self.weights = weights
        self.stride = stride

    def above(self, tile, other):
        return pltpu.roll(jnp.where(self.top_row, other, tile), 7, 0)

    def below(self, tile, other):
        return pltpu.roll(jnp.where(self.last_row, other, tile), 1, 0)

    def brick(self, table, unit):
        base, up, down, north, south, east, west, px = (table[unit * 8 + k] for k in range(8))
        lane, x_cell = (self.lane, self.x_cell)
        own_lane = 31 * px
        brick_at = jnp.where(px == 1, west, east)
        slab_at = jnp.where(px == 1, east, west)
        from_brick = x_cell == own_lane
        to_brick = x_cell == 31 - own_lane
        index = jnp.where(to_brick, 32 * self.y_block + own_lane, self.y_block)
        step = jnp.where(to_brick, 0, 4)

        def around(ref, j):
            tile = ref[base + j]
            after = ref[base + j + 1] if j < 7 else ref[north]
            before = ref[base + j - 1] if j > 0 else ref[south + 7]
            beside = ref[slab_at]
            moved = 0
            if j == 0:
                beside, moved = (pltpu.roll(beside, 4, 1), 1)
            elif j == 7:
                beside, moved = (jnp.where(px == 1, pltpu.roll(beside, 4, 1), beside), px)
            both = jnp.where(from_brick, ref[brick_at + j], beside)
            edge = take(both, index + step * (j + moved))
            return tile, (
                jnp.where(x_cell == 31, edge, pltpu.roll(tile, 127, 1)),
                jnp.where(x_cell == 0, edge, pltpu.roll(tile, 1, 1)),
                pltpu.roll(jnp.where(lane < 32, after, tile), 96, 1),
                pltpu.roll(jnp.where(lane >= 96, before, tile), 32, 1),
                self.above(tile, ref[up + j]),
                self.below(tile, ref[down + j]),
            )

        return base, around

    def slab(self, table, unit):
        at, up, down, north, south, face, column = (table[unit * 8 + k] for k in range(7))
        lane, x_cell = (self.lane, self.x_cell)
        index = self.face_lane + column

        def around(ref):
            tile = ref[at]
            edge = take(ref[face], index)
            for j in range(1, 8):
                edge = jnp.where(self.face_block == j, take(ref[face + j], index), edge)
            return tile, (
                pltpu.roll(tile, 96, 1),
                jnp.where(lane < 32, edge, pltpu.roll(tile, 32, 1)),
                jnp.where(x_cell == 31, pltpu.roll(ref[north], 31, 1), pltpu.roll(tile, 127, 1)),
                jnp.where(x_cell == 0, pltpu.roll(ref[south], 97, 1), pltpu.roll(tile, 1, 1)),
                self.above(tile, ref[up]),
                self.below(tile, ref[down]),
            )

        return at, around

    def first(self, t, source, inverse, dual1, own_kappa, beside_kappa, beside):
        total = jnp.full((8, 128), HEAT, F32)
        flux = source[t]
        for k in range(6):
            weight = conduct(own_kappa, beside_kappa[k])
            self.weights[k * self.stride + t] = weight
            total = total + weight
            flux = flux + weight * beside[k]
        scale = 1.0 / total
        inverse[t] = scale
        dual1[t] = flux * scale

    def later(self, t, source, inverse, beside):
        flux = source[t]
        for k in range(6):
            flux = flux + self.weights[k * self.stride + t] * beside[k]
        return flux * inverse[t]

    def sensitivity(self, t, warm, warms, dual, duals):
        total = jnp.zeros((8, 128), F32)
        for k in range(6):
            total = total + jnp.where(
                self.weights[k * self.stride + t] > 0,
                (warms[k] - warm) * (duals[k] - dual),
                0.0,
            )
        return total


def factor_of(fraction):
    return (-1.5 * (1.0 - KMIN)) * fraction * fraction


def spread(to, first, second, kappa, temperature, source, dual0):
    kappa[to] = conductivity(first)
    dual0[to] = jnp.where(lanes() < 64, second, 0.0)
    source[to] = pltpu.roll(second, 64, 1)
    temperature[to] = pltpu.roll(first, 32, 1)


def shrink_table():
    cell = lax.broadcasted_iota(I32, (512, 128), 0)
    coarse = lax.broadcasted_iota(I32, (512, 128), 1)
    matches = (cell // 64 == coarse // 16) & (cell % 32 // 2 == coarse % 16)
    return jnp.where(matches, 0.125, 0.0).astype(F32)


def restrict(sens, summed, out, count):
    shrink = shrink_table()
    for half in range(2):
        summed[...] = jnp.dot(
            sens[:, 512 * half : 512 * half + 512],
            shrink,
            precision=lax.Precision.HIGHEST,
            preferred_element_type=F32,
        )
        for r in range(count):
            out[half, 8 * r : 8 * r + 8, :] = (
                summed[pl.ds(16 * r, 8, stride=2), :] + summed[pl.ds(16 * r + 1, 8, stride=2), :]
            )


def early_kernel(
    place,
    parity_ref,
    near_meta,
    far_meta,
    mat,
    heat,
    load,
    prior,
    near,
    far,
    dual1,
    dual2,
    coarse,
    cells,
    brick_table,
    slab_table,
    kappa,
    temperature,
    source,
    dual0,
    weights,
    inverse,
    sens,
    summed,
):
    parity = parity_ref[0]
    clear_cells(cells, E_ZERO)
    own = [place[s] for s in range(SLOTS)]
    own_cell = [enter(cells, q, q >= 0, q % 2, q // 8, 32 * s) for s, q in enumerate(own)]
    slab_cell = []
    slab_live = []
    for b, meta in enumerate((near_meta, far_meta)):
        east = parity == b
        column = jnp.where(east, 0, 1)
        x = jnp.where(east, 2, -1)
        for s in range(SLOTS):
            q = position_at(meta, s)
            wanted = (q >= 0) & (q % 2 == column)
            slab_live.append((wanted, q))
            slab_cell.append(
                enter(cells, q, wanted, x, q // 8, E_SLAB + 16 * b + 4 * s)
            )
    for s in range(SLOTS):
        here = own_cell[s]
        px = jnp.where(own[s] >= 0, own[s] % 2, 0)
        lift = jnp.where(own[s] >= 8, 24, 0)
        north, south = (cells[here + 4], cells[here - 4])
        east, west = (cells[here + 1], cells[here - 1])
        above, below = (cells[here + 24], cells[here - 24] + lift)
        for c in range(4):
            base = s * 32 + c * 8
            fill(
                brick_table,
                s * 4 + c,
                (
                    base,
                    base + 8 if c < 3 else above,
                    base - 8 if c > 0 else below,
                    north + 8 * c,
                    south + 8 * c,
                    east + jnp.where(px == 1, c, 8 * c),
                    west + jnp.where(px == 0, c, 8 * c),
                    px,
                ),
            )
    for b in range(2):
        inward = jnp.where(parity == b, -1, 1)
        column = jnp.where(parity == b, 31, 0)
        for s in range(SLOTS):
            here = slab_cell[4 * b + s]
            wanted, q = slab_live[4 * b + s]
            lift = jnp.where(q >= 8, 3, 0)
            north, south = (cells[here + 4], cells[here - 4])
            above, below = (cells[here + 24], cells[here - 24] + lift)
            face = cells[here + inward]
            live = as_int(wanted)
            for c in range(4):
                unit = 16 * b + 4 * s + c
                fill(
                    slab_table,
                    unit,
                    (
                        E_SLAB + unit,
                        E_SLAB + unit + 1 if c < 3 else above,
                        E_SLAB + unit - 1 if c > 0 else below,
                        north + c,
                        south + c,
                        face + 8 * c,
                        column,
                        live,
                    ),
                )

    zeros = jnp.zeros((8, 128), F32)
    for ref in (kappa, temperature, dual0, dual1, dual2):
        for t in range(32):
            ref[E_ZERO + t] = zeros

    def own_unit(unit, carry):
        at = pl.multiple_of(unit * 8, 8)
        active = place[unit // 4] >= 0
        for j in range(8):
            span = slice(128 * j, 128 * j + 128)
            t = unit * 8 + j
            kappa[t] = jnp.where(active, conductivity(mat[pl.ds(at, 8), span]), 0.0)
            source[t] = jnp.where(active, load[pl.ds(at, 8), span], 0.0)
            dual0[t] = prior[pl.ds(at, 8), span]
            temperature[t] = heat[pl.ds(at, 8), span]
        return carry

    lax.fori_loop(0, 16, own_unit, 0)
    for b, message in enumerate((near, far)):
        for t in range(16):
            to = E_SLAB + 16 * b + t
            spread(to, message[t], message[t + 16], kappa, temperature, source, dual0)

    stencil = Stencil(weights, E_TILES)

    def slabs(body):
        def slot(index, carry):
            @pl.when(slab_table[index * 32 + 7] > 0)
            def _():
                for c in range(4):
                    body(*stencil.slab(slab_table, index * 4 + c))

            return carry

        lax.fori_loop(0, 8, slot, 0)

    def bricks(body):
        def four(step, carry):
            for k in range(4):
                unit = 4 * step + k
                base, around = stencil.brick(brick_table, unit)
                for j in range(8):
                    body(unit, base, around, j)
            return carry

        lax.fori_loop(0, 4, four, 0)

    def brick_first(unit, base, around, j):
        own_kappa, beside_kappa = around(kappa, j)
        stencil.first(
            base + j, source, inverse, dual1, own_kappa, beside_kappa, around(dual0, j)[1]
        )

    def slab_first(t, around):
        own_kappa, beside_kappa = around(kappa)
        stencil.first(t, source, inverse, dual1, own_kappa, beside_kappa, around(dual0)[1])

    def brick_second(unit, base, around, j):
        dual2[base + j] = stencil.later(base + j, source, inverse, around(dual1, j)[1])

    def slab_second(t, around):
        dual2[t] = stencil.later(t, source, inverse, around(dual1)[1])

    def brick_third(unit, base, around, j):
        at = pl.multiple_of(unit * 8, 8)
        dual, duals = around(dual2, j)
        warm, warms = around(temperature, j)
        total = stencil.sensitivity(base + j, warm, warms, dual, duals)
        span = slice(128 * j, 128 * j + 128)
        sens[pl.ds(at, 8), span] = factor_of(mat[pl.ds(at, 8), span]) * total

    bricks(brick_first)
    slabs(slab_first)
    bricks(brick_second)
    slabs(slab_second)
    bricks(brick_third)
    restrict(sens, summed, coarse, 8)


def late_kernel(
    parts,
    place,
    parity_ref,
    near_meta,
    far_meta,
    up_meta,
    down_meta,
    mat,
    heat,
    load,
    prior,
    near,
    far,
    z_up,
    z_down,
    early1,
    early2,
    coarse,
    dual_out,
    chunks,
    dual_rows,
    dual_sem,
    cells,
    brick_table,
    slab_table,
    brick_list,
    slab_list,
    kappa,
    temperature,
    source,
    dual0,
    dual1,
    dual2,
    weights,
    inverse,
    factor,
    sens,
    summed,
    edge,
    whole,
    turned,
):
    parity = parity_ref[0]
    lane = lanes()
    row = rows()
    clear_cells(cells, L_ZERO)
    own = [place[s] for s in range(SLOTS)]

    def at_edge(q):
        return ((q >= 0) & (q < 8)) | (q >= 24)

    own_cell = [
        enter(cells, q, at_edge(q), q % 2, q // 8, 8 * s) for s, q in enumerate(own)
    ]
    lists_up = [[position_at(up_meta, 4 * k + s) for s in range(SLOTS)] for k in range(3)]
    lists_down = [[position_at(down_meta, 4 * k + s) for s in range(SLOTS)] for k in range(3)]

    def shifted(listed):
        full = listed[SLOTS - 1] >= 0
        return [jnp.where(full, listed[i + 1], listed[i]) for i in range(3)]

    ups = [listed[:3] for listed in lists_up]
    downs = [shifted(listed) for listed in lists_down]
    brick_live = [at_edge(q) for q in own]
    brick_live += [(q >= 0) & (q < 8) for q in ups[0]]
    brick_live += [q >= 24 for q in downs[0]]
    halo_cell = [
        enter(cells, q, brick_live[4 + i], q % 2, 4, L_UP + 8 * i) for i, q in enumerate(ups[0])
    ]
    halo_cell += [
        enter(cells, q, brick_live[7 + i], q % 2, -1, L_DOWN + 8 * i)
        for i, q in enumerate(downs[0])
    ]
    slab_cell = []
    slab_live = []
    slab_own = []
    for b, meta in enumerate((near_meta, far_meta)):
        east = parity == b
        column = jnp.where(east, 0, 1)
        x = jnp.where(east, 2, -1)
        base = L_SLAB + 14 * b
        mine = [position_at(meta, s) for s in range(SLOTS)]
        slab_own.append(mine)
        tests = [at_edge(q) & (q % 2 == column) for q in mine]
        tests += [(q >= 0) & (q < 8) & (q % 2 == column) for q in ups[1 + b]]
        tests += [(q >= 24) & (q % 2 == column) for q in downs[1 + b]]
        slab_live += tests
        for k, q in enumerate(mine + ups[1 + b] + downs[1 + b]):
            z = q // 8 if k < 4 else 4 if k < 7 else -1
            slab_cell.append(enter(cells, q, tests[k], x, z, base + (k if k < 4 else 4 + k)))

    high = [as_int(q >= 24) for q in own]
    for s in range(SLOTS):
        here = own_cell[s]
        px = jnp.where(own[s] >= 0, own[s] % 2, 0)
        inner = L_INNER + 8 * s
        fill(
            brick_table,
            s,
            (
                jnp.int32(8 * s),
                jnp.where(high[s] == 1, cells[here + 24], inner),
                jnp.where(high[s] == 1, inner, cells[here - 24]),
                cells[here + 4],
                cells[here - 4],
                cells[here + 1],
                cells[here - 1],
                px,
            ),
        )
    for i in range(6):
        here = halo_cell[i]
        q = (ups[0] + downs[0])[i]
        px = jnp.where(q >= 0, q % 2, 0)
        fill(
            brick_table,
            4 + i,
            (
                jnp.int32(L_UP + 8 * i),
                jnp.int32(L_ZERO) if i < 3 else cells[here + 24],
                cells[here - 24] if i < 3 else jnp.int32(L_ZERO),
                cells[here + 4],
                cells[here - 4],
                cells[here + 1],
                cells[here - 1],
                px,
            ),
        )
    for b in range(2):
        inward = jnp.where(parity == b, -1, 1)
        column = jnp.where(parity == b, 31, 0)
        base = L_SLAB + 14 * b
        for k in range(10):
            here = slab_cell[10 * b + k]
            above = jnp.int32(L_ZERO) if 4 <= k < 7 else cells[here + 24]
            below = jnp.int32(L_ZERO) if k >= 7 else cells[here - 24]
            if k < 4:
                top = slab_own[b][k] >= 24
                inner = base + 4 + k
                above, below = (jnp.where(top, above, inner), jnp.where(top, inner, below))
            fill(
                slab_table,
                10 * b + k,
                (
                    jnp.int32(base + (k if k < 4 else 4 + k)),
                    above,
                    below,
                    cells[here + 4],
                    cells[here - 4],
                    cells[here + inward],
                    column,
                ),
            )

    def listed(target, flags):
        count = jnp.int32(0)
        for index, flag in enumerate(flags):
            target[count] = index
            count = count + as_int(flag)
        last = target[jnp.maximum(count - 1, 0)]
        for k in range(3):
            target[count + k] = last
        return count

    brick_count = listed(brick_list, brick_live)
    slab_count = listed(slab_list, slab_live)

    zeros = jnp.zeros((8, 128), F32)
    for ref in (kappa, temperature, dual0, dual1, dual2):
        for t in range(8):
            ref[L_ZERO + t] = zeros

    for s in range(SLOTS):
        active = own[s] >= 0
        for to, chunk in ((8 * s, 3 * high[s]), (L_INNER + 8 * s, 1 + high[s])):
            at = pl.multiple_of(s * 32 + 8 * chunk, 8)
            for j in range(8):
                span = slice(128 * j, 128 * j + 128)
                fraction = mat[pl.ds(at, 8), span]
                kappa[to + j] = jnp.where(active, conductivity(fraction), 0.0)
                dual0[to + j] = prior[pl.ds(at, 8), span]
                temperature[to + j] = heat[pl.ds(at, 8), span]
                if to < L_INNER:
                    source[to + j] = load[pl.ds(at, 8), span]
                    factor[to + j] = factor_of(fraction)
                else:
                    dual1[to + j] = early1[32 * s + 8 * chunk + j]
                    dual2[to + j] = early2[32 * s + 8 * chunk + j]

    for k, message in enumerate((z_up, z_down)):
        for t in range(24):
            to = L_UP + 24 * k + t
            one, two, three = (message[t], message[24 + t], message[48 + t])
            a, b, c = ((3, 4, 6) if k else (1, 3, 5))
            kappa[to] = conductivity(one)
            dual0[to] = jnp.where(row >= 2 if k else row < 6, two, 0.0)
            source[to] = three
            temperature[to] = jnp.where(
                row == 3 if k else row == 0,
                pltpu.roll(one, a, 0),
                jnp.where(
                    row < 6 if k else row < 3,
                    pltpu.roll(two, b, 0),
                    pltpu.roll(three, c, 0),
                ),
            )
            factor[to] = factor_of(one)

    def slab_tile(to, message, at, step):
        spread(to, message[at], message[at + step], kappa, temperature, source, dual0)

    for b, message in enumerate((near, far)):
        base = L_SLAB + 14 * b
        for s in range(SLOTS):
            top = as_int(slab_own[b][s] >= 24)
            slab_tile(base + s, message, 4 * s + 3 * top, 16)
            inner = 4 * s + 1 + top
            slab_tile(base + 4 + s, message, inner, 16)
            dual1[base + 4 + s] = early1[E_SLAB + 16 * b + inner]
            dual2[base + 4 + s] = early2[E_SLAB + 16 * b + inner]
        for i in range(3):
            slab_tile(base + 8 + i, z_up, Z_SLABS + 6 * b + i, 3)
            slab_tile(base + 11 + i, z_down, Z_SLABS + 6 * b + i, 3)

    stencil = Stencil(weights, L_TILES)

    def bricks(body):
        def two(step, carry):
            for k in range(2):
                unit = brick_list[2 * step + k]
                base, around = stencil.brick(brick_table, unit)
                for j in range(8):
                    body(base, around, j)
            return carry

        lax.fori_loop(0, (brick_count + 1) // 2, two, 0)

    def slabs(body):
        def four(step, carry):
            for k in range(4):
                body(*stencil.slab(slab_table, slab_list[4 * step + k]))
            return carry

        lax.fori_loop(0, (slab_count + 3) // 4, four, 0)

    def brick_first(base, around, j):
        own_kappa, beside_kappa = around(kappa, j)
        stencil.first(
            base + j, source, inverse, dual1, own_kappa, beside_kappa, around(dual0, j)[1]
        )

    def slab_first(t, around):
        own_kappa, beside_kappa = around(kappa)
        stencil.first(t, source, inverse, dual1, own_kappa, beside_kappa, around(dual0)[1])

    def brick_second(base, around, j):
        dual2[base + j] = stencil.later(base + j, source, inverse, around(dual1, j)[1])

    def slab_second(t, around):
        dual2[t] = stencil.later(t, source, inverse, around(dual1)[1])

    def brick_third(base, around, j):
        dual, duals = around(dual2, j)
        warm, warms = around(temperature, j)
        total = stencil.sensitivity(base + j, warm, warms, dual, duals)
        at = jnp.where(base < L_INNER, base, base - 32)
        sens[pl.ds(pl.multiple_of(at, 8), 8), 128 * j : 128 * j + 128] = factor[base + j] * total

    bricks(brick_first)
    slabs(slab_first)
    bricks(brick_second)
    slabs(slab_second)
    for s in range(SLOTS):
        for c in range(4):
            for j in range(8):
                dual_rows[32 * s + 8 * c : 32 * s + 8 * c + 8, 128 * j : 128 * j + 128] = early2[
                    32 * s + 8 * c + j
                ]
        at = pl.multiple_of(32 * s + 24 * high[s], 8)
        for j in range(8):
            dual_rows[pl.ds(at, 8), 128 * j : 128 * j + 128] = jnp.where(
                brick_live[s], dual2[8 * s + j], early2[32 * s + 24 * high[s] + j]
            )

    writing = pltpu.make_async_copy(dual_rows, dual_out, dual_sem)
    writing.start()
    bricks(brick_third)

    restrict(sens, summed, edge, 5)
    for half in range(2):
        whole[...] = coarse[half]
        for s in range(SLOTS):
            at = 16 * s + 12 * high[s]
            whole[pl.ds(at, 4), :] = jnp.where(
                brick_live[s], edge[half, 4 * s : 4 * s + 4, :], coarse[half, pl.ds(at, 4), :]
            )

        for r in range(11):
            if r < 8:
                tile = whole[8 * r : 8 * r + 8, :]
            else:
                tile = edge[half, 8 * r - 48 : 8 * r - 40, :]
            for bit in (1, 2, 4):
                low_row = (row & bit) == 0
                low_lane = (lane & (16 * bit)) == 0
                swap_a = pltpu.roll(pltpu.roll(tile, 8 - bit, 0), 16 * bit, 1)
                swap_b = pltpu.roll(pltpu.roll(tile, bit, 0), 128 - 16 * bit, 1)
                tile = jnp.where(low_row == low_lane, tile, jnp.where(low_row, swap_a, swap_b))
            turned[2 * r + half] = tile

    y_block = lane // 32

    planes = 64 // parts
    level = [jnp.where(q >= 0, q // 8, 9) for q in own]

    def count(test):
        return functools.reduce(lambda a, b: a + b, [as_int(test(v)) for v in level])

    before = [count(lambda v, z=z: v < z) for z in range(5)]

    def nth(z, e):
        index = before[z] + e
        valid = index < before[z + 1]
        slot = jnp.minimum(index, SLOTS - 1)
        code = jnp.where(valid, place[slot] - 8 * z, -1)
        return slot, code

    for d in range(parts):
        z = d * planes // 16
        half = d * planes % 16 // 8
        codes = []
        for e in range(3):
            slot, code = nth(z, e)
            codes.append(code)
            for k in range(2):
                chunks[d * 8 + 2 * e + k] = turned[(slot * 2 + half) * 2 + k]
        start = d * planes % 8 == 0
        end = (d + 1) * planes % 8 == 0
        if planes >= 8:
            outside = -1 if half == 0 else 1
        else:
            outside = -1 if start else 1 if end else 0
        beyond = half + outside
        beside = [zeros, zeros]
        for e in range(3):
            if outside == 0:
                tile_at, lane_at, code = (0, 0, jnp.int32(-1))
            elif beyond in (0, 1):
                slot, code = nth(z, e)
                tile_at, lane_at = (slot * 2 + beyond, 96 if outside < 0 else 0)
            elif 0 <= z + outside <= 3:
                slot, code = nth(z + outside, e)
                tile_at, lane_at = (slot * 2 + (1 if outside < 0 else 0), 96 if outside < 0 else 0)
            elif outside < 0:
                q = downs[0][e]
                code = jnp.where(q >= 24, q - 24, -1)
                tile_at, lane_at = (8 + (3 + e) // 2, 64 * ((3 + e) % 2) + 32)
            else:
                q = ups[0][e]
                code = jnp.where((q >= 0) & (q < 8), q, -1)
                tile_at, lane_at = (8 + e // 2, 64 * (e % 2))
            codes.append(code)
            for k in range(2):
                tile = turned[tile_at * 2 + k]
                shift = (32 * e - lane_at) % 128
                if shift:
                    tile = pltpu.roll(tile, shift, 1)
                beside[k] = jnp.where(y_block == e, tile, beside[k])
        for e, code in enumerate(codes):
            beside[0] = jnp.where(lane == 96 + e, (code + 1).astype(F32), beside[0])
        for k in range(2):
            chunks[d * 8 + 6 + k] = beside[k]
    writing.wait()


class Placer:
    def __init__(self, grid, size, wide, across, code, column):
        self.grid = grid
        self.stride = 8 * wide
        self.wide = wide
        self.to = jnp.where(code >= 0, 0, size) + lax.div(column, across)
        code = jnp.maximum(code, 0)
        self.to = self.to + (code >> 1) * (2 * wide)
        self.at = (column * 2 + (code & 1)) & 7
        self.here = lanes() // 16 == self.at

    def planes(self, tile, k, windows, first, moved=0):
        found = []
        for p, window in enumerate(windows):
            shift = (self.at * 16 + moved + (-first - 16 * p) % 128) & 127
            to = self.to + k * self.wide + window * self.stride
            found.append((to, pltpu.roll(tile, shift, 1)))
        return found

    def put(self, planes):
        old = [self.grid[to] for to, _ in planes]
        for (to, moved), before in zip(planes, old):
            self.grid[to] = jnp.where(self.here, moved, before)


def code_of(meta, column, index):
    return meta[column, 0, 0, 96 + index].astype(I32) - 1


def filter_kernel(parts, planes, across, spot, meta, received, swapped, out, grid, once):
    depth = planes + 4
    wide = parts // across
    lane = lanes()
    row = rows()
    zeros = jnp.zeros((8, 128), F32)

    def clear(index, carry):
        grid[index] = zeros
        return carry

    lax.fori_loop(0, depth * 8 * wide, clear, 0, unroll=16)
    begin = spot[0] * planes
    half = begin % 16 // 8
    side = jnp.where(begin % 8 == 0, 0, planes + 2) if planes < 8 else half * (planes + 2)

    def from_device(column, carry):
        work = []
        for e in range(3):
            placer = Placer(grid, depth * 8 * wide, wide, across, code_of(meta, column, e), column)
            pair = [received[column * 8 + 2 * e + k] for k in range(2)]
            if planes == 8:
                found = []
                for k in range(2):
                    found += placer.planes(pair[k], k, range(2, 10), 0)
                    found += placer.planes(
                        swapped[column * 8 + 2 * e + k],
                        k,
                        [jnp.where(half == 0, 10 + p, p) for p in range(2)],
                        0,
                        jnp.where(half == 0, 0, 32),
                    )
                work.append((placer, found))
            else:
                for window in range(depth):
                    p = begin % 8 + window - 2

                    @pl.when((p >= 0) & (p < 8))
                    def _(p=p, window=window, pair=pair, placer=placer):
                        found = []
                        for k in range(2):
                            found += placer.planes(pair[k], k, [window], 0, 128 - 16 * p)
                        placer.put(found)

        for e in range(3):
            code = code_of(meta, column, 3 + e)
            placer = Placer(grid, depth * 8 * wide, wide, across, code, column)
            found = []
            for k in range(2):
                found += placer.planes(received[column * 8 + 6 + k], k, [side, side + 1], 32 * e)
            work.append((placer, found))
        for placer, found in work:
            placer.put(found)
        return carry

    lax.fori_loop(0, parts, from_device, 0)

    def relax(ref, window, y, x):
        here = (window * 8 + y) * wide + x
        tile = ref[here]
        north = ref[here + wide] if y < 7 else zeros
        south = ref[here - wide] if y > 0 else zeros
        east = ref[here + 1] if x < wide - 1 else zeros
        west = ref[here - 1] if x > 0 else zeros
        near = ref[here + 8 * wide] + ref[here - 8 * wide]
        near = near + pltpu.roll(jnp.where(row == 0, north, tile), 7, 0)
        near = near + pltpu.roll(jnp.where(row == 7, south, tile), 1, 0)
        near = near + pltpu.roll(jnp.where(lane == 0, east, tile), 127, 1)
        near = near + pltpu.roll(jnp.where(lane == 127, west, tile), 1, 1)
        return (grid[here] + 2.0 * near) * (1.0 / 13.0)

    first = spot[1] == 0
    last = spot[1] == spot[2] - 1

    def sweep_once(window, carry):
        gone = (first & (window < 2)) | (last & (window >= planes + 2))
        keep = jnp.where(gone, 0.0, 1.0).astype(F32)
        for y in range(8):
            for x in range(wide):
                once[(window * 8 + y) * wide + x] = relax(grid, window, y, x) * keep
        return carry

    lax.fori_loop(1, depth - 1, sweep_once, 0, unroll=5)

    def sweep_again(window, carry):
        for y in range(8):
            for x in range(wide):
                out[window - 2, 8 * y : 8 * y + 8, 128 * x : 128 * x + 128] = relax(
                    once, window, y, x
                )
        return carry

    lax.fori_loop(2, depth - 2, sweep_again, 0, unroll=4)


VMEM = pl.BlockSpec(memory_space=pltpu.VMEM)
SMEM = pl.BlockSpec(memory_space=pltpu.SMEM)
HBM = pl.BlockSpec(memory_space=pltpu.HBM)
BIG = 32 * 1024 * 1024
WHOLE = 60 * 1024 * 1024


def meta_of(index):
    return pl.BlockSpec((1, 8, 128), lambda i: (index, 0, 0), memory_space=pltpu.SMEM)


def params(limit=BIG):
    return pltpu.CompilerParams(vmem_limit_bytes=limit)


def tiles(count):
    return jax.ShapeDtypeStruct((count, 8, 128), F32)


def per_device(
    material_fraction, primal_heat_solution, dual_load, dual_prior_design, holder_cube_location
):
    parts = lax.axis_size("ba")
    groups = lax.axis_size("gz")
    member = lax.axis_index("ba")
    group = lax.axis_index("gz")
    planes = 64 // parts
    parity = (member % 2).reshape(1).astype(I32)
    place = holder_cube_location
    fields = [
        field.reshape(128, 1024)
        for field in (material_fraction, primal_heat_solution, dual_load, dual_prior_design)
    ]
    near, far = pl.pallas_call(
        pack_kernel,
        out_shape=(tiles(X_TILES), tiles(X_TILES)),
        in_specs=[SMEM, SMEM, HBM, HBM, HBM, HBM],
        out_specs=(VMEM, VMEM),
        scratch_shapes=[pltpu.VMEM((128, 1024), F32)] * 4
        + [pltpu.VMEM((384 * GROUP, 1024), jnp.bfloat16), pltpu.SemaphoreType.DMA((4, 4))],
        compiler_params=params(WHOLE),
        name="pack",
    )(place, parity, *fields)
    inner = [(i, i ^ 1) for i in range(parts)]
    outer = [(i, i + 1 if i % 2 else i - 1) for i in range(1, parts - 1)]
    near = lax.ppermute(near, "ba", inner)
    far = lax.ppermute(far, "ba", outer)
    up, down = pl.pallas_call(
        corner_kernel,
        out_shape=(tiles(Z_TILES), tiles(Z_TILES)),
        in_specs=[SMEM, meta_of(X_TILES - 1), meta_of(X_TILES - 1)] + [VMEM] * 6,
        out_specs=(VMEM, VMEM),
        grid=(1,),
        compiler_params=params(),
        name="corners",
    )(place, near, far, *fields, near, far)
    rising = [(i, i + 1) for i in range(groups - 1)]
    falling = [(i + 1, i) for i in range(groups - 1)]
    from_below = lax.ppermute(up, "gz", rising)
    from_above = lax.ppermute(down, "gz", falling)
    meta_z = meta_of(Z_TILES - 1)
    meta_x = meta_of(X_TILES - 1)
    early = pltpu.VMEM((E_TILES, 8, 128), F32)
    dual1, dual2, coarse = pl.pallas_call(
        early_kernel,
        out_shape=(tiles(E_TILES), tiles(E_TILES), jax.ShapeDtypeStruct((2, 64, 128), F32)),
        in_specs=[SMEM, SMEM, meta_x, meta_x] + [VMEM] * 6,
        out_specs=(VMEM, VMEM, VMEM),
        scratch_shapes=[
            pltpu.SMEM((145,), I32),
            pltpu.SMEM((16 * 8,), I32),
            pltpu.SMEM((32 * 8,), I32),
            early,
            early,
            early,
            early,
            pltpu.VMEM((6 * E_TILES, 8, 128), F32),
            early,
            pltpu.VMEM((128, 1024), F32),
            pltpu.VMEM((128, 128), F32),
        ],
        grid=(1,),
        cost_estimate=pl.CostEstimate(flops=10**9, bytes_accessed=3 * 10**7, transcendentals=0),
        compiler_params=params(),
        name="early",
    )(place, parity, near, far, *fields, near, far)
    late = pltpu.VMEM((L_TILES, 8, 128), F32)
    dual, chunks = pl.pallas_call(
        functools.partial(late_kernel, parts),
        out_shape=(jax.ShapeDtypeStruct((128, 1024), F32), tiles(8 * parts)),
        in_specs=[SMEM, SMEM, meta_x, meta_x, meta_z, meta_z] + [VMEM] * 11,
        out_specs=(HBM, VMEM),
        scratch_shapes=[
            pltpu.VMEM((128, 1024), F32),
            pltpu.SemaphoreType.DMA,
            pltpu.SMEM((145,), I32),
            pltpu.SMEM((10 * 8,), I32),
            pltpu.SMEM((20 * 8,), I32),
            pltpu.SMEM((16,), I32),
            pltpu.SMEM((24,), I32),
            late,
            late,
            late,
            late,
            late,
            late,
            pltpu.VMEM((6 * L_TILES, 8, 128), F32),
            late,
            pltpu.VMEM((L_SLAB, 8, 128), F32),
            pltpu.VMEM((80, 1024), F32),
            pltpu.VMEM((80, 128), F32),
            pltpu.VMEM((2, 40, 128), F32),
            pltpu.VMEM((64, 128), F32),
            pltpu.VMEM((22, 8, 128), F32),
        ],
        grid=(1,),
        compiler_params=params(),
        name="late",
    )(
        place,
        parity,
        near,
        far,
        from_above,
        from_below,
        *fields,
        near,
        far,
        from_above,
        from_below,
        dual1,
        dual2,
        coarse,
    )
    received = lax.all_to_all(chunks, "ba", split_axis=0, concat_axis=0, tiled=True)
    swapped = lax.ppermute(received, "ba", inner) if planes == 8 else received
    spot = jnp.stack([member, group * parts + member, jnp.int32(groups * parts)]).astype(I32)
    wide = 32 * parts // 128
    codes = received.reshape(parts, 8, 8, 128)
    codes_spec = pl.BlockSpec((parts, 1, 8, 128), lambda i: (0, 6, 0, 0), memory_space=pltpu.SMEM)
    window = (planes + 4) * 8 * wide
    filtered = pl.pallas_call(
        functools.partial(filter_kernel, parts, planes, 4),
        out_shape=jax.ShapeDtypeStruct((planes, 64, 32 * parts), F32),
        in_specs=[SMEM, codes_spec, VMEM, VMEM],
        out_specs=VMEM,
        scratch_shapes=[pltpu.VMEM((2 * window, 8, 128), F32), pltpu.VMEM((window, 8, 128), F32)],
        grid=(1,),
        compiler_params=params(),
        name="smooth",
    )(spot, codes, received, swapped)
    return (dual.reshape(material_fraction.shape), filtered)


def solution(mesh):
    spec = P(("gz", "ba"), None, None)
    return jax.shard_map(
        per_device,
        mesh=mesh,
        in_specs=(spec, spec, spec, spec, P(("gz", "ba"))),
        out_specs=(spec, spec),
        check_vma=False,
    )
```
